128 devices in a mesh: seq: 32 (over y, x, core), dp: 4 (over z).
Axes of the slice: x: 4, y: 4, z: 4, core: 2. Of those that a mesh axis runs over, the one named last changes fastest.
Arguments:
- features: bfloat16 [4, 8192, 512], P('dp', 'seq'), may hold values from -6 to 6
- curve_pos: int32 [4, 8192], P('dp'), may hold values from 0 to 8191, as said below
- pattern: int32 [4, 64, 8], P('dp'), may hold values from 0 to 63, as said below
- ln1_gain: float32 [512], replicated, may hold values from 0.5 to 1.5
- w_qkv: bfloat16 [512, 1536], replicated, may hold values from -1 to 1
- w_out: bfloat16 [512, 512], replicated, may hold values from -0.25 to 0.25
- ln2_gain: float32 [512], replicated, may hold values from 0.5 to 1.5
- w_up: bfloat16 [512, 2048], replicated, may hold values from -0.25 to 0.25
- w_down: bfloat16 [2048, 512], replicated, may hold values from -0.125 to 0.125
- out_grad: bfloat16 [4, 8192, 512], P('dp', 'seq'), may hold values from -6 to 6
Outputs:
- block_out: bfloat16 [4, 8192, 512], P('dp', 'seq')
- input_grad: bfloat16 [4, 8192, 512], P('dp', 'seq')
- grad_qkv: float32 [512, 1536], replicated
- grad_out: float32 [512, 512], replicated
- grad_up: float32 [512, 2048], replicated
- grad_down: float32 [2048, 512], replicated
- grad_gain1: float32 [512], replicated
- grad_gain2: float32 [512], replicated
The draws below stay inside these ranges and needn't reach their ends.
Inputs may be any that keep to these rules, and one draw needn't show every extreme that they name: `curve_pos`: for each tile a permutation of the 8192 curve positions. Of the 256 nodes of one aligned block, at most 16 have positions in one aligned block of 256 curve positions, and in every tile some node block sends exactly 16 to some curve block. `pattern`: each list holds 8 distinct blocks: first the query block q itself, then blocks (q + 2**j) or (q - 2**j) modulo 64.
All inputs are finite; a program needn't handle non-finite values.
Results may differ from the reference program's by a relative error of at most 0.018.
Values may be sent and summed in bfloat16 or wider, within the bound.
A program may use at most 128 MiB of HBM per device.

```python
from functools import partial
import jax
import jax.numpy as jnp
from jax import lax

D = 512
HEADS = 8
FF = 2048
ROWS_DEV = 256
BLK = 128
KB = 8
HEAD_DIM = 64
TILES = 4
NODES = 8192
NBLK = 64
CAP = 16
N_SEQ = 32


def curve_tile(tile_key):
    seq_devices = N_SEQ
    sub_keys = jax.random.split(tile_key, 5)
    pairing = jax.random.permutation(sub_keys[0], seq_devices)
    shares = jax.random.randint(sub_keys[1], (seq_devices // 2,), 0, CAP + 1).astype(jnp.int32)
    shares = shares.at[0].set(CAP)
    offsets = jnp.zeros((seq_devices,), jnp.int32).at[pairing[0::2]].set(shares).at[pairing[1::2]].set(CAP - shares)
    labels = jax.random.permutation(sub_keys[2], seq_devices)
    counts = offsets[(labels[None, :] - labels[:, None]) % seq_devices]
    ends = jnp.cumsum(counts, axis=1).astype(jnp.int32)
    starts = ends - counts
    sorted_rows = jnp.arange(ROWS_DEV, dtype=jnp.int32)
    targets = jax.vmap(lambda edge_row: jnp.searchsorted(edge_row, sorted_rows, side='right'))(ends).astype(jnp.int32)
    send_rank = sorted_rows[None, :] - jnp.take_along_axis(starts, targets, axis=1)
    arrive_base = (jnp.cumsum(counts, axis=0) - counts).astype(jnp.int32)
    arrive_rank = jnp.take_along_axis(arrive_base, targets, axis=1) + send_rank
    slot_perms = jax.vmap(lambda sub_key: jax.random.permutation(sub_key, ROWS_DEV))(jax.random.split(sub_keys[3], seq_devices)).astype(jnp.int32)
    slots = slot_perms[targets, arrive_rank]
    positions = targets * ROWS_DEV + slots
    node_perms = jax.vmap(lambda sub_key: jax.random.permutation(sub_key, ROWS_DEV))(jax.random.split(sub_keys[4], seq_devices)).astype(jnp.int32)
    device_rows = jnp.arange(seq_devices, dtype=jnp.int32)[:, None]
    result = jnp.zeros((seq_devices, ROWS_DEV), jnp.int32).at[device_rows, node_perms].set(positions)
    return result.reshape(-1)


def draw_curve_pos(key, part):
    return jax.vmap(curve_tile)(jax.random.split(key, TILES)).astype(jnp.int32)


def draw_pattern(key, part):
    levels = NBLK.bit_length() - 1
    offset_list = [2 ** level_idx for level_idx in range(levels)] + [-2 ** level_idx for level_idx in range(levels - 1)]
    offset_table = jnp.array(offset_list, dtype=jnp.int32)
    chosen = jax.vmap(lambda sub_key: jax.random.permutation(sub_key, len(offset_list))[:KB - 1])(jax.random.split(key, TILES * NBLK))
    chosen = chosen.reshape(TILES, NBLK, KB - 1).astype(jnp.int32)
    own_block = jnp.broadcast_to(jnp.arange(NBLK, dtype=jnp.int32)[None, :, None], (TILES, NBLK, 1))
    others = (own_block + offset_table[chosen]) % NBLK
    return jnp.concatenate([own_block, others], axis=-1).astype(jnp.int32)


def draw_w_qkv(key, part):
    matrix = jax.random.normal(key, (D, 3 * D), jnp.float32) * D ** (-0.5)
    return jnp.clip(matrix, -1.0, 1.0).astype(jnp.bfloat16)


def block_levels(stream_key, shape, cuts, least, high):
    gain = 1.0
    for dim, blocks in cuts:
        draws = jax.random.uniform(jax.random.fold_in(jax.random.fold_in(stream_key, 6), dim), (blocks,), jnp.float32, least / len(cuts), high / len(cuts))
        gain = gain * jnp.repeat(jnp.exp(draws), shape[dim] // blocks).reshape((-1,) + (1,) * (len(shape) - 1 - dim))
    return gain


def noise(key, dims, deviation, limit, cuts=(), kind=jnp.bfloat16):
    level = block_levels(key, dims, cuts, -0.22, 0.18) if cuts else 1.0
    drawn = jax.random.normal(key, dims, jnp.float32) * deviation * level
    return jnp.minimum(jnp.maximum(drawn, -limit), limit).astype(kind)


def setup_inputs(seed: int = 0) -> dict:
    splits = jax.random.split(jax.random.key(seed), 11)
    features = noise(splits[0], (TILES, NODES, D), 1.0, 6.0, ((0, 4), (1, 32)))
    curve_pos = draw_curve_pos(jax.random.fold_in(splits[10], 71), 0)
    pattern = draw_pattern(jax.random.fold_in(splits[10], 71), 0)
    ln1_gain = jnp.clip(1.0 + 0.1 * jax.random.normal(splits[3], (D,), jnp.float32), 0.5, 1.5)
    w_qkv = draw_w_qkv(jax.random.fold_in(splits[10], 71), 0)
    w_out = noise(splits[5], (D, D), D ** -0.5, 0.25)
    ln2_gain = jnp.clip(1.0 + 0.1 * jax.random.normal(splits[6], (D,), jnp.float32), 0.5, 1.5)
    w_up = noise(splits[7], (D, FF), D ** -0.5, 0.25)
    w_down = noise(splits[8], (FF, D), FF ** -0.5, 0.125)
    out_grad = noise(splits[9], (TILES, NODES, D), 1.0, 6.0, ((0, 4), (1, 32)))
    return dict(features=features, curve_pos=curve_pos, pattern=pattern, ln1_gain=ln1_gain, w_qkv=w_qkv, w_out=w_out, ln2_gain=ln2_gain, w_up=w_up, w_down=w_down, out_grad=out_grad)


EPSILON = 1e-05

def layer_norm(rows_in, gain_vec):
    values = rows_in.astype(jnp.float32)
    centered = values - lax.optimization_barrier(jnp.mean(values, axis=-1, keepdims=True))
    inverse = lax.rsqrt(lax.optimization_barrier(jnp.mean(centered * centered, axis=-1, keepdims=True)) + EPSILON)
    normed = centered * inverse
    return ((normed * gain_vec).astype(jnp.bfloat16), normed, inverse)

def norm_back(incoming, gain_vec, normed, inverse):
    scaled = incoming * gain_vec
    return inverse * (scaled - lax.optimization_barrier(jnp.mean(scaled, axis=-1, keepdims=True)) - normed * lax.optimization_barrier(jnp.mean(scaled * normed, axis=-1, keepdims=True)))

def gelu_back(pre_act, incoming):
    return jax.vjp(partial(jax.nn.gelu, approximate=True), pre_act)[1](incoming)[0]

def inner_rows(left_mat, right_mat):
    return lax.dot_general(left_mat, right_mat, (((0,), (0,)), ((), ())), preferred_element_type=jnp.float32)

def times_transposed(left_mat, right_mat):
    return lax.dot_general(left_mat, right_mat, (((1,), (1,)), ((), ())), preferred_element_type=jnp.float32)

def block_rows(block_list):
    return (block_list[:, None].astype(jnp.int32) * BLK + jnp.arange(BLK, dtype=jnp.int32)[None, :]).reshape(-1).astype(jnp.int32)

def rounded(values):
    return lax.optimization_barrier(values.astype(jnp.bfloat16)).astype(jnp.float32)

def ref_attention(queries, keys, values, lists):
    query_blocks = queries.reshape(NBLK, BLK, HEADS, HEAD_DIM)
    key_heads = keys.reshape(NODES, HEADS, HEAD_DIM)
    value_heads = values.reshape(NODES, HEADS, HEAD_DIM)

    def one_block(packed):
        query_blk, block_list = packed
        key_rows = block_rows(block_list)
        scores = jnp.einsum('ihd,jhd->hij', query_blk.astype(jnp.float32), key_heads[key_rows].astype(jnp.float32)) * 0.125
        largest = lax.optimization_barrier(jnp.max(scores, axis=-1, keepdims=True))
        log_totals = largest + jnp.log(lax.optimization_barrier(jnp.sum(jnp.exp(scores - largest), axis=-1, keepdims=True)))
        attn_probs = rounded(jnp.exp(scores - log_totals))
        result = jnp.einsum('hij,jhd->ihd', attn_probs, value_heads[key_rows].astype(jnp.float32)).astype(jnp.bfloat16)
        return (result, log_totals)
    outputs, log_totals = lax.map(one_block, (query_blocks, lists))
    return (outputs.reshape(NODES, D), log_totals)

def ref_attention_back(queries, keys, values, lists, attn_out, log_totals, grad_attn):
    query_blocks = queries.reshape(NBLK, BLK, HEADS, HEAD_DIM)
    out_blocks = attn_out.reshape(NBLK, BLK, HEADS, HEAD_DIM)
    grad_blocks = grad_attn.reshape(NBLK, BLK, HEADS, HEAD_DIM)
    key_heads = keys.reshape(NODES, HEADS, HEAD_DIM)
    value_heads = values.reshape(NODES, HEADS, HEAD_DIM)

    def one_block(carry, packed):
        grad_keys, grad_values = carry
        query_blk, out_blk, grad_blk, log_blk, block_list = packed
        key_rows = block_rows(block_list)
        key_blk = key_heads[key_rows].astype(jnp.float32)
        value_blk = value_heads[key_rows].astype(jnp.float32)
        query_f = query_blk.astype(jnp.float32)
        grad_f = grad_blk.astype(jnp.float32)
        scores = jnp.einsum('ihd,jhd->hij', query_f, key_blk) * 0.125
        attn_exact = jnp.exp(scores - log_blk)
        attn_probs = rounded(attn_exact)
        grad_probs = jnp.einsum('ihd,jhd->hij', grad_f, value_blk)
        row_dots = jnp.einsum('ihd,ihd->hi', grad_f, out_blk.astype(jnp.float32))[..., None]
        grad_scores = rounded(attn_exact * (grad_probs - row_dots) * 0.125)
        grad_query = jnp.einsum('hij,jhd->ihd', grad_scores, key_blk).astype(jnp.bfloat16)
        grad_keys = grad_keys.at[key_rows].add(jnp.einsum('hij,ihd->jhd', grad_scores, query_f))
        grad_values = grad_values.at[key_rows].add(jnp.einsum('hij,ihd->jhd', attn_probs, grad_f))
        return ((grad_keys, grad_values), grad_query)
    zeros_kv = jnp.zeros((NODES, HEADS, HEAD_DIM), jnp.float32)
    (grad_keys, grad_values), grad_query = lax.scan(one_block, (zeros_kv, zeros_kv), (query_blocks, out_blocks, grad_blocks, log_totals, lists))
    return (grad_query.reshape(NODES, D), grad_keys.astype(jnp.bfloat16).reshape(NODES, D), grad_values.astype(jnp.bfloat16).reshape(NODES, D))

def reference(features, curve_pos, pattern, ln1_gain, w_qkv, w_out, ln2_gain, w_up, w_down, out_grad):
    outputs = []
    input_grads = []
    grad_qkv = jnp.zeros((D, 3 * D), jnp.float32)
    grad_out = jnp.zeros((D, D), jnp.float32)
    grad_up = jnp.zeros((D, FF), jnp.float32)
    grad_down = jnp.zeros((FF, D), jnp.float32)
    grad_gain1 = jnp.zeros((D,), jnp.float32)
    grad_gain2 = jnp.zeros((D,), jnp.float32)
    for tile_id in range(TILES):
        position = curve_pos[tile_id].astype(jnp.int32)
        curve_rows = jnp.zeros((NODES, D), jnp.bfloat16).at[position].set(features[tile_id])
        normed_a, normed1, inverse1 = layer_norm(curve_rows, ln1_gain)
        qkv = jnp.dot(normed_a, w_qkv, preferred_element_type=jnp.float32).astype(jnp.bfloat16)
        queries = qkv[:, :D]
        keys = qkv[:, D:2 * D]
        values = qkv[:, 2 * D:]
        lists = pattern[tile_id].astype(jnp.int32)
        attn_out, log_totals = ref_attention(queries, keys, values, lists)
        hidden_res = (curve_rows.astype(jnp.float32) + jnp.dot(attn_out, w_out, preferred_element_type=jnp.float32)).astype(jnp.bfloat16)
        normed_b, normed2, inverse2 = layer_norm(hidden_res, ln2_gain)
        pre_act = jnp.dot(normed_b, w_up, preferred_element_type=jnp.float32)
        activated = jax.nn.gelu(pre_act, approximate=True).astype(jnp.bfloat16)
        curve_out = (hidden_res.astype(jnp.float32) + jnp.dot(activated, w_down, preferred_element_type=jnp.float32)).astype(jnp.bfloat16)
        outputs.append(curve_out[position])
        grad_curve = jnp.zeros((NODES, D), jnp.bfloat16).at[position].set(out_grad[tile_id])
        grad_pre = gelu_back(pre_act, times_transposed(grad_curve, w_down)).astype(jnp.bfloat16)
        grad_down = grad_down + inner_rows(activated, grad_curve)
        grad_normed_b = times_transposed(grad_pre, w_up)
        grad_up = grad_up + inner_rows(normed_b, grad_pre)
        grad_gain2 = grad_gain2 + lax.optimization_barrier(jnp.sum(grad_normed_b * normed2, axis=0))
        grad_hidden = (grad_curve.astype(jnp.float32) + norm_back(grad_normed_b, ln2_gain, normed2, inverse2)).astype(jnp.bfloat16)
        grad_attn = times_transposed(grad_hidden, w_out).astype(jnp.bfloat16)
        grad_out = grad_out + inner_rows(attn_out, grad_hidden)
        grad_query, grad_keys, grad_values = ref_attention_back(queries, keys, values, lists, attn_out, log_totals, grad_attn)
        grad_qkv_rows = jnp.concatenate([grad_query, grad_keys, grad_values], axis=1)
        grad_normed_a = times_transposed(grad_qkv_rows, w_qkv)
        grad_qkv = grad_qkv + inner_rows(normed_a, grad_qkv_rows)
        grad_gain1 = grad_gain1 + lax.optimization_barrier(jnp.sum(grad_normed_a * normed1, axis=0))
        grad_curve_in = (grad_hidden.astype(jnp.float32) + norm_back(grad_normed_a, ln1_gain, normed1, inverse1)).astype(jnp.bfloat16)
        input_grads.append(grad_curve_in[position])
    return (jnp.stack(outputs), jnp.stack(input_grads), grad_qkv, grad_out, grad_up, grad_down, grad_gain1, grad_gain2)
```

```python
from functools import partial

import jax
import jax.numpy as jnp
from jax import lax
from jax.sharding import PartitionSpec as P

D = 512
HEADS = 8
BLK = 128


EPSILON = 1e-05


def from_behind(x, axis, by):
    length = lax.axis_size(axis)
    return lax.ppermute(x, axis, [(i, (i + by) % length) for i in range(length)])


def layer_norm(rows_in, gain_vec):
    values = rows_in.astype(jnp.float32)
    centered = values - jnp.mean(values, axis=-1, keepdims=True)
    inverse = lax.rsqrt(jnp.mean(centered * centered, axis=-1, keepdims=True) + EPSILON)
    normed = centered * inverse
    return ((normed * gain_vec).astype(jnp.bfloat16), normed, inverse)


def norm_back(incoming, gain_vec, normed, inverse):
    scaled = incoming * gain_vec
    return inverse * (
        scaled
        - jnp.mean(scaled, axis=-1, keepdims=True)
        - normed * jnp.mean(scaled * normed, axis=-1, keepdims=True)
    )


def gelu_back(pre_act, incoming):
    return jax.vjp(partial(jax.nn.gelu, approximate=True), pre_act)[1](incoming)[0]


def inner_rows(left_mat, right_mat):
    return lax.dot_general(
        left_mat, right_mat, (((0,), (0,)), ((), ())), preferred_element_type=jnp.float32
    )


def times_transposed(left_mat, right_mat):
    return lax.dot_general(
        left_mat, right_mat, (((1,), (1,)), ((), ())), preferred_element_type=jnp.float32
    )


def split_heads(rows_in):
    return rows_in.reshape(rows_in.shape[0] // BLK, BLK, HEADS, D // HEADS)


def listed_heads(keyval_all, selected):
    blocks = keyval_all.reshape(keyval_all.shape[0] // BLK, BLK, 2 * D)
    picked = blocks[selected]
    shape_out = picked.shape[:3] + (HEADS, D // HEADS)
    return (picked[..., :D].reshape(shape_out), picked[..., D:].reshape(shape_out))


def shift_distances(seq_devices):
    levels = seq_devices.bit_length() - 1
    distances = []
    for level_idx in range(levels):
        stride = 2**level_idx
        if 2 * stride == seq_devices:
            distances.append(stride)
        else:
            distances.extend([stride, -stride])
    return distances


def node_plan(position, seq_index, dev_rows, capacity, seq_devices):
    own_position = lax.dynamic_slice_in_dim(position, seq_index * dev_rows, dev_rows)
    target_dev = own_position // dev_rows
    dest_hits = (target_dev[:, None] == jnp.arange(seq_devices, dtype=jnp.int32)[None, :]).astype(
        jnp.int32
    )
    send_rank = jnp.sum((jnp.cumsum(dest_hits, axis=0) - dest_hits) * dest_hits, axis=1)
    send_index = target_dev * capacity + send_rank
    layout = position.reshape(seq_devices, dev_rows)
    arriving = (layout // dev_rows == seq_index).astype(jnp.int32)
    arrive_rank = jnp.cumsum(arriving, axis=1) - arriving
    source_index = jnp.arange(seq_devices, dtype=jnp.int32)[:, None] * capacity + arrive_rank
    del source_index
    total = position.shape[0]
    inverse = (
        jnp.zeros((total,), jnp.int32)
        .at[position]
        .set(jnp.arange(total, dtype=jnp.int32), unique_indices=True)
    )
    slot_node = lax.dynamic_slice_in_dim(inverse, seq_index * dev_rows, dev_rows)
    source_for_slot = (slot_node // dev_rows) * capacity + arrive_rank.reshape(-1)[slot_node]
    return (send_index, source_for_slot)


def attention_forward(queries, keyval_all, selected):
    query_heads = split_heads(queries)
    key_heads, value_heads = listed_heads(keyval_all, selected)
    scores = (
        jnp.einsum("aihd,akjhd->haikj", query_heads, key_heads, preferred_element_type=jnp.float32)
        * 0.125
    )
    largest = jnp.max(scores, axis=(3, 4), keepdims=True)
    totals = jnp.sum(jnp.exp(scores - largest), axis=(3, 4), keepdims=True)
    log_totals = largest + jnp.log(totals)
    attn_probs = jnp.exp(scores - log_totals).astype(jnp.bfloat16)
    result = jnp.einsum(
        "haikj,akjhd->aihd", attn_probs, value_heads, preferred_element_type=jnp.float32
    )
    return (result.astype(jnp.bfloat16).reshape(queries.shape[0], D), log_totals)


def attention_backward(queries, keyval_all, selected, attn_out, log_totals, grad_attn):
    query_heads = split_heads(queries)
    key_heads, value_heads = listed_heads(keyval_all, selected)
    out_heads = split_heads(attn_out)
    grad_heads = split_heads(grad_attn)
    scores = (
        jnp.einsum("aihd,akjhd->haikj", query_heads, key_heads, preferred_element_type=jnp.float32)
        * 0.125
    )
    attn_exact = jnp.exp(scores - log_totals)
    attn_probs = attn_exact.astype(jnp.bfloat16)
    grad_probs = jnp.einsum(
        "aihd,akjhd->haikj", grad_heads, value_heads, preferred_element_type=jnp.float32
    )
    row_dots = jnp.einsum(
        "aihd,aihd->hai", grad_heads, out_heads, preferred_element_type=jnp.float32
    )[..., None, None]
    grad_scores = (attn_exact * (grad_probs - row_dots) * 0.125).astype(jnp.bfloat16)
    grad_query = jnp.einsum(
        "haikj,akjhd->aihd", grad_scores, key_heads, preferred_element_type=jnp.float32
    )
    grad_keys = jnp.einsum(
        "haikj,aihd->akjhd", grad_scores, query_heads, preferred_element_type=jnp.float32
    )
    grad_values = jnp.einsum(
        "haikj,aihd->akjhd", attn_probs, grad_heads, preferred_element_type=jnp.float32
    )
    block_shape = grad_keys.shape[:3] + (D,)
    grad_picked = jnp.concatenate(
        [grad_keys.reshape(block_shape), grad_values.reshape(block_shape)], axis=-1
    )
    total_rows = keyval_all.shape[0]
    grad_keyval = (
        jnp.zeros((total_rows // BLK, BLK, 2 * D), jnp.float32).at[selected].add(grad_picked)
    )
    return (
        grad_query.astype(jnp.bfloat16).reshape(queries.shape[0], D),
        grad_keyval.reshape(total_rows, 2 * D),
    )


def ring_position(kind):
    seq_index = lax.axis_index("seq")
    if kind == "x":
        return (seq_index // 2) % 4
    if kind == "y":
        return seq_index // 8
    return lax.axis_index("dp")


def ring_send(rows, kind, shift):
    if kind == "z":
        size = lax.axis_size("dp")
        return lax.ppermute(rows, "dp", [(i, (i + shift) % size) for i in range(size)])
    size = lax.axis_size("seq")
    if kind == "x":
        move = lambda i: i - ((i // 2) % 4) * 2 + (((i // 2) % 4 + shift) % 4) * 2
    else:
        move = lambda i: ((i // 8 + shift) % 4) * 8 + i % 8
    return lax.ppermute(rows, "seq", [(i, move(i)) for i in range(size)])


def in_member_order(pieces, position):
    count = len(pieces)
    stacked = jnp.stack(pieces)
    order = (position - jnp.arange(count, dtype=jnp.int32)) % count
    return jnp.take(stacked, order, axis=0)


def scatter_stage(rows, gains, kind):
    position = ring_position(kind)
    part = rows.shape[0] // 4
    chunks = rows.reshape(4, part, rows.shape[1])
    total = lax.dynamic_index_in_dim(chunks, position, keepdims=False)
    gains_sent = None if gains is None else gains.astype(jnp.bfloat16)
    gains_got = [gains_sent]
    for shift in (1, 2, 3):
        piece = lax.dynamic_index_in_dim(chunks, (position + shift) % 4, keepdims=False)
        message = piece.astype(jnp.bfloat16)
        if gains is not None:
            message = jnp.concatenate([message, gains_sent], axis=0)
        got = ring_send(message, kind, shift)
        total = total + got[:part].astype(jnp.float32)
        if gains is not None:
            gains_got.append(got[part:])
    if gains is not None:
        canon = in_member_order(gains_got, position).astype(jnp.float32)
        gains = (canon[0] + canon[1]) + (canon[2] + canon[3])
    return total, gains


def gather_stage(rows, kind):
    position = ring_position(kind)
    pieces = [rows] + [ring_send(rows, kind, shift) for shift in (1, 2, 3)]
    canon = in_member_order(pieces, position)
    return canon.reshape(4 * rows.shape[0], rows.shape[1])


AXIS_ORDERS = (("x", "y", "z"), ("y", "z", "x"), ("z", "x", "y"))


def reduce_everywhere(rows, gains):
    seq_devices = lax.axis_size("seq")
    core = lax.axis_index("seq") % 2
    pairs = [(i, i ^ 1) for i in range(seq_devices)]
    half = rows.shape[0] // 2
    halves = rows.reshape(2, half, rows.shape[1])
    own = lax.dynamic_index_in_dim(halves, core, keepdims=False)
    other = lax.dynamic_index_in_dim(halves, 1 - core, keepdims=False)
    gains_sent = gains.astype(jnp.bfloat16)
    got = lax.ppermute(
        jnp.concatenate([other.astype(jnp.bfloat16), gains_sent], axis=0), "seq", pairs
    )
    summed = own + got[:half].astype(jnp.float32)
    gains = gains_sent.astype(jnp.float32) + got[half:].astype(jnp.float32)
    third = half // len(AXIS_ORDERS)
    done = []
    for part_idx, order in enumerate(AXIS_ORDERS):
        part = summed[part_idx * third : (part_idx + 1) * third]
        part_gains = gains if part_idx == 0 else None
        for kind in order:
            part, part_gains = scatter_stage(part, part_gains, kind)
        if part_idx == 0:
            gains = part_gains
        part = part.astype(jnp.bfloat16)
        for kind in reversed(order):
            part = gather_stage(part, kind)
        done.append(part)
    mine = jnp.concatenate(done, axis=0)
    partner = lax.ppermute(mine, "seq", pairs)
    full = in_member_order([mine, partner], core).reshape(rows.shape)
    return full.astype(jnp.float32), gains


def on_device(
    features, curve_pos, pattern, ln1_gain, w_qkv, w_out, ln2_gain, w_up, w_down, out_grad
):
    seq_devices = lax.axis_size("seq")
    seq_index = lax.axis_index("seq")
    dev_rows = features.shape[1]
    capacity = 2 * dev_rows // seq_devices
    blocks_dev = dev_rows // BLK
    position = curve_pos[0]
    send_index, source_for_slot = node_plan(position, seq_index, dev_rows, capacity, seq_devices)
    outgoing = jnp.zeros((seq_devices * capacity, D), jnp.bfloat16).at[send_index].set(features[0])
    arrived = lax.all_to_all(
        outgoing.reshape(seq_devices, capacity, D), "seq", split_axis=0, concat_axis=0, tiled=True
    )
    curve_rows = arrived.reshape(seq_devices * capacity, D)[source_for_slot]
    normed_a, normed1, inverse1 = layer_norm(curve_rows, ln1_gain)
    qkv = jnp.dot(normed_a, w_qkv, preferred_element_type=jnp.float32).astype(jnp.bfloat16)
    queries = qkv[:, :D]
    keyval = qkv[:, D:]
    distances = shift_distances(seq_devices)
    pieces = [keyval]
    for distance in distances:
        pieces.append(from_behind(keyval, "seq", distance))
    keyval_all = jnp.concatenate(pieces, axis=0)
    source_dev = jnp.stack(
        [seq_index] + [(seq_index - distance) % seq_devices for distance in distances]
    )
    key_blocks = (
        source_dev[:, None] * blocks_dev + jnp.arange(blocks_dev, dtype=jnp.int32)[None, :]
    ).reshape(-1)
    own_lists = lax.dynamic_slice_in_dim(pattern[0], seq_index * blocks_dev, blocks_dev, axis=0)
    matches = (own_lists[:, :, None] == key_blocks[None, None, :]).astype(jnp.int32)
    selected = jnp.sum(
        matches * jnp.arange(key_blocks.shape[0], dtype=jnp.int32)[None, None, :], axis=-1
    )
    attn_out, log_totals = attention_forward(queries, keyval_all, selected)
    hidden_res = (
        curve_rows.astype(jnp.float32)
        + jnp.dot(attn_out, w_out, preferred_element_type=jnp.float32)
    ).astype(jnp.bfloat16)
    normed_b, normed2, inverse2 = layer_norm(hidden_res, ln2_gain)
    pre_act = jnp.dot(normed_b, w_up, preferred_element_type=jnp.float32)
    activated = jax.nn.gelu(pre_act, approximate=True).astype(jnp.bfloat16)
    curve_out = (
        hidden_res.astype(jnp.float32)
        + jnp.dot(activated, w_down, preferred_element_type=jnp.float32)
    ).astype(jnp.bfloat16)
    leaving = (
        jnp.zeros((seq_devices * capacity, D), jnp.bfloat16).at[source_for_slot].set(curve_out)
    )
    returned = lax.all_to_all(
        leaving.reshape(seq_devices, capacity, D), "seq", split_axis=0, concat_axis=0, tiled=True
    )
    block_out = returned.reshape(seq_devices * capacity, D)[send_index]
    grad_outgoing = (
        jnp.zeros((seq_devices * capacity, D), jnp.bfloat16).at[send_index].set(out_grad[0])
    )
    grad_arrived = lax.all_to_all(
        grad_outgoing.reshape(seq_devices, capacity, D),
        "seq",
        split_axis=0,
        concat_axis=0,
        tiled=True,
    )
    grad_curve = grad_arrived.reshape(seq_devices * capacity, D)[source_for_slot]
    grad_pre = gelu_back(pre_act, times_transposed(grad_curve, w_down)).astype(jnp.bfloat16)
    grad_down = inner_rows(activated, grad_curve)
    grad_normed_b = times_transposed(grad_pre, w_up)
    grad_up = inner_rows(normed_b, grad_pre)
    grad_gain2 = jnp.sum(grad_normed_b * normed2, axis=0)
    grad_hidden = (
        grad_curve.astype(jnp.float32) + norm_back(grad_normed_b, ln2_gain, normed2, inverse2)
    ).astype(jnp.bfloat16)
    grad_attn = times_transposed(grad_hidden, w_out).astype(jnp.bfloat16)
    grad_out = inner_rows(attn_out, grad_hidden)
    resent = [keyval]
    for distance in distances:
        resent.append(from_behind(keyval, "seq", distance))
    keyval_back = jnp.concatenate(resent, axis=0)
    grad_query, grad_keyval_all = attention_backward(
        queries, keyval_back, selected, attn_out, log_totals, grad_attn
    )
    grad_keyval = grad_keyval_all[:dev_rows]
    for index_pos, distance in enumerate(distances):
        partial_rows = grad_keyval_all[(index_pos + 1) * dev_rows : (index_pos + 2) * dev_rows]
        grad_keyval = grad_keyval + from_behind(
            partial_rows.astype(jnp.bfloat16), "seq", -distance
        ).astype(partial_rows.dtype)
    grad_qkv_rows = jnp.concatenate([grad_query, grad_keyval.astype(jnp.bfloat16)], axis=1)
    grad_normed_a = times_transposed(grad_qkv_rows, w_qkv)
    grad_qkv = inner_rows(normed_a, grad_qkv_rows)
    grad_gain1 = jnp.sum(grad_normed_a * normed1, axis=0)
    grad_curve_in = (
        grad_hidden.astype(jnp.float32) + norm_back(grad_normed_a, ln1_gain, normed1, inverse1)
    ).astype(jnp.bfloat16)
    grad_leaving = (
        jnp.zeros((seq_devices * capacity, D), jnp.bfloat16).at[source_for_slot].set(grad_curve_in)
    )
    grad_returned = lax.all_to_all(
        grad_leaving.reshape(seq_devices, capacity, D),
        "seq",
        split_axis=0,
        concat_axis=0,
        tiled=True,
    )
    input_grad = grad_returned.reshape(seq_devices * capacity, D)[send_index]
    weight_rows = jnp.concatenate(
        [
            grad_qkv.reshape(-1, D),
            grad_out.reshape(-1, D),
            grad_up.reshape(-1, D),
            grad_down.reshape(-1, D),
        ],
        axis=0,
    )
    gain_rows = jnp.zeros((8, D), jnp.float32).at[0].set(grad_gain1).at[1].set(grad_gain2)
    weight_rows, gain_rows = reduce_everywhere(weight_rows, gain_rows)
    sizes = [grad_qkv.size // D, grad_out.size // D, grad_up.size // D, grad_down.size // D]
    offsets = [0, sizes[0], sizes[0] + sizes[1], sizes[0] + sizes[1] + sizes[2]]
    grad_qkv = weight_rows[offsets[0] : offsets[0] + sizes[0]].reshape(grad_qkv.shape)
    grad_out = weight_rows[offsets[1] : offsets[1] + sizes[1]].reshape(grad_out.shape)
    grad_up = weight_rows[offsets[2] : offsets[2] + sizes[2]].reshape(grad_up.shape)
    grad_down = weight_rows[offsets[3] : offsets[3] + sizes[3]].reshape(grad_down.shape)
    grad_gain1 = gain_rows[0]
    grad_gain2 = gain_rows[1]
    return (
        block_out[None],
        input_grad[None],
        grad_qkv,
        grad_out,
        grad_up,
        grad_down,
        grad_gain1,
        grad_gain2,
    )


def solution(mesh):
    return jax.shard_map(
        on_device,
        mesh=mesh,
        in_specs=(
            P("dp", "seq", None),
            P("dp", None),
            P("dp", None, None),
            P(),
            P(),
            P(),
            P(),
            P(),
            P(),
            P("dp", "seq", None),
        ),
        out_specs=(P("dp", "seq", None), P("dp", "seq", None), P(), P(), P(), P(), P(), P()),
        check_vma=False,
    )
```

```python
from functools import partial

import jax
import jax.numpy as jnp
from jax import lax
from jax.sharding import PartitionSpec as P

D = 512
HEADS = 8
BLK = 128


EPSILON = 1e-05


def from_behind(x, axis, by):
    length = lax.axis_size(axis)
    return lax.ppermute(x, axis, [(i, (i + by) % length) for i in range(length)])


def layer_norm(rows_in, gain_vec):
    values = rows_in.astype(jnp.float32)
    centered = values - jnp.mean(values, axis=-1, keepdims=True)
    inverse = lax.rsqrt(jnp.mean(centered * centered, axis=-1, keepdims=True) + EPSILON)
    normed = centered * inverse
    return ((normed * gain_vec).astype(jnp.bfloat16), normed, inverse)


def norm_back(incoming, gain_vec, normed, inverse):
    scaled = incoming * gain_vec
    return inverse * (
        scaled
        - jnp.mean(scaled, axis=-1, keepdims=True)
        - normed * jnp.mean(scaled * normed, axis=-1, keepdims=True)
    )


def gelu_back(pre_act, incoming):
    return jax.vjp(partial(jax.nn.gelu, approximate=True), pre_act)[1](incoming)[0]


def inner_rows(left_mat, right_mat):
    return lax.dot_general(
        left_mat, right_mat, (((0,), (0,)), ((), ())), preferred_element_type=jnp.float32
    )


def times_transposed(left_mat, right_mat):
    return lax.dot_general(
        left_mat, right_mat, (((1,), (1,)), ((), ())), preferred_element_type=jnp.float32
    )


def split_heads(rows_in):
    return rows_in.reshape(rows_in.shape[0] // BLK, BLK, HEADS, D // HEADS)


def listed_heads(keyval_all, selected):
    blocks = keyval_all.reshape(keyval_all.shape[0] // BLK, BLK, 2 * D)
    picked = blocks[selected]
    shape_out = picked.shape[:3] + (HEADS, D // HEADS)
    return (picked[..., :D].reshape(shape_out), picked[..., D:].reshape(shape_out))


def shift_distances(seq_devices):
    levels = seq_devices.bit_length() - 1
    distances = []
    for level_idx in range(levels):
        stride = 2**level_idx
        if 2 * stride == seq_devices:
            distances.append(stride)
        else:
            distances.extend([stride, -stride])
    return distances


def node_plan(position, seq_index, dev_rows, capacity, seq_devices):
    own_position = lax.dynamic_slice_in_dim(position, seq_index * dev_rows, dev_rows)
    target_dev = own_position // dev_rows
    dest_hits = (target_dev[:, None] == jnp.arange(seq_devices, dtype=jnp.int32)[None, :]).astype(
        jnp.int32
    )
    send_rank = jnp.sum((jnp.cumsum(dest_hits, axis=0) - dest_hits) * dest_hits, axis=1)
    send_index = target_dev * capacity + send_rank
    layout = position.reshape(seq_devices, dev_rows)
    arriving = (layout // dev_rows == seq_index).astype(jnp.int32)
    arrive_rank = jnp.cumsum(arriving, axis=1) - arriving
    source_index = jnp.arange(seq_devices, dtype=jnp.int32)[:, None] * capacity + arrive_rank
    del source_index
    total = position.shape[0]
    wanted = seq_index * dev_rows + jnp.arange(dev_rows, dtype=jnp.int32)
    slot_node = jnp.sum(
        jnp.where(
            position[None, :] == wanted[:, None], jnp.arange(total, dtype=jnp.int32)[None, :], 0
        ),
        axis=1,
    )
    source_for_slot = (slot_node // dev_rows) * capacity + arrive_rank.reshape(-1)[slot_node]
    return (send_index, source_for_slot)


def attention_forward(queries, keyval_all, selected):
    query_heads = split_heads(queries)
    key_heads, value_heads = listed_heads(keyval_all, selected)
    scores = (
        jnp.einsum("aihd,akjhd->haikj", query_heads, key_heads, preferred_element_type=jnp.float32)
        * 0.125
    )
    largest = jnp.max(scores, axis=(3, 4), keepdims=True)
    totals = jnp.sum(jnp.exp(scores - largest), axis=(3, 4), keepdims=True)
    log_totals = largest + jnp.log(totals)
    attn_probs = jnp.exp(scores - log_totals).astype(jnp.bfloat16)
    result = jnp.einsum(
        "haikj,akjhd->aihd", attn_probs, value_heads, preferred_element_type=jnp.float32
    )
    return (result.astype(jnp.bfloat16).reshape(queries.shape[0], D), log_totals)


def attention_backward(queries, keyval_all, selected, attn_out, log_totals, grad_attn):
    query_heads = split_heads(queries)
    key_heads, value_heads = listed_heads(keyval_all, selected)
    out_heads = split_heads(attn_out)
    grad_heads = split_heads(grad_attn)
    scores = (
        jnp.einsum("aihd,akjhd->haikj", query_heads, key_heads, preferred_element_type=jnp.float32)
        * 0.125
    )
    attn_exact = jnp.exp(scores - log_totals)
    attn_probs = attn_exact.astype(jnp.bfloat16)
    grad_probs = jnp.einsum(
        "aihd,akjhd->haikj", grad_heads, value_heads, preferred_element_type=jnp.float32
    )
    row_dots = jnp.einsum(
        "aihd,aihd->hai", grad_heads, out_heads, preferred_element_type=jnp.float32
    )[..., None, None]
    grad_scores = (attn_exact * (grad_probs - row_dots) * 0.125).astype(jnp.bfloat16)
    grad_query = jnp.einsum(
        "haikj,akjhd->aihd", grad_scores, key_heads, preferred_element_type=jnp.float32
    )
    grad_keys = jnp.einsum(
        "haikj,aihd->akjhd", grad_scores, query_heads, preferred_element_type=jnp.float32
    )
    grad_values = jnp.einsum(
        "haikj,aihd->akjhd", attn_probs, grad_heads, preferred_element_type=jnp.float32
    )
    block_shape = grad_keys.shape[:3] + (D,)
    grad_picked = jnp.concatenate(
        [grad_keys.reshape(block_shape), grad_values.reshape(block_shape)], axis=-1
    )
    total_rows = keyval_all.shape[0]
    grad_keyval = (
        jnp.zeros((total_rows // BLK, BLK, 2 * D), jnp.float32).at[selected].add(grad_picked)
    )
    return (
        grad_query.astype(jnp.bfloat16).reshape(queries.shape[0], D),
        grad_keyval.reshape(total_rows, 2 * D),
    )


def ring_position(kind):
    seq_index = lax.axis_index("seq")
    if kind == "x":
        return (seq_index // 2) % 4
    if kind == "y":
        return seq_index // 8
    return lax.axis_index("dp")


def ring_send(rows, kind, shift):
    if kind == "z":
        size = lax.axis_size("dp")
        return lax.ppermute(rows, "dp", [(i, (i + shift) % size) for i in range(size)])
    size = lax.axis_size("seq")
    if kind == "x":
        move = lambda i: i - ((i // 2) % 4) * 2 + (((i // 2) % 4 + shift) % 4) * 2
    else:
        move = lambda i: ((i // 8 + shift) % 4) * 8 + i % 8
    return lax.ppermute(rows, "seq", [(i, move(i)) for i in range(size)])


def in_member_order(pieces, position):
    count = len(pieces)
    placed = jnp.zeros((count,) + pieces[0].shape, pieces[0].dtype)
    for offset, piece in enumerate(pieces):
        placed = lax.dynamic_update_index_in_dim(placed, piece, (position - offset) % count, 0)
    return placed


def scatter_stage(rows, gains, kind):
    position = ring_position(kind)
    part = rows.shape[0] // 4
    chunks = rows.reshape(4, part, rows.shape[1])
    total = lax.dynamic_index_in_dim(chunks, position, keepdims=False)
    gains_sent = None if gains is None else gains.astype(jnp.bfloat16)
    gains_got = [gains_sent]
    for shift in (1, 2, 3):
        piece = lax.dynamic_index_in_dim(chunks, (position + shift) % 4, keepdims=False)
        message = piece.astype(jnp.bfloat16)
        if gains is not None:
            message = jnp.concatenate([message, gains_sent], axis=0)
        got = ring_send(message, kind, shift)
        total = total + got[:part].astype(jnp.float32)
        if gains is not None:
            gains_got.append(got[part:])
    if gains is not None:
        canon = in_member_order(gains_got, position).astype(jnp.float32)
        gains = (canon[0] + canon[1]) + (canon[2] + canon[3])
    return total, gains


def gather_stage(rows, kind):
    position = ring_position(kind)
    pieces = [rows] + [ring_send(rows, kind, shift) for shift in (1, 2, 3)]
    canon = in_member_order(pieces, position)
    return canon.reshape(4 * rows.shape[0], rows.shape[1])


AXIS_ORDERS = (("x", "y", "z"),)


def reduce_everywhere(rows, gains):
    seq_devices = lax.axis_size("seq")
    core = lax.axis_index("seq") % 2
    pairs = [(i, i ^ 1) for i in range(seq_devices)]
    half = rows.shape[0] // 2
    halves = rows.reshape(2, half, rows.shape[1])
    own = lax.dynamic_index_in_dim(halves, core, keepdims=False)
    other = lax.dynamic_index_in_dim(halves, 1 - core, keepdims=False)
    gains_sent = gains.astype(jnp.bfloat16)
    got = lax.ppermute(
        jnp.concatenate([other.astype(jnp.bfloat16), gains_sent], axis=0), "seq", pairs
    )
    summed = own + got[:half].astype(jnp.float32)
    gains = gains_sent.astype(jnp.float32) + got[half:].astype(jnp.float32)
    third = half // len(AXIS_ORDERS)
    done = []
    for part_idx, order in enumerate(AXIS_ORDERS):
        part = summed[part_idx * third : (part_idx + 1) * third]
        part_gains = gains if part_idx == 0 else None
        for kind in order:
            part, part_gains = scatter_stage(part, part_gains, kind)
        if part_idx == 0:
            gains = part_gains
        part = part.astype(jnp.bfloat16)
        for kind in reversed(order):
            part = gather_stage(part, kind)
        done.append(part)
    mine = jnp.concatenate(done, axis=0)
    partner = lax.ppermute(mine, "seq", pairs)
    full = in_member_order([mine, partner], core).reshape(rows.shape)
    return full.astype(jnp.float32), gains


def on_device(
    features, curve_pos, pattern, ln1_gain, w_qkv, w_out, ln2_gain, w_up, w_down, out_grad
):
    seq_devices = lax.axis_size("seq")
    seq_index = lax.axis_index("seq")
    dev_rows = features.shape[1]
    capacity = 2 * dev_rows // seq_devices
    blocks_dev = dev_rows // BLK
    position = curve_pos[0]
    send_index, source_for_slot = node_plan(position, seq_index, dev_rows, capacity, seq_devices)
    outgoing = jnp.zeros((seq_devices * capacity, D), jnp.bfloat16).at[send_index].set(features[0])
    arrived = lax.all_to_all(
        outgoing.reshape(seq_devices, capacity, D), "seq", split_axis=0, concat_axis=0, tiled=True
    )
    curve_rows = arrived.reshape(seq_devices * capacity, D)[source_for_slot]
    normed_a, normed1, inverse1 = layer_norm(curve_rows, ln1_gain)
    qkv = jnp.dot(normed_a, w_qkv, preferred_element_type=jnp.float32).astype(jnp.bfloat16)
    queries = qkv[:, :D]
    keyval = qkv[:, D:]
    distances = shift_distances(seq_devices)
    pieces = [keyval]
    for distance in distances:
        pieces.append(from_behind(keyval, "seq", distance))
    keyval_all = jnp.concatenate(pieces, axis=0)
    source_dev = jnp.stack(
        [seq_index] + [(seq_index - distance) % seq_devices for distance in distances]
    )
    key_blocks = (
        source_dev[:, None] * blocks_dev + jnp.arange(blocks_dev, dtype=jnp.int32)[None, :]
    ).reshape(-1)
    own_lists = lax.dynamic_slice_in_dim(pattern[0], seq_index * blocks_dev, blocks_dev, axis=0)
    matches = (own_lists[:, :, None] == key_blocks[None, None, :]).astype(jnp.int32)
    selected = jnp.sum(
        matches * jnp.arange(key_blocks.shape[0], dtype=jnp.int32)[None, None, :], axis=-1
    )
    attn_out, log_totals = attention_forward(queries, keyval_all, selected)
    hidden_res = (
        curve_rows.astype(jnp.float32)
        + jnp.dot(attn_out, w_out, preferred_element_type=jnp.float32)
    ).astype(jnp.bfloat16)
    normed_b, normed2, inverse2 = layer_norm(hidden_res, ln2_gain)
    pre_act = jnp.dot(normed_b, w_up, preferred_element_type=jnp.float32)
    activated = jax.nn.gelu(pre_act, approximate=True).astype(jnp.bfloat16)
    curve_out = (
        hidden_res.astype(jnp.float32)
        + jnp.dot(activated, w_down, preferred_element_type=jnp.float32)
    ).astype(jnp.bfloat16)
    leaving = (
        jnp.zeros((seq_devices * capacity, D), jnp.bfloat16).at[source_for_slot].set(curve_out)
    )
    returned = lax.all_to_all(
        leaving.reshape(seq_devices, capacity, D), "seq", split_axis=0, concat_axis=0, tiled=True
    )
    block_out = returned.reshape(seq_devices * capacity, D)[send_index]
    grad_outgoing = (
        jnp.zeros((seq_devices * capacity, D), jnp.bfloat16).at[send_index].set(out_grad[0])
    )
    grad_arrived = lax.all_to_all(
        grad_outgoing.reshape(seq_devices, capacity, D),
        "seq",
        split_axis=0,
        concat_axis=0,
        tiled=True,
    )
    grad_curve = grad_arrived.reshape(seq_devices * capacity, D)[source_for_slot]
    grad_pre = gelu_back(pre_act, times_transposed(grad_curve, w_down)).astype(jnp.bfloat16)
    grad_down = inner_rows(activated, grad_curve)
    grad_normed_b = times_transposed(grad_pre, w_up)
    grad_up = inner_rows(normed_b, grad_pre)
    grad_gain2 = jnp.sum(grad_normed_b * normed2, axis=0)
    grad_up, grad_down = lax.psum((grad_up, grad_down), ("seq", "dp"))
    grad_hidden = (
        grad_curve.astype(jnp.float32) + norm_back(grad_normed_b, ln2_gain, normed2, inverse2)
    ).astype(jnp.bfloat16)
    grad_attn = times_transposed(grad_hidden, w_out).astype(jnp.bfloat16)
    grad_out = inner_rows(attn_out, grad_hidden)
    resent = [keyval]
    for distance in distances:
        resent.append(from_behind(keyval, "seq", distance))
    keyval_back = jnp.concatenate(resent, axis=0)
    grad_query, grad_keyval_all = attention_backward(
        queries, keyval_back, selected, attn_out, log_totals, grad_attn
    )
    grad_keyval = grad_keyval_all[:dev_rows]
    for index_pos, distance in enumerate(distances):
        partial_rows = grad_keyval_all[(index_pos + 1) * dev_rows : (index_pos + 2) * dev_rows]
        grad_keyval = grad_keyval + from_behind(
            partial_rows.astype(jnp.bfloat16), "seq", -distance
        ).astype(partial_rows.dtype)
    grad_qkv_rows = jnp.concatenate([grad_query, grad_keyval.astype(jnp.bfloat16)], axis=1)
    grad_normed_a = times_transposed(grad_qkv_rows, w_qkv)
    grad_qkv = inner_rows(normed_a, grad_qkv_rows)
    grad_gain1 = jnp.sum(grad_normed_a * normed1, axis=0)
    grad_curve_in = (
        grad_hidden.astype(jnp.float32) + norm_back(grad_normed_a, ln1_gain, normed1, inverse1)
    ).astype(jnp.bfloat16)
    grad_leaving = (
        jnp.zeros((seq_devices * capacity, D), jnp.bfloat16).at[source_for_slot].set(grad_curve_in)
    )
    grad_returned = lax.all_to_all(
        grad_leaving.reshape(seq_devices, capacity, D),
        "seq",
        split_axis=0,
        concat_axis=0,
        tiled=True,
    )
    input_grad = grad_returned.reshape(seq_devices * capacity, D)[send_index]
    weight_rows = jnp.concatenate(
        [grad_qkv[:, index * D : (index + 1) * D] for index in range(3)] + [grad_out], axis=0
    )
    gain_rows = jnp.zeros((8, D), jnp.float32).at[0].set(grad_gain1).at[1].set(grad_gain2)
    weight_rows, gain_rows = reduce_everywhere(weight_rows, gain_rows)
    grad_qkv = jnp.concatenate([weight_rows[index * D : (index + 1) * D] for index in range(3)], axis=1)
    grad_out = weight_rows[3 * D :]
    grad_gain1 = gain_rows[0]
    grad_gain2 = gain_rows[1]
    return (
        block_out[None],
        input_grad[None],
        grad_qkv,
        grad_out,
        grad_up,
        grad_down,
        grad_gain1,
        grad_gain2,
    )


def solution(mesh):
    return jax.shard_map(
        on_device,
        mesh=mesh,
        in_specs=(
            P("dp", "seq", None),
            P("dp", None),
            P("dp", None, None),
            P(),
            P(),
            P(),
            P(),
            P(),
            P(),
            P("dp", "seq", None),
        ),
        out_specs=(P("dp", "seq", None), P("dp", "seq", None), P(), P(), P(), P(), P(), P()),
        check_vma=False,
    )
```

```python
from functools import partial

import jax
import jax.numpy as jnp
from jax import lax
from jax.experimental import pallas as pl
from jax.experimental.pallas import tpu as pltpu
from jax.sharding import PartitionSpec as P

D = 512
HEADS = 8
BLK = 128


EPSILON = 1e-05


def from_behind(x, axis, by):
    length = lax.axis_size(axis)
    return lax.ppermute(x, axis, [(i, (i + by) % length) for i in range(length)])


def layer_norm(rows_in, gain_vec):
    values = rows_in.astype(jnp.float32)
    centered = values - jnp.mean(values, axis=-1, keepdims=True)
    inverse = lax.rsqrt(jnp.mean(centered * centered, axis=-1, keepdims=True) + EPSILON)
    normed = centered * inverse
    return ((normed * gain_vec).astype(jnp.bfloat16), normed, inverse)


def norm_back(incoming, gain_vec, normed, inverse):
    scaled = incoming * gain_vec
    return inverse * (
        scaled
        - jnp.mean(scaled, axis=-1, keepdims=True)
        - normed * jnp.mean(scaled * normed, axis=-1, keepdims=True)
    )


def gelu_back(pre_act, incoming):
    return jax.vjp(partial(jax.nn.gelu, approximate=True), pre_act)[1](incoming)[0]


def inner_rows(left_mat, right_mat):
    return lax.dot_general(
        left_mat, right_mat, (((0,), (0,)), ((), ())), preferred_element_type=jnp.float32
    )


def times_transposed(left_mat, right_mat):
    return lax.dot_general(
        left_mat, right_mat, (((1,), (1,)), ((), ())), preferred_element_type=jnp.float32
    )


def split_heads(rows_in):
    return rows_in.reshape(rows_in.shape[0] // BLK, BLK, HEADS, D // HEADS)


def listed_heads(keyval_all, selected):
    blocks = keyval_all.reshape(keyval_all.shape[0] // BLK, BLK, 2 * D)
    picked = blocks[selected]
    shape_out = picked.shape[:3] + (HEADS, D // HEADS)
    return (picked[..., :D].reshape(shape_out), picked[..., D:].reshape(shape_out))


def shift_distances(seq_devices):
    levels = seq_devices.bit_length() - 1
    distances = []
    for level_idx in range(levels):
        stride = 2**level_idx
        if 2 * stride == seq_devices:
            distances.append(stride)
        else:
            distances.extend([stride, -stride])
    return distances


def node_plan(position, seq_index, dev_rows, capacity, seq_devices):
    own_position = lax.dynamic_slice_in_dim(position, seq_index * dev_rows, dev_rows)
    target_dev = own_position // dev_rows
    dest_hits = (target_dev[:, None] == jnp.arange(seq_devices, dtype=jnp.int32)[None, :]).astype(
        jnp.int32
    )
    send_rank = jnp.sum((jnp.cumsum(dest_hits, axis=0) - dest_hits) * dest_hits, axis=1)
    send_index = target_dev * capacity + send_rank
    layout = position.reshape(seq_devices, dev_rows)
    arriving = (layout // dev_rows == seq_index).astype(jnp.int32)
    arrive_rank = jnp.cumsum(arriving, axis=1) - arriving
    source_index = jnp.arange(seq_devices, dtype=jnp.int32)[:, None] * capacity + arrive_rank
    del source_index
    total = position.shape[0]
    wanted = seq_index * dev_rows + jnp.arange(dev_rows, dtype=jnp.int32)
    slot_node = jnp.sum(
        jnp.where(
            position[None, :] == wanted[:, None], jnp.arange(total, dtype=jnp.int32)[None, :], 0
        ),
        axis=1,
    )
    source_for_slot = (slot_node // dev_rows) * capacity + arrive_rank.reshape(-1)[slot_node]
    return (send_index, source_for_slot)


def attention_forward(queries, keyval_all, selected):
    query_heads = split_heads(queries)
    key_heads, value_heads = listed_heads(keyval_all, selected)
    scores = (
        jnp.einsum("aihd,akjhd->haikj", query_heads, key_heads, preferred_element_type=jnp.float32)
        * 0.125
    )
    largest = jnp.max(scores, axis=(3, 4), keepdims=True)
    totals = jnp.sum(jnp.exp(scores - largest), axis=(3, 4), keepdims=True)
    log_totals = largest + jnp.log(totals)
    attn_probs = jnp.exp(scores - log_totals).astype(jnp.bfloat16)
    result = jnp.einsum(
        "haikj,akjhd->aihd", attn_probs, value_heads, preferred_element_type=jnp.float32
    )
    return (result.astype(jnp.bfloat16).reshape(queries.shape[0], D), log_totals)


def attention_backward(queries, keyval_all, selected, attn_out, log_totals, grad_attn):
    query_heads = split_heads(queries)
    key_heads, value_heads = listed_heads(keyval_all, selected)
    out_heads = split_heads(attn_out)
    grad_heads = split_heads(grad_attn)
    scores = (
        jnp.einsum("aihd,akjhd->haikj", query_heads, key_heads, preferred_element_type=jnp.float32)
        * 0.125
    )
    attn_exact = jnp.exp(scores - log_totals)
    attn_probs = attn_exact.astype(jnp.bfloat16)
    grad_probs = jnp.einsum(
        "aihd,akjhd->haikj", grad_heads, value_heads, preferred_element_type=jnp.float32
    )
    row_dots = jnp.einsum(
        "aihd,aihd->hai", grad_heads, out_heads, preferred_element_type=jnp.float32
    )[..., None, None]
    grad_scores = (attn_exact * (grad_probs - row_dots) * 0.125).astype(jnp.bfloat16)
    grad_query = jnp.einsum(
        "haikj,akjhd->aihd", grad_scores, key_heads, preferred_element_type=jnp.float32
    )
    grad_keys = jnp.einsum(
        "haikj,aihd->akjhd", grad_scores, query_heads, preferred_element_type=jnp.float32
    )
    grad_values = jnp.einsum(
        "haikj,aihd->akjhd", attn_probs, grad_heads, preferred_element_type=jnp.float32
    )
    block_shape = grad_keys.shape[:3] + (D,)
    grad_picked = jnp.concatenate(
        [grad_keys.reshape(block_shape), grad_values.reshape(block_shape)], axis=-1
    )
    total_rows = keyval_all.shape[0]
    grad_keyval = (
        jnp.zeros((total_rows // BLK, BLK, 2 * D), jnp.float32).at[selected].add(grad_picked)
    )
    return (
        grad_query.astype(jnp.bfloat16).reshape(queries.shape[0], D),
        grad_keyval.reshape(total_rows, 2 * D),
    )


MESH_IDS = pl.DeviceIdType.MESH
RING_KINDS = ("x", "y", "z")


def reduce_kernel(w_ref, g_ref, wout_ref, gout_ref, send0, recv0, gsend0, grecv0, *rest):
    ring_bufs = [rest[7 * i : 7 * i + 7] for i in range(3)]
    agz, agy, agx, send_sem, recv_sem = rest[21:]
    seq = lax.axis_index("seq")
    dp = lax.axis_index("dp")
    core = seq % 2
    place = {"x": (seq // 2) % 4, "y": seq // 8, "z": dp}

    def peer(kind, member):
        if kind == "core":
            return (seq + 1 - 2 * core, dp)
        if kind == "x":
            return (seq + (member - place["x"]) * 2, dp)
        if kind == "y":
            return (seq + (member - place["y"]) * 8, dp)
        return (seq, member)

    barrier = pltpu.get_barrier_semaphore()
    peers = [peer("core", 0)]
    for kind in RING_KINDS:
        for shift in (1, 2, 3):
            peers.append(peer(kind, (place[kind] + shift) % 4))
    for target in peers:
        pl.semaphore_signal(barrier, inc=1, device_id=target, device_id_type=MESH_IDS)
    pl.semaphore_wait(barrier, len(peers))

    counter = [0]
    sent = []

    def send(src, dst, recv_index, target):
        copy = pltpu.make_async_remote_copy(
            src_ref=src,
            dst_ref=dst,
            send_sem=send_sem.at[counter[0]],
            recv_sem=recv_sem.at[recv_index],
            device_id=target,
            device_id_type=MESH_IDS,
        )
        counter[0] += 1
        copy.start()
        sent.append(copy)

    def arrive(dst, recv_index):
        pltpu.make_async_remote_copy(
            src_ref=dst,
            dst_ref=dst,
            send_sem=send_sem.at[0],
            recv_sem=recv_sem.at[recv_index],
            device_id=peers[0],
            device_id_type=MESH_IDS,
        ).wait_recv()

    half = send0.shape[0]
    own_rows = pl.ds(pl.multiple_of(core * half, 16), half)
    other_rows = pl.ds(pl.multiple_of((1 - core) * half, 16), half)
    send0[...] = w_ref[other_rows, :].astype(jnp.bfloat16)
    gsend0[...] = g_ref[...].astype(jnp.bfloat16)
    send(send0, recv0, 0, peers[0])
    send(gsend0, grecv0, 1, peers[0])
    arrive(recv0, 0)
    arrive(grecv0, 1)
    gains = gsend0[...].astype(jnp.float32) + grecv0[...].astype(jnp.float32)

    def first_chunk(member, size):
        rows = pl.ds(pl.multiple_of(member * size, 16), size)
        mine = w_ref[pl.ds(pl.multiple_of(core * half + member * size, 16), size), :]
        return mine + recv0[rows, :].astype(jnp.float32)

    source = None
    for stage, kind in enumerate(RING_KINDS):
        sbuf, rbuf, gsend, grecv, total, _, _ = ring_bufs[stage]
        size = sbuf.shape[1]
        pos = place[kind]
        base = 2 + 8 * stage

        def chunk(member, source=source, size=size):
            if source is None:
                return first_chunk(member, size)
            return source[pl.ds(pl.multiple_of(member * size, 16), size), :]

        gsend[...] = gains.astype(jnp.bfloat16)
        grecv[pos] = gsend[...]
        for shift in (1, 2, 3):
            member = (pos + shift) % 4
            sbuf[member] = chunk(member).astype(jnp.bfloat16)
            send(sbuf.at[member], rbuf.at[pos], base + pos, peer(kind, member))
            send(gsend, grecv.at[pos], base + 4 + pos, peer(kind, member))
        total[...] = chunk(pos)
        for shift in (1, 2, 3):
            slot = (pos - shift) % 4
            arrive(rbuf.at[slot], base + slot)
            total[...] += rbuf[slot].astype(jnp.float32)
            arrive(grecv.at[slot], base + 4 + slot)
        parts = grecv[...].astype(jnp.float32)
        gains = (parts[0] + parts[1]) + (parts[2] + parts[3])
        source = total
    gout_ref[...] = gains

    own = source[...].astype(jnp.bfloat16)
    for stage, (kind, gathered) in enumerate(zip(("z", "y", "x"), (agz, agy, agx))):
        pos = place[kind]
        base = 26 + 4 * stage
        gathered[pos] = own
        for shift in (1, 2, 3):
            member = (pos + shift) % 4
            send(gathered.at[pos], gathered.at[pos], base + pos, peer(kind, member))
        for shift in (1, 2, 3):
            arrive(gathered.at[(pos - shift) % 4], base + (pos - shift) % 4)
        own = gathered[...].reshape(4 * gathered.shape[1], gathered.shape[2])
    wout_ref[own_rows, :] = own
    send(wout_ref.at[own_rows], wout_ref.at[own_rows], 38, peers[0])
    arrive(wout_ref.at[other_rows], 38)
    for copy in sent:
        copy.wait_send()


def reduce_everywhere(rows, gains):
    total_rows, width = rows.shape
    half = total_rows // 2
    sizes = [half // 4, half // 16, half // 64]
    scratch = [
        pltpu.VMEM((half, width), jnp.bfloat16),
        pltpu.VMEM((half, width), jnp.bfloat16),
        pltpu.VMEM(gains.shape, jnp.bfloat16),
        pltpu.VMEM(gains.shape, jnp.bfloat16),
    ]
    for size in sizes:
        scratch += [
            pltpu.VMEM((4, size, width), jnp.bfloat16),
            pltpu.VMEM((4, size, width), jnp.bfloat16),
            pltpu.VMEM(gains.shape, jnp.bfloat16),
            pltpu.VMEM((4,) + gains.shape, jnp.bfloat16),
            pltpu.VMEM((size, width), jnp.float32),
            pltpu.VMEM((8, 128), jnp.float32),
            pltpu.VMEM((8, 128), jnp.float32),
        ]
    scratch += [
        pltpu.VMEM((4, sizes[2], width), jnp.bfloat16),
        pltpu.VMEM((4, sizes[1], width), jnp.bfloat16),
        pltpu.VMEM((4, sizes[0], width), jnp.bfloat16),
        pltpu.SemaphoreType.DMA((40,)),
        pltpu.SemaphoreType.DMA((40,)),
    ]
    full, gains = pl.pallas_call(
        reduce_kernel,
        out_shape=(
            jax.ShapeDtypeStruct((total_rows, width), jnp.bfloat16),
            jax.ShapeDtypeStruct(gains.shape, jnp.float32),
        ),
        in_specs=[pl.BlockSpec(memory_space=pltpu.VMEM)] * 2,
        out_specs=(
            pl.BlockSpec(memory_space=pltpu.VMEM),
            pl.BlockSpec(memory_space=pltpu.VMEM),
        ),
        scratch_shapes=scratch,
        compiler_params=pltpu.CompilerParams(
            collective_id=0, has_side_effects=True, vmem_limit_bytes=60 * 1024 * 1024
        ),
    )(rows, gains)
    return full.astype(jnp.float32), gains


def on_device(
    features, curve_pos, pattern, ln1_gain, w_qkv, w_out, ln2_gain, w_up, w_down, out_grad
):
    seq_devices = lax.axis_size("seq")
    seq_index = lax.axis_index("seq")
    dev_rows = features.shape[1]
    capacity = 2 * dev_rows // seq_devices
    blocks_dev = dev_rows // BLK
    position = curve_pos[0]
    send_index, source_for_slot = node_plan(position, seq_index, dev_rows, capacity, seq_devices)
    outgoing = jnp.zeros((seq_devices * capacity, D), jnp.bfloat16).at[send_index].set(features[0])
    arrived = lax.all_to_all(
        outgoing.reshape(seq_devices, capacity, D), "seq", split_axis=0, concat_axis=0, tiled=True
    )
    curve_rows = arrived.reshape(seq_devices * capacity, D)[source_for_slot]
    normed_a, normed1, inverse1 = layer_norm(curve_rows, ln1_gain)
    qkv = jnp.dot(normed_a, w_qkv, preferred_element_type=jnp.float32).astype(jnp.bfloat16)
    queries = qkv[:, :D]
    keyval = qkv[:, D:]
    distances = shift_distances(seq_devices)
    pieces = [keyval]
    for distance in distances:
        pieces.append(from_behind(keyval, "seq", distance))
    keyval_all = jnp.concatenate(pieces, axis=0)
    source_dev = jnp.stack(
        [seq_index] + [(seq_index - distance) % seq_devices for distance in distances]
    )
    key_blocks = (
        source_dev[:, None] * blocks_dev + jnp.arange(blocks_dev, dtype=jnp.int32)[None, :]
    ).reshape(-1)
    own_lists = lax.dynamic_slice_in_dim(pattern[0], seq_index * blocks_dev, blocks_dev, axis=0)
    matches = (own_lists[:, :, None] == key_blocks[None, None, :]).astype(jnp.int32)
    selected = jnp.sum(
        matches * jnp.arange(key_blocks.shape[0], dtype=jnp.int32)[None, None, :], axis=-1
    )
    attn_out, log_totals = attention_forward(queries, keyval_all, selected)
    hidden_res = (
        curve_rows.astype(jnp.float32)
        + jnp.dot(attn_out, w_out, preferred_element_type=jnp.float32)
    ).astype(jnp.bfloat16)
    normed_b, normed2, inverse2 = layer_norm(hidden_res, ln2_gain)
    pre_act = jnp.dot(normed_b, w_up, preferred_element_type=jnp.float32)
    activated = jax.nn.gelu(pre_act, approximate=True).astype(jnp.bfloat16)
    curve_out = (
        hidden_res.astype(jnp.float32)
        + jnp.dot(activated, w_down, preferred_element_type=jnp.float32)
    ).astype(jnp.bfloat16)
    leaving = (
        jnp.zeros((seq_devices * capacity, D), jnp.bfloat16).at[source_for_slot].set(curve_out)
    )
    returned = lax.all_to_all(
        leaving.reshape(seq_devices, capacity, D), "seq", split_axis=0, concat_axis=0, tiled=True
    )
    block_out = returned.reshape(seq_devices * capacity, D)[send_index]
    grad_outgoing = (
        jnp.zeros((seq_devices * capacity, D), jnp.bfloat16).at[send_index].set(out_grad[0])
    )
    grad_arrived = lax.all_to_all(
        grad_outgoing.reshape(seq_devices, capacity, D),
        "seq",
        split_axis=0,
        concat_axis=0,
        tiled=True,
    )
    grad_curve = grad_arrived.reshape(seq_devices * capacity, D)[source_for_slot]
    grad_pre = gelu_back(pre_act, times_transposed(grad_curve, w_down)).astype(jnp.bfloat16)
    grad_down = inner_rows(activated, grad_curve)
    grad_normed_b = times_transposed(grad_pre, w_up)
    grad_up = inner_rows(normed_b, grad_pre)
    grad_gain2 = jnp.sum(grad_normed_b * normed2, axis=0)
    grad_hidden = (
        grad_curve.astype(jnp.float32) + norm_back(grad_normed_b, ln2_gain, normed2, inverse2)
    ).astype(jnp.bfloat16)
    grad_attn = times_transposed(grad_hidden, w_out).astype(jnp.bfloat16)
    grad_out = inner_rows(attn_out, grad_hidden)
    resent = [keyval]
    for distance in distances:
        resent.append(from_behind(keyval, "seq", distance))
    keyval_back = jnp.concatenate(resent, axis=0)
    grad_query, grad_keyval_all = attention_backward(
        queries, keyval_back, selected, attn_out, log_totals, grad_attn
    )
    grad_keyval = grad_keyval_all[:dev_rows]
    for index_pos, distance in enumerate(distances):
        partial_rows = grad_keyval_all[(index_pos + 1) * dev_rows : (index_pos + 2) * dev_rows]
        grad_keyval = grad_keyval + from_behind(
            partial_rows.astype(jnp.bfloat16), "seq", -distance
        ).astype(partial_rows.dtype)
    grad_qkv_rows = jnp.concatenate([grad_query, grad_keyval.astype(jnp.bfloat16)], axis=1)
    grad_normed_a = times_transposed(grad_qkv_rows, w_qkv)
    grad_qkv = inner_rows(normed_a, grad_qkv_rows)
    grad_gain1 = jnp.sum(grad_normed_a * normed1, axis=0)
    grad_curve_in = (
        grad_hidden.astype(jnp.float32) + norm_back(grad_normed_a, ln1_gain, normed1, inverse1)
    ).astype(jnp.bfloat16)
    grad_leaving = (
        jnp.zeros((seq_devices * capacity, D), jnp.bfloat16).at[source_for_slot].set(grad_curve_in)
    )
    grad_returned = lax.all_to_all(
        grad_leaving.reshape(seq_devices, capacity, D),
        "seq",
        split_axis=0,
        concat_axis=0,
        tiled=True,
    )
    input_grad = grad_returned.reshape(seq_devices * capacity, D)[send_index]
    weight_rows = jnp.concatenate(
        [grad_qkv[:, index * D : (index + 1) * D] for index in range(3)]
        + [grad_out, grad_up.reshape(-1, D), grad_down],
        axis=0,
    )
    gain_rows = jnp.zeros((8, D), jnp.float32).at[0].set(grad_gain1).at[1].set(grad_gain2)
    weight_rows, gain_rows = reduce_everywhere(weight_rows, gain_rows)
    grad_qkv = jnp.concatenate([weight_rows[index * D : (index + 1) * D] for index in range(3)], axis=1)
    grad_out = weight_rows[3 * D : 4 * D]
    grad_up = weight_rows[4 * D : 8 * D].reshape(grad_up.shape)
    grad_down = weight_rows[8 * D :]
    grad_gain1 = gain_rows[0]
    grad_gain2 = gain_rows[1]
    return (
        block_out[None],
        input_grad[None],
        grad_qkv,
        grad_out,
        grad_up,
        grad_down,
        grad_gain1,
        grad_gain2,
    )


def solution(mesh):
    return jax.shard_map(
        on_device,
        mesh=mesh,
        in_specs=(
            P("dp", "seq", None),
            P("dp", None),
            P("dp", None, None),
            P(),
            P(),
            P(),
            P(),
            P(),
            P(),
            P("dp", "seq", None),
        ),
        out_specs=(P("dp", "seq", None), P("dp", "seq", None), P(), P(), P(), P(), P(), P()),
        check_vma=False,
    )
```

```python
from functools import partial

import jax
import jax.numpy as jnp
from jax import lax
from jax.experimental import pallas as pl
from jax.experimental.pallas import tpu as pltpu
from jax.sharding import PartitionSpec as P

D = 512
HEADS = 8
BLK = 128


EPSILON = 1e-05


def from_behind(x, axis, by):
    length = lax.axis_size(axis)
    return lax.ppermute(x, axis, [(i, (i + by) % length) for i in range(length)])


def layer_norm(rows_in, gain_vec):
    values = rows_in.astype(jnp.float32)
    centered = values - jnp.mean(values, axis=-1, keepdims=True)
    inverse = lax.rsqrt(jnp.mean(centered * centered, axis=-1, keepdims=True) + EPSILON)
    normed = centered * inverse
    return ((normed * gain_vec).astype(jnp.bfloat16), normed, inverse)


def norm_back(incoming, gain_vec, normed, inverse):
    scaled = incoming * gain_vec
    return inverse * (
        scaled
        - jnp.mean(scaled, axis=-1, keepdims=True)
        - normed * jnp.mean(scaled * normed, axis=-1, keepdims=True)
    )


def gelu_back(pre_act, incoming):
    return jax.vjp(partial(jax.nn.gelu, approximate=True), pre_act)[1](incoming)[0]


def inner_rows(left_mat, right_mat):
    return lax.dot_general(
        left_mat, right_mat, (((0,), (0,)), ((), ())), preferred_element_type=jnp.float32
    )


def times_transposed(left_mat, right_mat):
    return lax.dot_general(
        left_mat, right_mat, (((1,), (1,)), ((), ())), preferred_element_type=jnp.float32
    )


def split_heads(rows_in):
    return rows_in.reshape(rows_in.shape[0] // BLK, BLK, HEADS, D // HEADS)


def listed_heads(keyval_all, selected):
    blocks = keyval_all.reshape(keyval_all.shape[0] // BLK, BLK, 2 * D)
    picked = blocks[selected]
    shape_out = picked.shape[:3] + (HEADS, D // HEADS)
    return (picked[..., :D].reshape(shape_out), picked[..., D:].reshape(shape_out))


def shift_distances(seq_devices):
    levels = seq_devices.bit_length() - 1
    distances = []
    for level_idx in range(levels):
        stride = 2**level_idx
        if 2 * stride == seq_devices:
            distances.append(stride)
        else:
            distances.extend([stride, -stride])
    return distances


def node_plan(position, seq_index, dev_rows, capacity, seq_devices):
    own_position = lax.dynamic_slice_in_dim(position, seq_index * dev_rows, dev_rows)
    target_dev = own_position // dev_rows
    dest_hits = (target_dev[:, None] == jnp.arange(seq_devices, dtype=jnp.int32)[None, :]).astype(
        jnp.int32
    )
    send_rank = jnp.sum((jnp.cumsum(dest_hits, axis=0) - dest_hits) * dest_hits, axis=1)
    send_index = target_dev * capacity + send_rank
    layout = position.reshape(seq_devices, dev_rows)
    arriving = (layout // dev_rows == seq_index).astype(jnp.int32)
    arrive_rank = jnp.cumsum(arriving, axis=1) - arriving
    source_index = jnp.arange(seq_devices, dtype=jnp.int32)[:, None] * capacity + arrive_rank
    del source_index
    total = position.shape[0]
    wanted = seq_index * dev_rows + jnp.arange(dev_rows, dtype=jnp.int32)
    slot_node = jnp.sum(
        jnp.where(
            position[None, :] == wanted[:, None], jnp.arange(total, dtype=jnp.int32)[None, :], 0
        ),
        axis=1,
    )
    source_for_slot = (slot_node // dev_rows) * capacity + arrive_rank.reshape(-1)[slot_node]
    return (send_index, source_for_slot)


def attention_forward(queries, keyval_all, selected):
    query_heads = split_heads(queries)
    key_heads, value_heads = listed_heads(keyval_all, selected)
    scores = (
        jnp.einsum("aihd,akjhd->haikj", query_heads, key_heads, preferred_element_type=jnp.float32)
        * 0.125
    )
    largest = jnp.max(scores, axis=(3, 4), keepdims=True)
    totals = jnp.sum(jnp.exp(scores - largest), axis=(3, 4), keepdims=True)
    log_totals = largest + jnp.log(totals)
    attn_probs = jnp.exp(scores - log_totals).astype(jnp.bfloat16)
    result = jnp.einsum(
        "haikj,akjhd->aihd", attn_probs, value_heads, preferred_element_type=jnp.float32
    )
    return (result.astype(jnp.bfloat16).reshape(queries.shape[0], D), log_totals)


def attention_backward(queries, keyval_all, selected, attn_out, log_totals, grad_attn):
    query_heads = split_heads(queries)
    key_heads, value_heads = listed_heads(keyval_all, selected)
    out_heads = split_heads(attn_out)
    grad_heads = split_heads(grad_attn)
    scores = (
        jnp.einsum("aihd,akjhd->haikj", query_heads, key_heads, preferred_element_type=jnp.float32)
        * 0.125
    )
    attn_exact = jnp.exp(scores - log_totals)
    attn_probs = attn_exact.astype(jnp.bfloat16)
    grad_probs = jnp.einsum(
        "aihd,akjhd->haikj", grad_heads, value_heads, preferred_element_type=jnp.float32
    )
    row_dots = jnp.einsum(
        "aihd,aihd->hai", grad_heads, out_heads, preferred_element_type=jnp.float32
    )[..., None, None]
    grad_scores = (attn_exact * (grad_probs - row_dots) * 0.125).astype(jnp.bfloat16)
    grad_query = jnp.einsum(
        "haikj,akjhd->aihd", grad_scores, key_heads, preferred_element_type=jnp.float32
    )
    grad_keys = jnp.einsum(
        "haikj,aihd->akjhd", grad_scores, query_heads, preferred_element_type=jnp.float32
    )
    grad_values = jnp.einsum(
        "haikj,aihd->akjhd", attn_probs, grad_heads, preferred_element_type=jnp.float32
    )
    block_shape = grad_keys.shape[:3] + (D,)
    grad_picked = jnp.concatenate(
        [grad_keys.reshape(block_shape), grad_values.reshape(block_shape)], axis=-1
    )
    total_rows = keyval_all.shape[0]
    grad_keyval = (
        jnp.zeros((total_rows // BLK, BLK, 2 * D), jnp.float32).at[selected].add(grad_picked)
    )
    return (
        grad_query.astype(jnp.bfloat16).reshape(queries.shape[0], D),
        grad_keyval.reshape(total_rows, 2 * D),
    )


MESH_IDS = pl.DeviceIdType.MESH
RING_KINDS = ("x", "y", "z")
AXIS_ORDERS = (("x", "y", "z"), ("y", "z", "x"), ("z", "x", "y"))


def reduce_kernel(w_ref, g_ref, wout_ref, gout_ref, send0, recv0, gsend0, grecv0, *rest):
    parts = len(AXIS_ORDERS)
    ring_bufs = [[rest[9 * p + 3 * s : 9 * p + 3 * s + 3] for s in range(3)] for p in range(parts)]
    gather_bufs = [rest[9 * parts + 3 * p : 9 * parts + 3 * p + 3] for p in range(parts)]
    gsend, grecv, send_sem, recv_sem = rest[12 * parts :]
    seq = lax.axis_index("seq")
    dp = lax.axis_index("dp")
    core = seq % 2
    place = {"x": (seq // 2) % 4, "y": seq // 8, "z": dp}

    def peer(kind, member):
        if kind == "core":
            return (seq + 1 - 2 * core, dp)
        if kind == "x":
            return (seq + (member - place["x"]) * 2, dp)
        if kind == "y":
            return (seq + (member - place["y"]) * 8, dp)
        return (seq, member)

    barrier = pltpu.get_barrier_semaphore()
    peers = [peer("core", 0)]
    for kind in RING_KINDS:
        for shift in (1, 2, 3):
            peers.append(peer(kind, (place[kind] + shift) % 4))
    for target in peers:
        pl.semaphore_signal(barrier, inc=1, device_id=target, device_id_type=MESH_IDS)
    pl.semaphore_wait(barrier, len(peers))

    counter = [0]
    sent = []

    def send(src, dst, recv_index, target):
        copy = pltpu.make_async_remote_copy(
            src_ref=src,
            dst_ref=dst,
            send_sem=send_sem.at[counter[0]],
            recv_sem=recv_sem.at[recv_index],
            device_id=target,
            device_id_type=MESH_IDS,
        )
        counter[0] += 1
        copy.start()
        sent.append(copy)

    def arrive(dst, recv_index):
        pltpu.make_async_remote_copy(
            src_ref=dst,
            dst_ref=dst,
            send_sem=send_sem.at[0],
            recv_sem=recv_sem.at[recv_index],
            device_id=peers[0],
            device_id_type=MESH_IDS,
        ).wait_recv()

    half = send0.shape[0]
    third = half // parts
    own_rows = pl.ds(pl.multiple_of(core * half, 16), half)
    other_rows = pl.ds(pl.multiple_of((1 - core) * half, 16), half)
    send0[...] = w_ref[other_rows, :].astype(jnp.bfloat16)
    gsend0[...] = g_ref[...].astype(jnp.bfloat16)
    send(send0, recv0, 0, peers[0])
    send(gsend0, grecv0, 1, peers[0])
    arrive(recv0, 0)
    arrive(grecv0, 1)
    gains = gsend0[...].astype(jnp.float32) + grecv0[...].astype(jnp.float32)

    def first_chunk(part, member, size):
        offset = part * third + member * size
        mine = w_ref[pl.ds(pl.multiple_of(core * half + offset, 16), size), :]
        return mine + recv0[pl.ds(pl.multiple_of(offset, 16), size), :].astype(jnp.float32)

    sources = [None] * parts
    for stage in range(3):
        for part in range(parts):
            kind = AXIS_ORDERS[part][stage]
            sbuf, rbuf, total = ring_bufs[part][stage]
            size = sbuf.shape[1]
            pos = place[kind]
            base = 2 + 12 * (3 * part + stage)
            source = sources[part]

            def chunk(member, source=source, size=size, part=part):
                if source is None:
                    return first_chunk(part, member, size)
                return source[pl.ds(pl.multiple_of(member * size, 16), size), :]

            if part == 0:
                gsend[stage] = gains.astype(jnp.bfloat16)
                grecv[stage, pos] = gsend[stage]
            for shift in (1, 2, 3):
                member = (pos + shift) % 4
                sbuf[member] = chunk(member).astype(jnp.bfloat16)
                send(sbuf.at[member], rbuf.at[pos], base + pos, peer(kind, member))
                if part == 0:
                    send(gsend.at[stage], grecv.at[stage, pos], base + 4 + pos, peer(kind, member))
            total[...] = chunk(pos)
        for part in range(parts):
            kind = AXIS_ORDERS[part][stage]
            sbuf, rbuf, total = ring_bufs[part][stage]
            pos = place[kind]
            base = 2 + 12 * (3 * part + stage)
            for shift in (1, 2, 3):
                slot = (pos - shift) % 4
                arrive(rbuf.at[slot], base + slot)
                total[...] += rbuf[slot].astype(jnp.float32)
                if part == 0:
                    arrive(grecv.at[stage, slot], base + 4 + slot)
            if part == 0:
                got = grecv[stage].astype(jnp.float32)
                gains = (got[0] + got[1]) + (got[2] + got[3])
            sources[part] = total
    gout_ref[...] = gains

    owns = [sources[part][...].astype(jnp.bfloat16) for part in range(parts)]
    for stage in range(3):
        for part in range(parts):
            kind = AXIS_ORDERS[part][2 - stage]
            gathered = gather_bufs[part][stage]
            pos = place[kind]
            base = 2 + 12 * 9 + 4 * (3 * part + stage)
            gathered[pos] = owns[part]
            for shift in (1, 2, 3):
                member = (pos + shift) % 4
                send(gathered.at[pos], gathered.at[pos], base + pos, peer(kind, member))
        for part in range(parts):
            kind = AXIS_ORDERS[part][2 - stage]
            gathered = gather_bufs[part][stage]
            pos = place[kind]
            base = 2 + 12 * 9 + 4 * (3 * part + stage)
            for shift in (1, 2, 3):
                arrive(gathered.at[(pos - shift) % 4], base + (pos - shift) % 4)
            owns[part] = gathered[...].reshape(4 * gathered.shape[1], gathered.shape[2])
    for part in range(parts):
        wout_ref[pl.ds(pl.multiple_of(core * half + part * third, 16), third), :] = owns[part]
    last = 2 + 12 * 9 + 4 * 9
    send(wout_ref.at[own_rows], wout_ref.at[own_rows], last, peers[0])
    arrive(wout_ref.at[other_rows], last)
    for copy in sent:
        copy.wait_send()


def reduce_everywhere(rows, gains):
    total_rows, width = rows.shape
    parts = len(AXIS_ORDERS)
    third = total_rows // 2 // parts
    sizes = [third // 4, third // 16, third // 64]
    scratch = [
        pltpu.VMEM((total_rows // 2, width), jnp.bfloat16),
        pltpu.VMEM((total_rows // 2, width), jnp.bfloat16),
        pltpu.VMEM(gains.shape, jnp.bfloat16),
        pltpu.VMEM(gains.shape, jnp.bfloat16),
    ]
    for part in range(parts):
        for size in sizes:
            scratch += [
                pltpu.VMEM((4, size, width), jnp.bfloat16),
                pltpu.VMEM((4, size, width), jnp.bfloat16),
                pltpu.VMEM((size, width), jnp.float32),
            ]
    for part in range(parts):
        for size in reversed(sizes):
            scratch.append(pltpu.VMEM((4, size, width), jnp.bfloat16))
    scratch += [
        pltpu.VMEM((3,) + gains.shape, jnp.bfloat16),
        pltpu.VMEM((3, 4) + gains.shape, jnp.bfloat16),
        pltpu.SemaphoreType.DMA((160,)),
        pltpu.SemaphoreType.DMA((160,)),
    ]
    full, gains = pl.pallas_call(
        reduce_kernel,
        out_shape=(
            jax.ShapeDtypeStruct((total_rows, width), jnp.bfloat16),
            jax.ShapeDtypeStruct(gains.shape, jnp.float32),
        ),
        in_specs=[pl.BlockSpec(memory_space=pltpu.VMEM)] * 2,
        out_specs=(
            pl.BlockSpec(memory_space=pltpu.VMEM),
            pl.BlockSpec(memory_space=pltpu.VMEM),
        ),
        scratch_shapes=scratch,
        compiler_params=pltpu.CompilerParams(
            collective_id=0, has_side_effects=True, vmem_limit_bytes=60 * 1024 * 1024
        ),
    )(rows, gains)
    return full.astype(jnp.float32), gains

def on_device(
    features, curve_pos, pattern, ln1_gain, w_qkv, w_out, ln2_gain, w_up, w_down, out_grad
):
    seq_devices = lax.axis_size("seq")
    seq_index = lax.axis_index("seq")
    dev_rows = features.shape[1]
    capacity = 2 * dev_rows // seq_devices
    blocks_dev = dev_rows // BLK
    position = curve_pos[0]
    send_index, source_for_slot = node_plan(position, seq_index, dev_rows, capacity, seq_devices)
    outgoing = jnp.zeros((seq_devices * capacity, D), jnp.bfloat16).at[send_index].set(features[0])
    arrived = lax.all_to_all(
        outgoing.reshape(seq_devices, capacity, D), "seq", split_axis=0, concat_axis=0, tiled=True
    )
    curve_rows = arrived.reshape(seq_devices * capacity, D)[source_for_slot]
    normed_a, normed1, inverse1 = layer_norm(curve_rows, ln1_gain)
    qkv = jnp.dot(normed_a, w_qkv, preferred_element_type=jnp.float32).astype(jnp.bfloat16)
    queries = qkv[:, :D]
    keyval = qkv[:, D:]
    distances = shift_distances(seq_devices)
    pieces = [keyval]
    for distance in distances:
        pieces.append(from_behind(keyval, "seq", distance))
    keyval_all = jnp.concatenate(pieces, axis=0)
    source_dev = jnp.stack(
        [seq_index] + [(seq_index - distance) % seq_devices for distance in distances]
    )
    key_blocks = (
        source_dev[:, None] * blocks_dev + jnp.arange(blocks_dev, dtype=jnp.int32)[None, :]
    ).reshape(-1)
    own_lists = lax.dynamic_slice_in_dim(pattern[0], seq_index * blocks_dev, blocks_dev, axis=0)
    matches = (own_lists[:, :, None] == key_blocks[None, None, :]).astype(jnp.int32)
    selected = jnp.sum(
        matches * jnp.arange(key_blocks.shape[0], dtype=jnp.int32)[None, None, :], axis=-1
    )
    attn_out, log_totals = attention_forward(queries, keyval_all, selected)
    hidden_res = (
        curve_rows.astype(jnp.float32)
        + jnp.dot(attn_out, w_out, preferred_element_type=jnp.float32)
    ).astype(jnp.bfloat16)
    normed_b, normed2, inverse2 = layer_norm(hidden_res, ln2_gain)
    pre_act = jnp.dot(normed_b, w_up, preferred_element_type=jnp.float32)
    activated = jax.nn.gelu(pre_act, approximate=True).astype(jnp.bfloat16)
    curve_out = (
        hidden_res.astype(jnp.float32)
        + jnp.dot(activated, w_down, preferred_element_type=jnp.float32)
    ).astype(jnp.bfloat16)
    leaving = (
        jnp.zeros((seq_devices * capacity, D), jnp.bfloat16).at[source_for_slot].set(curve_out)
    )
    returned = lax.all_to_all(
        leaving.reshape(seq_devices, capacity, D), "seq", split_axis=0, concat_axis=0, tiled=True
    )
    block_out = returned.reshape(seq_devices * capacity, D)[send_index]
    grad_outgoing = (
        jnp.zeros((seq_devices * capacity, D), jnp.bfloat16).at[send_index].set(out_grad[0])
    )
    grad_arrived = lax.all_to_all(
        grad_outgoing.reshape(seq_devices, capacity, D),
        "seq",
        split_axis=0,
        concat_axis=0,
        tiled=True,
    )
    grad_curve = grad_arrived.reshape(seq_devices * capacity, D)[source_for_slot]
    grad_pre = gelu_back(pre_act, times_transposed(grad_curve, w_down)).astype(jnp.bfloat16)
    grad_down = inner_rows(activated, grad_curve)
    grad_normed_b = times_transposed(grad_pre, w_up)
    grad_up = inner_rows(normed_b, grad_pre)
    grad_gain2 = jnp.sum(grad_normed_b * normed2, axis=0)
    grad_hidden = (
        grad_curve.astype(jnp.float32) + norm_back(grad_normed_b, ln2_gain, normed2, inverse2)
    ).astype(jnp.bfloat16)
    grad_attn = times_transposed(grad_hidden, w_out).astype(jnp.bfloat16)
    grad_out = inner_rows(attn_out, grad_hidden)
    resent = [keyval]
    for distance in distances:
        resent.append(from_behind(keyval, "seq", distance))
    keyval_back = jnp.concatenate(resent, axis=0)
    grad_query, grad_keyval_all = attention_backward(
        queries, keyval_back, selected, attn_out, log_totals, grad_attn
    )
    grad_keyval = grad_keyval_all[:dev_rows]
    for index_pos, distance in enumerate(distances):
        partial_rows = grad_keyval_all[(index_pos + 1) * dev_rows : (index_pos + 2) * dev_rows]
        grad_keyval = grad_keyval + from_behind(
            partial_rows.astype(jnp.bfloat16), "seq", -distance
        ).astype(partial_rows.dtype)
    grad_qkv_rows = jnp.concatenate([grad_query, grad_keyval.astype(jnp.bfloat16)], axis=1)
    grad_normed_a = times_transposed(grad_qkv_rows, w_qkv)
    grad_qkv = inner_rows(normed_a, grad_qkv_rows)
    grad_gain1 = jnp.sum(grad_normed_a * normed1, axis=0)
    grad_curve_in = (
        grad_hidden.astype(jnp.float32) + norm_back(grad_normed_a, ln1_gain, normed1, inverse1)
    ).astype(jnp.bfloat16)
    grad_leaving = (
        jnp.zeros((seq_devices * capacity, D), jnp.bfloat16).at[source_for_slot].set(grad_curve_in)
    )
    grad_returned = lax.all_to_all(
        grad_leaving.reshape(seq_devices, capacity, D),
        "seq",
        split_axis=0,
        concat_axis=0,
        tiled=True,
    )
    input_grad = grad_returned.reshape(seq_devices * capacity, D)[send_index]
    weight_rows = jnp.concatenate(
        [grad_qkv[:, index * D : (index + 1) * D] for index in range(3)]
        + [grad_out, grad_up.reshape(-1, D), grad_down],
        axis=0,
    )
    gain_rows = jnp.zeros((8, D), jnp.float32).at[0].set(grad_gain1).at[1].set(grad_gain2)
    weight_rows, gain_rows = reduce_everywhere(weight_rows, gain_rows)
    grad_qkv = jnp.concatenate([weight_rows[index * D : (index + 1) * D] for index in range(3)], axis=1)
    grad_out = weight_rows[3 * D : 4 * D]
    grad_up = weight_rows[4 * D : 8 * D].reshape(grad_up.shape)
    grad_down = weight_rows[8 * D :]
    grad_gain1 = gain_rows[0]
    grad_gain2 = gain_rows[1]
    return (
        block_out[None],
        input_grad[None],
        grad_qkv,
        grad_out,
        grad_up,
        grad_down,
        grad_gain1,
        grad_gain2,
    )


def solution(mesh):
    return jax.shard_map(
        on_device,
        mesh=mesh,
        in_specs=(
            P("dp", "seq", None),
            P("dp", None),
            P("dp", None, None),
            P(),
            P(),
            P(),
            P(),
            P(),
            P(),
            P("dp", "seq", None),
        ),
        out_specs=(P("dp", "seq", None), P("dp", "seq", None), P(), P(), P(), P(), P(), P()),
        check_vma=False,
    )
```

```python
from functools import partial

import jax
import jax.numpy as jnp
from jax import lax
from jax.experimental import pallas as pl
from jax.experimental.pallas import tpu as pltpu
from jax.sharding import PartitionSpec as P

D = 512
HEADS = 8
BLK = 128


EPSILON = 1e-05


def from_behind(x, axis, by):
    length = lax.axis_size(axis)
    return lax.ppermute(x, axis, [(i, (i + by) % length) for i in range(length)])


def layer_norm(rows_in, gain_vec):
    values = rows_in.astype(jnp.float32)
    centered = values - jnp.mean(values, axis=-1, keepdims=True)
    inverse = lax.rsqrt(jnp.mean(centered * centered, axis=-1, keepdims=True) + EPSILON)
    normed = centered * inverse
    return ((normed * gain_vec).astype(jnp.bfloat16), normed, inverse)


def norm_back(incoming, gain_vec, normed, inverse):
    scaled = incoming * gain_vec
    return inverse * (
        scaled
        - jnp.mean(scaled, axis=-1, keepdims=True)
        - normed * jnp.mean(scaled * normed, axis=-1, keepdims=True)
    )


def gelu_back(pre_act, incoming):
    return jax.vjp(partial(jax.nn.gelu, approximate=True), pre_act)[1](incoming)[0]


def inner_rows(left_mat, right_mat):
    return lax.dot_general(
        left_mat, right_mat, (((0,), (0,)), ((), ())), preferred_element_type=jnp.float32
    )


def times_transposed(left_mat, right_mat):
    return lax.dot_general(
        left_mat, right_mat, (((1,), (1,)), ((), ())), preferred_element_type=jnp.float32
    )


def split_heads(rows_in):
    return rows_in.reshape(rows_in.shape[0] // BLK, BLK, HEADS, D // HEADS)


def listed_heads(keyval_all, selected):
    blocks = keyval_all.reshape(keyval_all.shape[0] // BLK, BLK, 2 * D)
    picked = blocks[selected]
    shape_out = picked.shape[:3] + (HEADS, D // HEADS)
    return (picked[..., :D].reshape(shape_out), picked[..., D:].reshape(shape_out))


def shift_distances(seq_devices):
    levels = seq_devices.bit_length() - 1
    distances = []
    for level_idx in range(levels):
        stride = 2**level_idx
        if 2 * stride == seq_devices:
            distances.append(stride)
        else:
            distances.extend([stride, -stride])
    return distances


def node_plan(position, seq_index, dev_rows, capacity, seq_devices):
    own_position = lax.dynamic_slice_in_dim(position, seq_index * dev_rows, dev_rows)
    target_dev = own_position // dev_rows
    dest_hits = (target_dev[:, None] == jnp.arange(seq_devices, dtype=jnp.int32)[None, :]).astype(
        jnp.int32
    )
    send_rank = jnp.sum((jnp.cumsum(dest_hits, axis=0) - dest_hits) * dest_hits, axis=1)
    send_index = target_dev * capacity + send_rank
    layout = position.reshape(seq_devices, dev_rows)
    arriving = (layout // dev_rows == seq_index).astype(jnp.int32)
    arrive_rank = jnp.cumsum(arriving, axis=1) - arriving
    source_index = jnp.arange(seq_devices, dtype=jnp.int32)[:, None] * capacity + arrive_rank
    del source_index
    total = position.shape[0]
    wanted = seq_index * dev_rows + jnp.arange(dev_rows, dtype=jnp.int32)
    slot_node = jnp.sum(
        jnp.where(
            position[None, :] == wanted[:, None], jnp.arange(total, dtype=jnp.int32)[None, :], 0
        ),
        axis=1,
    )
    source_for_slot = (slot_node // dev_rows) * capacity + arrive_rank.reshape(-1)[slot_node]
    return (send_index, source_for_slot)


def attention_forward(queries, keyval_all, selected):
    query_heads = split_heads(queries)
    key_heads, value_heads = listed_heads(keyval_all, selected)
    scores = (
        jnp.einsum("aihd,akjhd->haikj", query_heads, key_heads, preferred_element_type=jnp.float32)
        * 0.125
    )
    largest = jnp.max(scores, axis=(3, 4), keepdims=True)
    totals = jnp.sum(jnp.exp(scores - largest), axis=(3, 4), keepdims=True)
    log_totals = largest + jnp.log(totals)
    attn_probs = jnp.exp(scores - log_totals).astype(jnp.bfloat16)
    result = jnp.einsum(
        "haikj,akjhd->aihd", attn_probs, value_heads, preferred_element_type=jnp.float32
    )
    return (result.astype(jnp.bfloat16).reshape(queries.shape[0], D), log_totals)


def attention_backward(queries, keyval_all, selected, attn_out, log_totals, grad_attn):
    query_heads = split_heads(queries)
    key_heads, value_heads = listed_heads(keyval_all, selected)
    out_heads = split_heads(attn_out)
    grad_heads = split_heads(grad_attn)
    scores = (
        jnp.einsum("aihd,akjhd->haikj", query_heads, key_heads, preferred_element_type=jnp.float32)
        * 0.125
    )
    attn_exact = jnp.exp(scores - log_totals)
    attn_probs = attn_exact.astype(jnp.bfloat16)
    grad_probs = jnp.einsum(
        "aihd,akjhd->haikj", grad_heads, value_heads, preferred_element_type=jnp.float32
    )
    row_dots = jnp.einsum(
        "aihd,aihd->hai", grad_heads, out_heads, preferred_element_type=jnp.float32
    )[..., None, None]
    grad_scores = (attn_exact * (grad_probs - row_dots) * 0.125).astype(jnp.bfloat16)
    grad_query = jnp.einsum(
        "haikj,akjhd->aihd", grad_scores, key_heads, preferred_element_type=jnp.float32
    )
    grad_keys = jnp.einsum(
        "haikj,aihd->akjhd", grad_scores, query_heads, preferred_element_type=jnp.float32
    )
    grad_values = jnp.einsum(
        "haikj,aihd->akjhd", attn_probs, grad_heads, preferred_element_type=jnp.float32
    )
    block_shape = grad_keys.shape[:3] + (D,)
    grad_picked = jnp.concatenate(
        [grad_keys.reshape(block_shape), grad_values.reshape(block_shape)], axis=-1
    )
    total_rows = keyval_all.shape[0]
    grad_keyval = (
        jnp.zeros((total_rows // BLK, BLK, 2 * D), jnp.float32).at[selected].add(grad_picked)
    )
    return (
        grad_query.astype(jnp.bfloat16).reshape(queries.shape[0], D),
        grad_keyval.reshape(total_rows, 2 * D),
    )


MESH_IDS = pl.DeviceIdType.MESH
RING_KINDS = ("x", "y", "z")
AXIS_ORDERS = (("x", "y", "z"), ("y", "z", "x"), ("z", "x", "y"))


def reduce_kernel(w_ref, g_ref, wout_ref, gout_ref, send0, recv0, gsend0, grecv0, *rest):
    parts = len(AXIS_ORDERS)
    ring_bufs = [[rest[9 * p + 3 * s : 9 * p + 3 * s + 3] for s in range(3)] for p in range(parts)]
    gather_bufs = [rest[9 * parts + 3 * p : 9 * parts + 3 * p + 3] for p in range(parts)]
    gsend, grecv, send_sem, recv_sem = rest[12 * parts :]
    seq = lax.axis_index("seq")
    dp = lax.axis_index("dp")
    core = seq % 2
    place = {"x": (seq // 2) % 4, "y": seq // 8, "z": dp}

    def peer(kind, member):
        if kind == "core":
            return (seq + 1 - 2 * core, dp)
        if kind == "x":
            return (seq + (member - place["x"]) * 2, dp)
        if kind == "y":
            return (seq + (member - place["y"]) * 8, dp)
        return (seq, member)

    barrier = pltpu.get_barrier_semaphore()
    peers = [peer("core", 0)]
    for kind in RING_KINDS:
        for shift in (1, 2, 3):
            peers.append(peer(kind, (place[kind] + shift) % 4))
    for target in peers:
        pl.semaphore_signal(barrier, inc=1, device_id=target, device_id_type=MESH_IDS)
    pl.semaphore_wait(barrier, len(peers))

    counter = [0]
    sent = []

    def send(src, dst, recv_index, target):
        copy = pltpu.make_async_remote_copy(
            src_ref=src,
            dst_ref=dst,
            send_sem=send_sem.at[counter[0]],
            recv_sem=recv_sem.at[recv_index],
            device_id=target,
            device_id_type=MESH_IDS,
        )
        counter[0] += 1
        copy.start()
        sent.append(copy)

    def arrive(dst, recv_index):
        pltpu.make_async_remote_copy(
            src_ref=dst,
            dst_ref=dst,
            send_sem=send_sem.at[0],
            recv_sem=recv_sem.at[recv_index],
            device_id=peers[0],
            device_id_type=MESH_IDS,
        ).wait_recv()

    half = send0.shape[0]
    third = half // parts
    own_rows = pl.ds(pl.multiple_of(core * half, 16), half)
    other_rows = pl.ds(pl.multiple_of((1 - core) * half, 16), half)
    send0[...] = w_ref[other_rows, :].astype(jnp.bfloat16)
    gsend0[...] = g_ref[...].astype(jnp.bfloat16)
    send(send0, recv0, 0, peers[0])
    send(gsend0, grecv0, 1, peers[0])
    arrive(recv0, 0)
    arrive(grecv0, 1)
    gains = gsend0[...].astype(jnp.float32) + grecv0[...].astype(jnp.float32)

    def first_chunk(part, member, size):
        offset = part * third + member * size
        mine = w_ref[pl.ds(pl.multiple_of(core * half + offset, 16), size), :]
        return mine + recv0[pl.ds(pl.multiple_of(offset, 16), size), :].astype(jnp.float32)

    sources = [None] * parts
    for stage in range(3):
        for part in range(parts):
            kind = AXIS_ORDERS[part][stage]
            sbuf, rbuf, total = ring_bufs[part][stage]
            size = sbuf.shape[1]
            pos = place[kind]
            base = 2 + 12 * (3 * part + stage)
            source = sources[part]

            def chunk(member, source=source, size=size, part=part):
                if source is None:
                    return first_chunk(part, member, size)
                return source[pl.ds(pl.multiple_of(member * size, 16), size), :]

            if part == 0:
                gsend[stage] = gains.astype(jnp.bfloat16)
                grecv[stage, pos] = gsend[stage]
            for shift in (1, 2, 3):
                member = (pos + shift) % 4
                sbuf[member] = chunk(member).astype(jnp.bfloat16)
                send(sbuf.at[member], rbuf.at[pos], base + pos, peer(kind, member))
                if part == 0:
                    send(gsend.at[stage], grecv.at[stage, pos], base + 4 + pos, peer(kind, member))
            total[...] = chunk(pos)
        for part in range(parts):
            kind = AXIS_ORDERS[part][stage]
            sbuf, rbuf, total = ring_bufs[part][stage]
            pos = place[kind]
            base = 2 + 12 * (3 * part + stage)
            for shift in (1, 2, 3):
                slot = (pos - shift) % 4
                arrive(rbuf.at[slot], base + slot)
                total[...] += rbuf[slot].astype(jnp.float32)
                if part == 0:
                    arrive(grecv.at[stage, slot], base + 4 + slot)
            if part == 0:
                got = grecv[stage].astype(jnp.float32)
                gains = (got[0] + got[1]) + (got[2] + got[3])
            sources[part] = total
    gout_ref[...] = gains

    owns = [sources[part][...].astype(jnp.bfloat16) for part in range(parts)]
    for stage in range(3):
        for part in range(parts):
            kind = AXIS_ORDERS[part][2 - stage]
            gathered = gather_bufs[part][stage]
            pos = place[kind]
            base = 2 + 12 * 9 + 4 * (3 * part + stage)
            gathered[pos] = owns[part]
            for shift in (1, 2, 3):
                member = (pos + shift) % 4
                send(gathered.at[pos], gathered.at[pos], base + pos, peer(kind, member))
        for part in range(parts):
            kind = AXIS_ORDERS[part][2 - stage]
            gathered = gather_bufs[part][stage]
            pos = place[kind]
            base = 2 + 12 * 9 + 4 * (3 * part + stage)
            for shift in (1, 2, 3):
                arrive(gathered.at[(pos - shift) % 4], base + (pos - shift) % 4)
            owns[part] = gathered[...].reshape(4 * gathered.shape[1], gathered.shape[2])
    for part in range(parts):
        wout_ref[pl.ds(pl.multiple_of(core * half + part * third, 16), third), :] = owns[part]
    last = 2 + 12 * 9 + 4 * 9
    send(wout_ref.at[own_rows], wout_ref.at[own_rows], last, peers[0])
    arrive(wout_ref.at[other_rows], last)
    for copy in sent:
        copy.wait_send()


def reduce_everywhere(rows, gains):
    total_rows, width = rows.shape
    parts = len(AXIS_ORDERS)
    third = total_rows // 2 // parts
    sizes = [third // 4, third // 16, third // 64]
    scratch = [
        pltpu.VMEM((total_rows // 2, width), jnp.bfloat16),
        pltpu.VMEM((total_rows // 2, width), jnp.bfloat16),
        pltpu.VMEM(gains.shape, jnp.bfloat16),
        pltpu.VMEM(gains.shape, jnp.bfloat16),
    ]
    for part in range(parts):
        for size in sizes:
            scratch += [
                pltpu.VMEM((4, size, width), jnp.bfloat16),
                pltpu.VMEM((4, size, width), jnp.bfloat16),
                pltpu.VMEM((size, width), jnp.float32),
            ]
    for part in range(parts):
        for size in reversed(sizes):
            scratch.append(pltpu.VMEM((4, size, width), jnp.bfloat16))
    scratch += [
        pltpu.VMEM((3,) + gains.shape, jnp.bfloat16),
        pltpu.VMEM((3, 4) + gains.shape, jnp.bfloat16),
        pltpu.SemaphoreType.DMA((160,)),
        pltpu.SemaphoreType.DMA((160,)),
    ]
    full, gains = pl.pallas_call(
        reduce_kernel,
        out_shape=(
            jax.ShapeDtypeStruct((total_rows, width), jnp.bfloat16),
            jax.ShapeDtypeStruct(gains.shape, jnp.float32),
        ),
        in_specs=[pl.BlockSpec(memory_space=pltpu.VMEM)] * 2,
        out_specs=(
            pl.BlockSpec(memory_space=pltpu.VMEM),
            pl.BlockSpec(memory_space=pltpu.VMEM),
        ),
        scratch_shapes=scratch,
        compiler_params=pltpu.CompilerParams(
            collective_id=0, has_side_effects=True, vmem_limit_bytes=60 * 1024 * 1024
        ),
    )(rows, gains)
    return full.astype(jnp.float32), gains

def exchange_kernel(direction, rows_ref, out_ref, send_sem, recv_sem):
    seq = lax.axis_index("seq")
    dp = lax.axis_index("dp")
    seq_devices = lax.axis_size("seq")
    distances = shift_distances(seq_devices)
    barrier = pltpu.get_barrier_semaphore()
    for distance in distances:
        target = ((seq + distance) % seq_devices, dp)
        pl.semaphore_signal(barrier, inc=1, device_id=target, device_id_type=MESH_IDS)
    pl.semaphore_wait(barrier, len(distances))
    copies = []
    for index, distance in enumerate(distances):
        target = ((seq + direction * distance) % seq_devices, dp)
        source = rows_ref if direction == 1 else rows_ref.at[index]
        copy = pltpu.make_async_remote_copy(
            src_ref=source,
            dst_ref=out_ref.at[index],
            send_sem=send_sem.at[index],
            recv_sem=recv_sem.at[index],
            device_id=target,
            device_id_type=MESH_IDS,
        )
        copy.start()
        copies.append(copy)
    for copy in copies:
        copy.wait_recv()
    for copy in copies:
        copy.wait_send()


def exchange(rows, direction, collective):
    count = len(shift_distances(lax.axis_size("seq")))
    shape = rows.shape if direction == 1 else rows.shape[1:]
    return pl.pallas_call(
        partial(exchange_kernel, direction),
        out_shape=jax.ShapeDtypeStruct((count,) + shape, rows.dtype),
        in_specs=[pl.BlockSpec(memory_space=pltpu.VMEM)],
        out_specs=pl.BlockSpec(memory_space=pltpu.VMEM),
        scratch_shapes=[pltpu.SemaphoreType.DMA((count,)), pltpu.SemaphoreType.DMA((count,))],
        compiler_params=pltpu.CompilerParams(collective_id=collective, has_side_effects=True),
    )(rows)


def on_device(
    features, curve_pos, pattern, ln1_gain, w_qkv, w_out, ln2_gain, w_up, w_down, out_grad
):
    seq_devices = lax.axis_size("seq")
    seq_index = lax.axis_index("seq")
    dev_rows = features.shape[1]
    capacity = 2 * dev_rows // seq_devices
    blocks_dev = dev_rows // BLK
    position = curve_pos[0]
    send_index, source_for_slot = node_plan(position, seq_index, dev_rows, capacity, seq_devices)
    outgoing = jnp.zeros((seq_devices * capacity, D), jnp.bfloat16).at[send_index].set(features[0])
    arrived = lax.all_to_all(
        outgoing.reshape(seq_devices, capacity, D), "seq", split_axis=0, concat_axis=0, tiled=True
    )
    curve_rows = arrived.reshape(seq_devices * capacity, D)[source_for_slot]
    normed_a, normed1, inverse1 = layer_norm(curve_rows, ln1_gain)
    qkv = jnp.dot(normed_a, w_qkv, preferred_element_type=jnp.float32).astype(jnp.bfloat16)
    queries = qkv[:, :D]
    keyval = qkv[:, D:]
    distances = shift_distances(seq_devices)
    arrived_kv = exchange(keyval, 1, 1)
    keyval_all = jnp.concatenate([keyval, arrived_kv.reshape(-1, 2 * D)], axis=0)
    source_dev = jnp.stack(
        [seq_index] + [(seq_index - distance) % seq_devices for distance in distances]
    )
    key_blocks = (
        source_dev[:, None] * blocks_dev + jnp.arange(blocks_dev, dtype=jnp.int32)[None, :]
    ).reshape(-1)
    own_lists = lax.dynamic_slice_in_dim(pattern[0], seq_index * blocks_dev, blocks_dev, axis=0)
    matches = (own_lists[:, :, None] == key_blocks[None, None, :]).astype(jnp.int32)
    selected = jnp.sum(
        matches * jnp.arange(key_blocks.shape[0], dtype=jnp.int32)[None, None, :], axis=-1
    )
    attn_out, log_totals = attention_forward(queries, keyval_all, selected)
    hidden_res = (
        curve_rows.astype(jnp.float32)
        + jnp.dot(attn_out, w_out, preferred_element_type=jnp.float32)
    ).astype(jnp.bfloat16)
    normed_b, normed2, inverse2 = layer_norm(hidden_res, ln2_gain)
    pre_act = jnp.dot(normed_b, w_up, preferred_element_type=jnp.float32)
    activated = jax.nn.gelu(pre_act, approximate=True).astype(jnp.bfloat16)
    curve_out = (
        hidden_res.astype(jnp.float32)
        + jnp.dot(activated, w_down, preferred_element_type=jnp.float32)
    ).astype(jnp.bfloat16)
    leaving = (
        jnp.zeros((seq_devices * capacity, D), jnp.bfloat16).at[source_for_slot].set(curve_out)
    )
    returned = lax.all_to_all(
        leaving.reshape(seq_devices, capacity, D), "seq", split_axis=0, concat_axis=0, tiled=True
    )
    block_out = returned.reshape(seq_devices * capacity, D)[send_index]
    grad_outgoing = (
        jnp.zeros((seq_devices * capacity, D), jnp.bfloat16).at[send_index].set(out_grad[0])
    )
    grad_arrived = lax.all_to_all(
        grad_outgoing.reshape(seq_devices, capacity, D),
        "seq",
        split_axis=0,
        concat_axis=0,
        tiled=True,
    )
    grad_curve = grad_arrived.reshape(seq_devices * capacity, D)[source_for_slot]
    grad_pre = gelu_back(pre_act, times_transposed(grad_curve, w_down)).astype(jnp.bfloat16)
    grad_down = inner_rows(activated, grad_curve)
    grad_normed_b = times_transposed(grad_pre, w_up)
    grad_up = inner_rows(normed_b, grad_pre)
    grad_gain2 = jnp.sum(grad_normed_b * normed2, axis=0)
    grad_hidden = (
        grad_curve.astype(jnp.float32) + norm_back(grad_normed_b, ln2_gain, normed2, inverse2)
    ).astype(jnp.bfloat16)
    grad_attn = times_transposed(grad_hidden, w_out).astype(jnp.bfloat16)
    grad_out = inner_rows(attn_out, grad_hidden)
    grad_query, grad_keyval_all = attention_backward(
        queries, keyval_all, selected, attn_out, log_totals, grad_attn
    )
    returned_kv = exchange(
        grad_keyval_all[dev_rows:].astype(jnp.bfloat16).reshape(len(distances), dev_rows, 2 * D),
        -1,
        2,
    )
    grad_keyval = grad_keyval_all[:dev_rows] + jnp.sum(returned_kv.astype(jnp.float32), axis=0)
    grad_qkv_rows = jnp.concatenate([grad_query, grad_keyval.astype(jnp.bfloat16)], axis=1)
    grad_normed_a = times_transposed(grad_qkv_rows, w_qkv)
    grad_qkv = inner_rows(normed_a, grad_qkv_rows)
    grad_gain1 = jnp.sum(grad_normed_a * normed1, axis=0)
    grad_curve_in = (
        grad_hidden.astype(jnp.float32) + norm_back(grad_normed_a, ln1_gain, normed1, inverse1)
    ).astype(jnp.bfloat16)
    grad_leaving = (
        jnp.zeros((seq_devices * capacity, D), jnp.bfloat16).at[source_for_slot].set(grad_curve_in)
    )
    grad_returned = lax.all_to_all(
        grad_leaving.reshape(seq_devices, capacity, D),
        "seq",
        split_axis=0,
        concat_axis=0,
        tiled=True,
    )
    input_grad = grad_returned.reshape(seq_devices * capacity, D)[send_index]
    weight_rows = jnp.concatenate(
        [grad_qkv[:, index * D : (index + 1) * D] for index in range(3)]
        + [grad_out, grad_up.reshape(-1, D), grad_down],
        axis=0,
    )
    gain_rows = jnp.zeros((8, D), jnp.float32).at[0].set(grad_gain1).at[1].set(grad_gain2)
    weight_rows, gain_rows = reduce_everywhere(weight_rows, gain_rows)
    grad_qkv = jnp.concatenate([weight_rows[index * D : (index + 1) * D] for index in range(3)], axis=1)
    grad_out = weight_rows[3 * D : 4 * D]
    grad_up = weight_rows[4 * D : 8 * D].reshape(grad_up.shape)
    grad_down = weight_rows[8 * D :]
    grad_gain1 = gain_rows[0]
    grad_gain2 = gain_rows[1]
    return (
        block_out[None],
        input_grad[None],
        grad_qkv,
        grad_out,
        grad_up,
        grad_down,
        grad_gain1,
        grad_gain2,
    )


def solution(mesh):
    return jax.shard_map(
        on_device,
        mesh=mesh,
        in_specs=(
            P("dp", "seq", None),
            P("dp", None),
            P("dp", None, None),
            P(),
            P(),
            P(),
            P(),
            P(),
            P(),
            P("dp", "seq", None),
        ),
        out_specs=(P("dp", "seq", None), P("dp", "seq", None), P(), P(), P(), P(), P(), P()),
        check_vma=False,
    )
```

```python
from functools import partial

import jax
import jax.numpy as jnp
from jax import lax
from jax.experimental import pallas as pl
from jax.experimental.pallas import tpu as pltpu
from jax.sharding import PartitionSpec as P

D = 512
HEADS = 8
BLK = 128


EPSILON = 1e-05


def from_behind(x, axis, by):
    length = lax.axis_size(axis)
    return lax.ppermute(x, axis, [(i, (i + by) % length) for i in range(length)])


def layer_norm(rows_in, gain_vec):
    values = rows_in.astype(jnp.float32)
    centered = values - jnp.mean(values, axis=-1, keepdims=True)
    inverse = lax.rsqrt(jnp.mean(centered * centered, axis=-1, keepdims=True) + EPSILON)
    normed = centered * inverse
    return ((normed * gain_vec).astype(jnp.bfloat16), normed, inverse)


def norm_back(incoming, gain_vec, normed, inverse):
    scaled = incoming * gain_vec
    return inverse * (
        scaled
        - jnp.mean(scaled, axis=-1, keepdims=True)
        - normed * jnp.mean(scaled * normed, axis=-1, keepdims=True)
    )


def gelu_back(pre_act, incoming):
    return jax.vjp(partial(jax.nn.gelu, approximate=True), pre_act)[1](incoming)[0]


def inner_rows(left_mat, right_mat):
    return lax.dot_general(
        left_mat, right_mat, (((0,), (0,)), ((), ())), preferred_element_type=jnp.float32
    )


def times_transposed(left_mat, right_mat):
    return lax.dot_general(
        left_mat, right_mat, (((1,), (1,)), ((), ())), preferred_element_type=jnp.float32
    )


def split_heads(rows_in):
    return rows_in.reshape(rows_in.shape[0] // BLK, BLK, HEADS, D // HEADS)


def listed_heads(keyval_all, selected):
    blocks = keyval_all.reshape(keyval_all.shape[0] // BLK, BLK, 2 * D)
    picked = blocks[selected]
    shape_out = picked.shape[:3] + (HEADS, D // HEADS)
    return (picked[..., :D].reshape(shape_out), picked[..., D:].reshape(shape_out))


def shift_distances(seq_devices):
    levels = seq_devices.bit_length() - 1
    distances = []
    for level_idx in range(levels):
        stride = 2**level_idx
        if 2 * stride == seq_devices:
            distances.append(stride)
        else:
            distances.extend([stride, -stride])
    return distances


def node_plan(position, seq_index, dev_rows, capacity, seq_devices):
    own_position = lax.dynamic_slice_in_dim(position, seq_index * dev_rows, dev_rows)
    target_dev = own_position // dev_rows
    dest_hits = (target_dev[:, None] == jnp.arange(seq_devices, dtype=jnp.int32)[None, :]).astype(
        jnp.int32
    )
    send_rank = jnp.sum((jnp.cumsum(dest_hits, axis=0) - dest_hits) * dest_hits, axis=1)
    send_index = target_dev * capacity + send_rank
    layout = position.reshape(seq_devices, dev_rows)
    arriving = (layout // dev_rows == seq_index).astype(jnp.int32)
    arrive_rank = jnp.cumsum(arriving, axis=1) - arriving
    source_index = jnp.arange(seq_devices, dtype=jnp.int32)[:, None] * capacity + arrive_rank
    del source_index
    total = position.shape[0]
    wanted = seq_index * dev_rows + jnp.arange(dev_rows, dtype=jnp.int32)
    slot_node = jnp.sum(
        jnp.where(
            position[None, :] == wanted[:, None], jnp.arange(total, dtype=jnp.int32)[None, :], 0
        ),
        axis=1,
    )
    source_for_slot = (slot_node // dev_rows) * capacity + arrive_rank.reshape(-1)[slot_node]
    return (send_index, source_for_slot)


def attention_forward(queries, keyval_all, selected):
    query_heads = split_heads(queries)
    key_heads, value_heads = listed_heads(keyval_all, selected)
    scores = (
        jnp.einsum("aihd,akjhd->haikj", query_heads, key_heads, preferred_element_type=jnp.float32)
        * 0.125
    )
    largest = jnp.max(scores, axis=(3, 4), keepdims=True)
    totals = jnp.sum(jnp.exp(scores - largest), axis=(3, 4), keepdims=True)
    log_totals = largest + jnp.log(totals)
    attn_probs = jnp.exp(scores - log_totals).astype(jnp.bfloat16)
    result = jnp.einsum(
        "haikj,akjhd->aihd", attn_probs, value_heads, preferred_element_type=jnp.float32
    )
    return (result.astype(jnp.bfloat16).reshape(queries.shape[0], D), log_totals)


def attention_backward(queries, keyval_all, selected, attn_out, log_totals, grad_attn):
    query_heads = split_heads(queries)
    key_heads, value_heads = listed_heads(keyval_all, selected)
    out_heads = split_heads(attn_out)
    grad_heads = split_heads(grad_attn)
    scores = (
        jnp.einsum("aihd,akjhd->haikj", query_heads, key_heads, preferred_element_type=jnp.float32)
        * 0.125
    )
    attn_exact = jnp.exp(scores - log_totals)
    attn_probs = attn_exact.astype(jnp.bfloat16)
    grad_probs = jnp.einsum(
        "aihd,akjhd->haikj", grad_heads, value_heads, preferred_element_type=jnp.float32
    )
    row_dots = jnp.einsum(
        "aihd,aihd->hai", grad_heads, out_heads, preferred_element_type=jnp.float32
    )[..., None, None]
    grad_scores = (attn_exact * (grad_probs - row_dots) * 0.125).astype(jnp.bfloat16)
    grad_query = jnp.einsum(
        "haikj,akjhd->aihd", grad_scores, key_heads, preferred_element_type=jnp.float32
    )
    grad_keys = jnp.einsum(
        "haikj,aihd->akjhd", grad_scores, query_heads, preferred_element_type=jnp.float32
    )
    grad_values = jnp.einsum(
        "haikj,aihd->akjhd", attn_probs, grad_heads, preferred_element_type=jnp.float32
    )
    block_shape = grad_keys.shape[:3] + (D,)
    grad_picked = jnp.concatenate(
        [grad_keys.reshape(block_shape), grad_values.reshape(block_shape)], axis=-1
    )
    total_rows = keyval_all.shape[0]
    one_hot = (
        selected[:, :, None] == jnp.arange(total_rows // BLK, dtype=jnp.int32)[None, None, :]
    ).astype(jnp.float32)
    grad_keyval = jnp.einsum(
        "akb,akjc->bjc",
        one_hot,
        grad_picked,
        precision=lax.Precision.HIGHEST,
        preferred_element_type=jnp.float32,
    )
    return (
        grad_query.astype(jnp.bfloat16).reshape(queries.shape[0], D),
        grad_keyval.reshape(total_rows, 2 * D),
    )


MESH_IDS = pl.DeviceIdType.MESH
RING_KINDS = ("x", "y", "z")
AXIS_ORDERS = (("x", "y", "z"), ("y", "z", "x"), ("z", "x", "y"))


def reduce_kernel(w_ref, g_ref, wout_ref, gout_ref, send0, recv0, gsend0, grecv0, *rest):
    parts = len(AXIS_ORDERS)
    ring_bufs = [[rest[9 * p + 3 * s : 9 * p + 3 * s + 3] for s in range(3)] for p in range(parts)]
    gather_bufs = [rest[9 * parts + 3 * p : 9 * parts + 3 * p + 3] for p in range(parts)]
    gsend, grecv, send_sem, recv_sem = rest[12 * parts :]
    seq = lax.axis_index("seq")
    dp = lax.axis_index("dp")
    core = seq % 2
    place = {"x": (seq // 2) % 4, "y": seq // 8, "z": dp}

    def peer(kind, member):
        if kind == "core":
            return (seq + 1 - 2 * core, dp)
        if kind == "x":
            return (seq + (member - place["x"]) * 2, dp)
        if kind == "y":
            return (seq + (member - place["y"]) * 8, dp)
        return (seq, member)

    barrier = pltpu.get_barrier_semaphore()
    peers = [peer("core", 0)]
    for kind in RING_KINDS:
        for shift in (1, 2, 3):
            peers.append(peer(kind, (place[kind] + shift) % 4))
    for target in peers:
        pl.semaphore_signal(barrier, inc=1, device_id=target, device_id_type=MESH_IDS)
    pl.semaphore_wait(barrier, len(peers))

    counter = [0]
    sent = []

    def send(src, dst, recv_index, target):
        copy = pltpu.make_async_remote_copy(
            src_ref=src,
            dst_ref=dst,
            send_sem=send_sem.at[counter[0]],
            recv_sem=recv_sem.at[recv_index],
            device_id=target,
            device_id_type=MESH_IDS,
        )
        counter[0] += 1
        copy.start()
        sent.append(copy)

    def arrive(dst, recv_index):
        pltpu.make_async_remote_copy(
            src_ref=dst,
            dst_ref=dst,
            send_sem=send_sem.at[0],
            recv_sem=recv_sem.at[recv_index],
            device_id=peers[0],
            device_id_type=MESH_IDS,
        ).wait_recv()

    half = send0.shape[0]
    third = half // parts
    own_rows = pl.ds(pl.multiple_of(core * half, 16), half)
    other_rows = pl.ds(pl.multiple_of((1 - core) * half, 16), half)
    send0[...] = w_ref[other_rows, :].astype(jnp.bfloat16)
    gsend0[...] = g_ref[...].astype(jnp.bfloat16)
    send(send0, recv0, 0, peers[0])
    send(gsend0, grecv0, 1, peers[0])
    arrive(recv0, 0)
    arrive(grecv0, 1)
    gains = gsend0[...].astype(jnp.float32) + grecv0[...].astype(jnp.float32)

    def first_chunk(part, member, size):
        offset = part * third + member * size
        mine = w_ref[pl.ds(pl.multiple_of(core * half + offset, 16), size), :]
        return mine + recv0[pl.ds(pl.multiple_of(offset, 16), size), :].astype(jnp.float32)

    sources = [None] * parts
    for stage in range(3):
        for part in range(parts):
            kind = AXIS_ORDERS[part][stage]
            sbuf, rbuf, total = ring_bufs[part][stage]
            size = sbuf.shape[1]
            pos = place[kind]
            base = 2 + 12 * (3 * part + stage)
            source = sources[part]

            def chunk(member, source=source, size=size, part=part):
                if source is None:
                    return first_chunk(part, member, size)
                return source[pl.ds(pl.multiple_of(member * size, 16), size), :]

            if part == 0:
                gsend[stage] = gains.astype(jnp.bfloat16)
                grecv[stage, pos] = gsend[stage]
            for shift in (1, 2, 3):
                member = (pos + shift) % 4
                sbuf[member] = chunk(member).astype(jnp.bfloat16)
                send(sbuf.at[member], rbuf.at[pos], base + pos, peer(kind, member))
                if part == 0:
                    send(gsend.at[stage], grecv.at[stage, pos], base + 4 + pos, peer(kind, member))
            total[...] = chunk(pos)
        for part in range(parts):
            kind = AXIS_ORDERS[part][stage]
            sbuf, rbuf, total = ring_bufs[part][stage]
            pos = place[kind]
            base = 2 + 12 * (3 * part + stage)
            for shift in (1, 2, 3):
                slot = (pos - shift) % 4
                arrive(rbuf.at[slot], base + slot)
                total[...] += rbuf[slot].astype(jnp.float32)
                if part == 0:
                    arrive(grecv.at[stage, slot], base + 4 + slot)
            if part == 0:
                got = grecv[stage].astype(jnp.float32)
                gains = (got[0] + got[1]) + (got[2] + got[3])
            sources[part] = total
    gout_ref[...] = gains

    owns = [sources[part][...].astype(jnp.bfloat16) for part in range(parts)]
    for stage in range(3):
        for part in range(parts):
            kind = AXIS_ORDERS[part][2 - stage]
            gathered = gather_bufs[part][stage]
            pos = place[kind]
            base = 2 + 12 * 9 + 4 * (3 * part + stage)
            gathered[pos] = owns[part]
            for shift in (1, 2, 3):
                member = (pos + shift) % 4
                send(gathered.at[pos], gathered.at[pos], base + pos, peer(kind, member))
        for part in range(parts):
            kind = AXIS_ORDERS[part][2 - stage]
            gathered = gather_bufs[part][stage]
            pos = place[kind]
            base = 2 + 12 * 9 + 4 * (3 * part + stage)
            for shift in (1, 2, 3):
                arrive(gathered.at[(pos - shift) % 4], base + (pos - shift) % 4)
            owns[part] = gathered[...].reshape(4 * gathered.shape[1], gathered.shape[2])
    for part in range(parts):
        wout_ref[pl.ds(pl.multiple_of(core * half + part * third, 16), third), :] = owns[part]
    last = 2 + 12 * 9 + 4 * 9
    send(wout_ref.at[own_rows], wout_ref.at[own_rows], last, peers[0])
    arrive(wout_ref.at[other_rows], last)
    for copy in sent:
        copy.wait_send()


def reduce_everywhere(rows, gains):
    total_rows, width = rows.shape
    parts = len(AXIS_ORDERS)
    third = total_rows // 2 // parts
    sizes = [third // 4, third // 16, third // 64]
    scratch = [
        pltpu.VMEM((total_rows // 2, width), jnp.bfloat16),
        pltpu.VMEM((total_rows // 2, width), jnp.bfloat16),
        pltpu.VMEM(gains.shape, jnp.bfloat16),
        pltpu.VMEM(gains.shape, jnp.bfloat16),
    ]
    for part in range(parts):
        for size in sizes:
            scratch += [
                pltpu.VMEM((4, size, width), jnp.bfloat16),
                pltpu.VMEM((4, size, width), jnp.bfloat16),
                pltpu.VMEM((size, width), jnp.float32),
            ]
    for part in range(parts):
        for size in reversed(sizes):
            scratch.append(pltpu.VMEM((4, size, width), jnp.bfloat16))
    scratch += [
        pltpu.VMEM((3,) + gains.shape, jnp.bfloat16),
        pltpu.VMEM((3, 4) + gains.shape, jnp.bfloat16),
        pltpu.SemaphoreType.DMA((160,)),
        pltpu.SemaphoreType.DMA((160,)),
    ]
    full, gains = pl.pallas_call(
        reduce_kernel,
        out_shape=(
            jax.ShapeDtypeStruct((total_rows, width), jnp.bfloat16),
            jax.ShapeDtypeStruct(gains.shape, jnp.float32),
        ),
        in_specs=[pl.BlockSpec(memory_space=pltpu.VMEM)] * 2,
        out_specs=(
            pl.BlockSpec(memory_space=pltpu.VMEM),
            pl.BlockSpec(memory_space=pltpu.VMEM),
        ),
        scratch_shapes=scratch,
        compiler_params=pltpu.CompilerParams(
            collective_id=0, has_side_effects=True, vmem_limit_bytes=60 * 1024 * 1024
        ),
    )(rows, gains)
    return full.astype(jnp.float32), gains

def on_device(
    features, curve_pos, pattern, ln1_gain, w_qkv, w_out, ln2_gain, w_up, w_down, out_grad
):
    seq_devices = lax.axis_size("seq")
    seq_index = lax.axis_index("seq")
    dev_rows = features.shape[1]
    capacity = 2 * dev_rows // seq_devices
    blocks_dev = dev_rows // BLK
    position = curve_pos[0]
    send_index, source_for_slot = node_plan(position, seq_index, dev_rows, capacity, seq_devices)
    outgoing = jnp.zeros((seq_devices * capacity, D), jnp.bfloat16).at[send_index].set(features[0])
    arrived = lax.all_to_all(
        outgoing.reshape(seq_devices, capacity, D), "seq", split_axis=0, concat_axis=0, tiled=True
    )
    curve_rows = arrived.reshape(seq_devices * capacity, D)[source_for_slot]
    normed_a, normed1, inverse1 = layer_norm(curve_rows, ln1_gain)
    qkv = jnp.dot(normed_a, w_qkv, preferred_element_type=jnp.float32).astype(jnp.bfloat16)
    queries = qkv[:, :D]
    keyval = qkv[:, D:]
    distances = shift_distances(seq_devices)
    pieces = [keyval]
    for distance in distances:
        pieces.append(from_behind(keyval, "seq", distance))
    keyval_all = jnp.concatenate(pieces, axis=0)
    source_dev = jnp.stack(
        [seq_index] + [(seq_index - distance) % seq_devices for distance in distances]
    )
    key_blocks = (
        source_dev[:, None] * blocks_dev + jnp.arange(blocks_dev, dtype=jnp.int32)[None, :]
    ).reshape(-1)
    own_lists = lax.dynamic_slice_in_dim(pattern[0], seq_index * blocks_dev, blocks_dev, axis=0)
    matches = (own_lists[:, :, None] == key_blocks[None, None, :]).astype(jnp.int32)
    selected = jnp.sum(
        matches * jnp.arange(key_blocks.shape[0], dtype=jnp.int32)[None, None, :], axis=-1
    )
    attn_out, log_totals = attention_forward(queries, keyval_all, selected)
    hidden_res = (
        curve_rows.astype(jnp.float32)
        + jnp.dot(attn_out, w_out, preferred_element_type=jnp.float32)
    ).astype(jnp.bfloat16)
    normed_b, normed2, inverse2 = layer_norm(hidden_res, ln2_gain)
    pre_act = jnp.dot(normed_b, w_up, preferred_element_type=jnp.float32)
    activated = jax.nn.gelu(pre_act, approximate=True).astype(jnp.bfloat16)
    curve_out = (
        hidden_res.astype(jnp.float32)
        + jnp.dot(activated, w_down, preferred_element_type=jnp.float32)
    ).astype(jnp.bfloat16)
    leaving = (
        jnp.zeros((seq_devices * capacity, D), jnp.bfloat16).at[source_for_slot].set(curve_out)
    )
    returned = lax.all_to_all(
        leaving.reshape(seq_devices, capacity, D), "seq", split_axis=0, concat_axis=0, tiled=True
    )
    block_out = returned.reshape(seq_devices * capacity, D)[send_index]
    grad_outgoing = (
        jnp.zeros((seq_devices * capacity, D), jnp.bfloat16).at[send_index].set(out_grad[0])
    )
    grad_arrived = lax.all_to_all(
        grad_outgoing.reshape(seq_devices, capacity, D),
        "seq",
        split_axis=0,
        concat_axis=0,
        tiled=True,
    )
    grad_curve = grad_arrived.reshape(seq_devices * capacity, D)[source_for_slot]
    grad_pre = gelu_back(pre_act, times_transposed(grad_curve, w_down)).astype(jnp.bfloat16)
    grad_down = inner_rows(activated, grad_curve)
    grad_normed_b = times_transposed(grad_pre, w_up)
    grad_up = inner_rows(normed_b, grad_pre)
    grad_gain2 = jnp.sum(grad_normed_b * normed2, axis=0)
    grad_hidden = (
        grad_curve.astype(jnp.float32) + norm_back(grad_normed_b, ln2_gain, normed2, inverse2)
    ).astype(jnp.bfloat16)
    grad_attn = times_transposed(grad_hidden, w_out).astype(jnp.bfloat16)
    grad_out = inner_rows(attn_out, grad_hidden)
    resent = [keyval]
    for distance in distances:
        resent.append(from_behind(keyval, "seq", distance))
    keyval_back = jnp.concatenate(resent, axis=0)
    grad_query, grad_keyval_all = attention_backward(
        queries, keyval_back, selected, attn_out, log_totals, grad_attn
    )
    grad_keyval = grad_keyval_all[:dev_rows]
    for index_pos, distance in enumerate(distances):
        partial_rows = grad_keyval_all[(index_pos + 1) * dev_rows : (index_pos + 2) * dev_rows]
        grad_keyval = grad_keyval + from_behind(
            partial_rows.astype(jnp.bfloat16), "seq", -distance
        ).astype(partial_rows.dtype)
    grad_qkv_rows = jnp.concatenate([grad_query, grad_keyval.astype(jnp.bfloat16)], axis=1)
    grad_normed_a = times_transposed(grad_qkv_rows, w_qkv)
    grad_qkv = inner_rows(normed_a, grad_qkv_rows)
    grad_gain1 = jnp.sum(grad_normed_a * normed1, axis=0)
    grad_curve_in = (
        grad_hidden.astype(jnp.float32) + norm_back(grad_normed_a, ln1_gain, normed1, inverse1)
    ).astype(jnp.bfloat16)
    grad_leaving = (
        jnp.zeros((seq_devices * capacity, D), jnp.bfloat16).at[source_for_slot].set(grad_curve_in)
    )
    grad_returned = lax.all_to_all(
        grad_leaving.reshape(seq_devices, capacity, D),
        "seq",
        split_axis=0,
        concat_axis=0,
        tiled=True,
    )
    input_grad = grad_returned.reshape(seq_devices * capacity, D)[send_index]
    weight_rows = jnp.concatenate(
        [grad_qkv[:, index * D : (index + 1) * D] for index in range(3)]
        + [grad_out]
        + [grad_up[:, index * D : (index + 1) * D] for index in range(4)]
        + [grad_down],
        axis=0,
    )
    gain_rows = jnp.zeros((8, D), jnp.float32).at[0].set(grad_gain1).at[1].set(grad_gain2)
    weight_rows, gain_rows = reduce_everywhere(weight_rows, gain_rows)
    grad_qkv = jnp.concatenate([weight_rows[index * D : (index + 1) * D] for index in range(3)], axis=1)
    grad_out = weight_rows[3 * D : 4 * D]
    grad_up = jnp.concatenate(
        [weight_rows[(4 + index) * D : (5 + index) * D] for index in range(4)], axis=1
    )
    grad_down = weight_rows[8 * D :]
    grad_gain1 = gain_rows[0]
    grad_gain2 = gain_rows[1]
    return (
        block_out[None],
        input_grad[None],
        grad_qkv,
        grad_out,
        grad_up,
        grad_down,
        grad_gain1,
        grad_gain2,
    )


def solution(mesh):
    return jax.shard_map(
        on_device,
        mesh=mesh,
        in_specs=(
            P("dp", "seq", None),
            P("dp", None),
            P("dp", None, None),
            P(),
            P(),
            P(),
            P(),
            P(),
            P(),
            P("dp", "seq", None),
        ),
        out_specs=(P("dp", "seq", None), P("dp", "seq", None), P(), P(), P(), P(), P(), P()),
        check_vma=False,
    )
```

```python
from functools import partial

import jax
import jax.numpy as jnp
from jax import lax
from jax.experimental import pallas as pl
from jax.experimental.pallas import tpu as pltpu
from jax.sharding import PartitionSpec as P

D = 512
HEADS = 8
BLK = 128


EPSILON = 1e-05


def from_behind(x, axis, by):
    length = lax.axis_size(axis)
    return lax.ppermute(x, axis, [(i, (i + by) % length) for i in range(length)])


def layer_norm(rows_in, gain_vec):
    values = rows_in.astype(jnp.float32)
    centered = values - jnp.mean(values, axis=-1, keepdims=True)
    inverse = lax.rsqrt(jnp.mean(centered * centered, axis=-1, keepdims=True) + EPSILON)
    normed = centered * inverse
    return ((normed * gain_vec).astype(jnp.bfloat16), normed, inverse)


def norm_back(incoming, gain_vec, normed, inverse):
    scaled = incoming * gain_vec
    return inverse * (
        scaled
        - jnp.mean(scaled, axis=-1, keepdims=True)
        - normed * jnp.mean(scaled * normed, axis=-1, keepdims=True)
    )


def gelu_back(pre_act, incoming):
    return jax.vjp(partial(jax.nn.gelu, approximate=True), pre_act)[1](incoming)[0]


def inner_rows(left_mat, right_mat):
    return lax.dot_general(
        left_mat, right_mat, (((0,), (0,)), ((), ())), preferred_element_type=jnp.float32
    )


def times_transposed(left_mat, right_mat):
    return lax.dot_general(
        left_mat, right_mat, (((1,), (1,)), ((), ())), preferred_element_type=jnp.float32
    )


def split_heads(rows_in):
    return rows_in.reshape(rows_in.shape[0] // BLK, BLK, HEADS, D // HEADS)


def listed_heads(keyval_all, selected):
    blocks = keyval_all.reshape(keyval_all.shape[0] // BLK, BLK, 2 * D)
    picked = blocks[selected]
    shape_out = picked.shape[:3] + (HEADS, D // HEADS)
    return (picked[..., :D].reshape(shape_out), picked[..., D:].reshape(shape_out))


def shift_distances(seq_devices):
    levels = seq_devices.bit_length() - 1
    distances = []
    for level_idx in range(levels):
        stride = 2**level_idx
        if 2 * stride == seq_devices:
            distances.append(stride)
        else:
            distances.extend([stride, -stride])
    return distances


def node_plan(position, seq_index, dev_rows, capacity, seq_devices):
    own_position = lax.dynamic_slice_in_dim(position, seq_index * dev_rows, dev_rows)
    target_dev = own_position // dev_rows
    dest_hits = (target_dev[:, None] == jnp.arange(seq_devices, dtype=jnp.int32)[None, :]).astype(
        jnp.int32
    )
    send_rank = jnp.sum((jnp.cumsum(dest_hits, axis=0) - dest_hits) * dest_hits, axis=1)
    send_index = target_dev * capacity + send_rank
    layout = position.reshape(seq_devices, dev_rows)
    arriving = (layout // dev_rows == seq_index).astype(jnp.int32)
    arrive_rank = jnp.cumsum(arriving, axis=1) - arriving
    source_index = jnp.arange(seq_devices, dtype=jnp.int32)[:, None] * capacity + arrive_rank
    del source_index
    total = position.shape[0]
    wanted = seq_index * dev_rows + jnp.arange(dev_rows, dtype=jnp.int32)
    slot_node = jnp.sum(
        jnp.where(
            position[None, :] == wanted[:, None], jnp.arange(total, dtype=jnp.int32)[None, :], 0
        ),
        axis=1,
    )
    source_for_slot = (slot_node // dev_rows) * capacity + arrive_rank.reshape(-1)[slot_node]
    return (send_index, source_for_slot)


def attention_forward(queries, keyval_all, selected):
    query_heads = split_heads(queries)
    key_heads, value_heads = listed_heads(keyval_all, selected)
    scores = (
        jnp.einsum("aihd,akjhd->haikj", query_heads, key_heads, preferred_element_type=jnp.float32)
        * 0.125
    )
    largest = jnp.max(scores, axis=(3, 4), keepdims=True)
    totals = jnp.sum(jnp.exp(scores - largest), axis=(3, 4), keepdims=True)
    log_totals = largest + jnp.log(totals)
    attn_probs = jnp.exp(scores - log_totals).astype(jnp.bfloat16)
    result = jnp.einsum(
        "haikj,akjhd->aihd", attn_probs, value_heads, preferred_element_type=jnp.float32
    )
    return (result.astype(jnp.bfloat16).reshape(queries.shape[0], D), log_totals)


def attention_backward(queries, keyval_all, selected, attn_out, log_totals, grad_attn):
    query_heads = split_heads(queries)
    key_heads, value_heads = listed_heads(keyval_all, selected)
    out_heads = split_heads(attn_out)
    grad_heads = split_heads(grad_attn)
    scores = (
        jnp.einsum("aihd,akjhd->haikj", query_heads, key_heads, preferred_element_type=jnp.float32)
        * 0.125
    )
    attn_exact = jnp.exp(scores - log_totals)
    attn_probs = attn_exact.astype(jnp.bfloat16)
    grad_probs = jnp.einsum(
        "aihd,akjhd->haikj", grad_heads, value_heads, preferred_element_type=jnp.float32
    )
    row_dots = jnp.einsum(
        "aihd,aihd->hai", grad_heads, out_heads, preferred_element_type=jnp.float32
    )[..., None, None]
    grad_scores = (attn_exact * (grad_probs - row_dots) * 0.125).astype(jnp.bfloat16)
    grad_query = jnp.einsum(
        "haikj,akjhd->aihd", grad_scores, key_heads, preferred_element_type=jnp.float32
    )
    grad_keys = jnp.einsum(
        "haikj,aihd->akjhd", grad_scores, query_heads, preferred_element_type=jnp.float32
    )
    grad_values = jnp.einsum(
        "haikj,aihd->akjhd", attn_probs, grad_heads, preferred_element_type=jnp.float32
    )
    block_shape = grad_keys.shape[:3] + (D,)
    grad_picked = jnp.concatenate(
        [grad_keys.reshape(block_shape), grad_values.reshape(block_shape)], axis=-1
    )
    total_rows = keyval_all.shape[0]
    one_hot = (
        selected[:, :, None] == jnp.arange(total_rows // BLK, dtype=jnp.int32)[None, None, :]
    ).astype(jnp.float32)
    grad_keyval = jnp.einsum(
        "akb,akjc->bjc",
        one_hot,
        grad_picked,
        precision=lax.Precision.HIGHEST,
        preferred_element_type=jnp.float32,
    )
    return (
        grad_query.astype(jnp.bfloat16).reshape(queries.shape[0], D),
        grad_keyval.reshape(total_rows, 2 * D),
    )


MESH_IDS = pl.DeviceIdType.MESH
RING_KINDS = ("x", "y", "z")
AXIS_ORDERS = (("x", "y", "z"), ("y", "z", "x"), ("z", "x", "y"))


def reduce_kernel(w_ref, g_ref, wout_ref, gout_ref, send0, recv0, gsend0, grecv0, *rest):
    parts = len(AXIS_ORDERS)
    ring_bufs = [[rest[9 * p + 3 * s : 9 * p + 3 * s + 3] for s in range(3)] for p in range(parts)]
    gather_bufs = [rest[9 * parts + 3 * p : 9 * parts + 3 * p + 3] for p in range(parts)]
    gsend, grecv, send_sem, recv_sem = rest[12 * parts :]
    seq = lax.axis_index("seq")
    dp = lax.axis_index("dp")
    core = seq % 2
    place = {"x": (seq // 2) % 4, "y": seq // 8, "z": dp}

    def peer(kind, member):
        if kind == "core":
            return (seq + 1 - 2 * core, dp)
        if kind == "x":
            return (seq + (member - place["x"]) * 2, dp)
        if kind == "y":
            return (seq + (member - place["y"]) * 8, dp)
        return (seq, member)

    barrier = pltpu.get_barrier_semaphore()
    peers = [peer("core", 0)]
    for kind in RING_KINDS:
        for shift in (1, 2, 3):
            peers.append(peer(kind, (place[kind] + shift) % 4))
    for target in peers:
        pl.semaphore_signal(barrier, inc=1, device_id=target, device_id_type=MESH_IDS)
    pl.semaphore_wait(barrier, len(peers))

    counter = [0]
    sent = []

    def send(src, dst, recv_index, target):
        copy = pltpu.make_async_remote_copy(
            src_ref=src,
            dst_ref=dst,
            send_sem=send_sem.at[counter[0]],
            recv_sem=recv_sem.at[recv_index],
            device_id=target,
            device_id_type=MESH_IDS,
        )
        counter[0] += 1
        copy.start()
        sent.append(copy)

    def arrive(dst, recv_index):
        pltpu.make_async_remote_copy(
            src_ref=dst,
            dst_ref=dst,
            send_sem=send_sem.at[0],
            recv_sem=recv_sem.at[recv_index],
            device_id=peers[0],
            device_id_type=MESH_IDS,
        ).wait_recv()

    half = send0.shape[0]
    third = half // parts
    gsend0[...] = g_ref[...].astype(jnp.bfloat16)
    send(gsend0, grecv0, 1, peers[0])
    for part in range(parts):
        rows = pl.ds(pl.multiple_of(part * third, 16), third)
        source_rows = pl.ds(pl.multiple_of((1 - core) * half + part * third, 16), third)
        send0[rows, :] = w_ref[source_rows, :].astype(jnp.bfloat16)
        send(send0.at[rows], recv0.at[rows], 150 + part, peers[0])
    arrive(grecv0, 1)
    gains = gsend0[...].astype(jnp.float32) + grecv0[...].astype(jnp.float32)

    def first_chunk(part, member, size):
        offset = part * third + member * size
        mine = w_ref[pl.ds(pl.multiple_of(core * half + offset, 16), size), :]
        return mine + recv0[pl.ds(pl.multiple_of(offset, 16), size), :].astype(jnp.float32)

    sources = [None] * parts
    for stage in range(3):
        for part in range(parts):
            kind = AXIS_ORDERS[part][stage]
            sbuf, rbuf, total = ring_bufs[part][stage]
            size = sbuf.shape[1]
            pos = place[kind]
            base = 2 + 12 * (3 * part + stage)
            source = sources[part]

            def chunk(member, source=source, size=size, part=part):
                if source is None:
                    return first_chunk(part, member, size)
                return source[pl.ds(pl.multiple_of(member * size, 16), size), :]

            if stage == 0:
                arrive(recv0.at[pl.ds(pl.multiple_of(part * third, 16), third)], 150 + part)
            if part == 0:
                gsend[stage] = gains.astype(jnp.bfloat16)
                grecv[stage, pos] = gsend[stage]
            for shift in (1, 2, 3):
                member = (pos + shift) % 4
                sbuf[member] = chunk(member).astype(jnp.bfloat16)
                send(sbuf.at[member], rbuf.at[pos], base + pos, peer(kind, member))
                if part == 0:
                    send(gsend.at[stage], grecv.at[stage, pos], base + 4 + pos, peer(kind, member))
            total[...] = chunk(pos)
        for part in range(parts):
            kind = AXIS_ORDERS[part][stage]
            sbuf, rbuf, total = ring_bufs[part][stage]
            pos = place[kind]
            base = 2 + 12 * (3 * part + stage)
            for shift in (1, 2, 3):
                slot = (pos - shift) % 4
                arrive(rbuf.at[slot], base + slot)
                total[...] += rbuf[slot].astype(jnp.float32)
                if part == 0:
                    arrive(grecv.at[stage, slot], base + 4 + slot)
            if part == 0:
                got = grecv[stage].astype(jnp.float32)
                gains = (got[0] + got[1]) + (got[2] + got[3])
            sources[part] = total
    gout_ref[...] = gains

    owns = [sources[part][...].astype(jnp.bfloat16) for part in range(parts)]
    for stage in range(3):
        for part in range(parts):
            kind = AXIS_ORDERS[part][2 - stage]
            gathered = gather_bufs[part][stage]
            pos = place[kind]
            base = 2 + 12 * 9 + 4 * (3 * part + stage)
            gathered[pos] = owns[part]
            for shift in (1, 2, 3):
                member = (pos + shift) % 4
                send(gathered.at[pos], gathered.at[pos], base + pos, peer(kind, member))
        for part in range(parts):
            kind = AXIS_ORDERS[part][2 - stage]
            gathered = gather_bufs[part][stage]
            pos = place[kind]
            base = 2 + 12 * 9 + 4 * (3 * part + stage)
            for shift in (1, 2, 3):
                arrive(gathered.at[(pos - shift) % 4], base + (pos - shift) % 4)
            owns[part] = gathered[...].reshape(4 * gathered.shape[1], gathered.shape[2])
            if stage == 2:
                rows = pl.ds(pl.multiple_of(core * half + part * third, 16), third)
                wout_ref[rows, :] = owns[part]
                send(wout_ref.at[rows], wout_ref.at[rows], 154 + part, peers[0])
    for part in range(parts):
        rows = pl.ds(pl.multiple_of((1 - core) * half + part * third, 16), third)
        arrive(wout_ref.at[rows], 154 + part)
    for copy in sent:
        copy.wait_send()


def reduce_everywhere(rows, gains):
    total_rows, width = rows.shape
    parts = len(AXIS_ORDERS)
    third = total_rows // 2 // parts
    sizes = [third // 4, third // 16, third // 64]
    scratch = [
        pltpu.VMEM((total_rows // 2, width), jnp.bfloat16),
        pltpu.VMEM((total_rows // 2, width), jnp.bfloat16),
        pltpu.VMEM(gains.shape, jnp.bfloat16),
        pltpu.VMEM(gains.shape, jnp.bfloat16),
    ]
    for part in range(parts):
        for size in sizes:
            scratch += [
                pltpu.VMEM((4, size, width), jnp.bfloat16),
                pltpu.VMEM((4, size, width), jnp.bfloat16),
                pltpu.VMEM((size, width), jnp.float32),
            ]
    for part in range(parts):
        for size in reversed(sizes):
            scratch.append(pltpu.VMEM((4, size, width), jnp.bfloat16))
    scratch += [
        pltpu.VMEM((3,) + gains.shape, jnp.bfloat16),
        pltpu.VMEM((3, 4) + gains.shape, jnp.bfloat16),
        pltpu.SemaphoreType.DMA((160,)),
        pltpu.SemaphoreType.DMA((160,)),
    ]
    full, gains = pl.pallas_call(
        reduce_kernel,
        out_shape=(
            jax.ShapeDtypeStruct((total_rows, width), jnp.bfloat16),
            jax.ShapeDtypeStruct(gains.shape, jnp.float32),
        ),
        in_specs=[pl.BlockSpec(memory_space=pltpu.VMEM)] * 2,
        out_specs=(
            pl.BlockSpec(memory_space=pltpu.VMEM),
            pl.BlockSpec(memory_space=pltpu.VMEM),
        ),
        scratch_shapes=scratch,
        compiler_params=pltpu.CompilerParams(
            collective_id=0, has_side_effects=True, vmem_limit_bytes=60 * 1024 * 1024
        ),
    )(rows, gains)
    return full.astype(jnp.float32), gains

def on_device(
    features, curve_pos, pattern, ln1_gain, w_qkv, w_out, ln2_gain, w_up, w_down, out_grad
):
    seq_devices = lax.axis_size("seq")
    seq_index = lax.axis_index("seq")
    dev_rows = features.shape[1]
    capacity = 2 * dev_rows // seq_devices
    blocks_dev = dev_rows // BLK
    position = curve_pos[0]
    send_index, source_for_slot = node_plan(position, seq_index, dev_rows, capacity, seq_devices)
    outgoing = jnp.zeros((seq_devices * capacity, D), jnp.bfloat16).at[send_index].set(features[0])
    arrived = lax.all_to_all(
        outgoing.reshape(seq_devices, capacity, D), "seq", split_axis=0, concat_axis=0, tiled=True
    )
    curve_rows = arrived.reshape(seq_devices * capacity, D)[source_for_slot]
    normed_a, normed1, inverse1 = layer_norm(curve_rows, ln1_gain)
    qkv = jnp.dot(normed_a, w_qkv, preferred_element_type=jnp.float32).astype(jnp.bfloat16)
    queries = qkv[:, :D]
    keyval = qkv[:, D:]
    distances = shift_distances(seq_devices)
    pieces = [keyval]
    for distance in distances:
        pieces.append(from_behind(keyval, "seq", distance))
    keyval_all = jnp.concatenate(pieces, axis=0)
    source_dev = jnp.stack(
        [seq_index] + [(seq_index - distance) % seq_devices for distance in distances]
    )
    key_blocks = (
        source_dev[:, None] * blocks_dev + jnp.arange(blocks_dev, dtype=jnp.int32)[None, :]
    ).reshape(-1)
    own_lists = lax.dynamic_slice_in_dim(pattern[0], seq_index * blocks_dev, blocks_dev, axis=0)
    matches = (own_lists[:, :, None] == key_blocks[None, None, :]).astype(jnp.int32)
    selected = jnp.sum(
        matches * jnp.arange(key_blocks.shape[0], dtype=jnp.int32)[None, None, :], axis=-1
    )
    attn_out, log_totals = attention_forward(queries, keyval_all, selected)
    hidden_res = (
        curve_rows.astype(jnp.float32)
        + jnp.dot(attn_out, w_out, preferred_element_type=jnp.float32)
    ).astype(jnp.bfloat16)
    normed_b, normed2, inverse2 = layer_norm(hidden_res, ln2_gain)
    pre_act = jnp.dot(normed_b, w_up, preferred_element_type=jnp.float32)
    activated = jax.nn.gelu(pre_act, approximate=True).astype(jnp.bfloat16)
    curve_out = (
        hidden_res.astype(jnp.float32)
        + jnp.dot(activated, w_down, preferred_element_type=jnp.float32)
    ).astype(jnp.bfloat16)
    leaving = (
        jnp.zeros((seq_devices * capacity, D), jnp.bfloat16).at[source_for_slot].set(curve_out)
    )
    returned = lax.all_to_all(
        leaving.reshape(seq_devices, capacity, D), "seq", split_axis=0, concat_axis=0, tiled=True
    )
    block_out = returned.reshape(seq_devices * capacity, D)[send_index]
    grad_outgoing = (
        jnp.zeros((seq_devices * capacity, D), jnp.bfloat16).at[send_index].set(out_grad[0])
    )
    grad_arrived = lax.all_to_all(
        grad_outgoing.reshape(seq_devices, capacity, D),
        "seq",
        split_axis=0,
        concat_axis=0,
        tiled=True,
    )
    grad_curve = grad_arrived.reshape(seq_devices * capacity, D)[source_for_slot]
    grad_pre = gelu_back(pre_act, times_transposed(grad_curve, w_down)).astype(jnp.bfloat16)
    grad_down = inner_rows(activated, grad_curve)
    grad_normed_b = times_transposed(grad_pre, w_up)
    grad_up = inner_rows(normed_b, grad_pre)
    grad_gain2 = jnp.sum(grad_normed_b * normed2, axis=0)
    grad_hidden = (
        grad_curve.astype(jnp.float32) + norm_back(grad_normed_b, ln2_gain, normed2, inverse2)
    ).astype(jnp.bfloat16)
    grad_attn = times_transposed(grad_hidden, w_out).astype(jnp.bfloat16)
    grad_out = inner_rows(attn_out, grad_hidden)
    resent = [keyval]
    for distance in distances:
        resent.append(from_behind(keyval, "seq", distance))
    keyval_back = jnp.concatenate(resent, axis=0)
    grad_query, grad_keyval_all = attention_backward(
        queries, keyval_back, selected, attn_out, log_totals, grad_attn
    )
    grad_keyval = grad_keyval_all[:dev_rows]
    for index_pos, distance in enumerate(distances):
        partial_rows = grad_keyval_all[(index_pos + 1) * dev_rows : (index_pos + 2) * dev_rows]
        grad_keyval = grad_keyval + from_behind(
            partial_rows.astype(jnp.bfloat16), "seq", -distance
        ).astype(partial_rows.dtype)
    grad_qkv_rows = jnp.concatenate([grad_query, grad_keyval.astype(jnp.bfloat16)], axis=1)
    grad_normed_a = times_transposed(grad_qkv_rows, w_qkv)
    grad_qkv = inner_rows(normed_a, grad_qkv_rows)
    grad_gain1 = jnp.sum(grad_normed_a * normed1, axis=0)
    grad_curve_in = (
        grad_hidden.astype(jnp.float32) + norm_back(grad_normed_a, ln1_gain, normed1, inverse1)
    ).astype(jnp.bfloat16)
    grad_leaving = (
        jnp.zeros((seq_devices * capacity, D), jnp.bfloat16).at[source_for_slot].set(grad_curve_in)
    )
    grad_returned = lax.all_to_all(
        grad_leaving.reshape(seq_devices, capacity, D),
        "seq",
        split_axis=0,
        concat_axis=0,
        tiled=True,
    )
    input_grad = grad_returned.reshape(seq_devices * capacity, D)[send_index]
    weight_rows = jnp.concatenate(
        [grad_qkv[:, index * D : (index + 1) * D] for index in range(3)]
        + [grad_out]
        + [grad_up[:, index * D : (index + 1) * D] for index in range(4)]
        + [grad_down],
        axis=0,
    )
    gain_rows = jnp.zeros((8, D), jnp.float32).at[0].set(grad_gain1).at[1].set(grad_gain2)
    weight_rows, gain_rows = reduce_everywhere(weight_rows, gain_rows)
    grad_qkv = jnp.concatenate([weight_rows[index * D : (index + 1) * D] for index in range(3)], axis=1)
    grad_out = weight_rows[3 * D : 4 * D]
    grad_up = jnp.concatenate(
        [weight_rows[(4 + index) * D : (5 + index) * D] for index in range(4)], axis=1
    )
    grad_down = weight_rows[8 * D :]
    grad_gain1 = gain_rows[0]
    grad_gain2 = gain_rows[1]
    return (
        block_out[None],
        input_grad[None],
        grad_qkv,
        grad_out,
        grad_up,
        grad_down,
        grad_gain1,
        grad_gain2,
    )


def solution(mesh):
    return jax.shard_map(
        on_device,
        mesh=mesh,
        in_specs=(
            P("dp", "seq", None),
            P("dp", None),
            P("dp", None, None),
            P(),
            P(),
            P(),
            P(),
            P(),
            P(),
            P("dp", "seq", None),
        ),
        out_specs=(P("dp", "seq", None), P("dp", "seq", None), P(), P(), P(), P(), P(), P()),
        check_vma=False,
    )
```

```python
from functools import partial

import jax
import jax.numpy as jnp
from jax import lax
from jax.experimental import pallas as pl
from jax.experimental.pallas import tpu as pltpu
from jax.sharding import PartitionSpec as P

D = 512
HEADS = 8
BLK = 128


EPSILON = 1e-05


def from_behind(x, axis, by):
    length = lax.axis_size(axis)
    return lax.ppermute(x, axis, [(i, (i + by) % length) for i in range(length)])


def layer_norm(rows_in, gain_vec):
    values = rows_in.astype(jnp.float32)
    centered = values - jnp.mean(values, axis=-1, keepdims=True)
    inverse = lax.rsqrt(jnp.mean(centered * centered, axis=-1, keepdims=True) + EPSILON)
    normed = centered * inverse
    return ((normed * gain_vec).astype(jnp.bfloat16), normed, inverse)


def norm_back(incoming, gain_vec, normed, inverse):
    scaled = incoming * gain_vec
    return inverse * (
        scaled
        - jnp.mean(scaled, axis=-1, keepdims=True)
        - normed * jnp.mean(scaled * normed, axis=-1, keepdims=True)
    )


def gelu_back(pre_act, incoming):
    return jax.vjp(partial(jax.nn.gelu, approximate=True), pre_act)[1](incoming)[0]


def inner_rows(left_mat, right_mat):
    return lax.dot_general(
        left_mat, right_mat, (((0,), (0,)), ((), ())), preferred_element_type=jnp.float32
    )


def times_transposed(left_mat, right_mat):
    return lax.dot_general(
        left_mat, right_mat, (((1,), (1,)), ((), ())), preferred_element_type=jnp.float32
    )


def split_heads(rows_in):
    return rows_in.reshape(rows_in.shape[0] // BLK, BLK, HEADS, D // HEADS)


def listed_heads(keyval_all, selected):
    blocks = keyval_all.reshape(keyval_all.shape[0] // BLK, BLK, 2 * D)
    picked = blocks[selected]
    shape_out = picked.shape[:3] + (HEADS, D // HEADS)
    return (picked[..., :D].reshape(shape_out), picked[..., D:].reshape(shape_out))


def shift_distances(seq_devices):
    levels = seq_devices.bit_length() - 1
    distances = []
    for level_idx in range(levels):
        stride = 2**level_idx
        if 2 * stride == seq_devices:
            distances.append(stride)
        else:
            distances.extend([stride, -stride])
    return distances


def node_plan(position, seq_index, dev_rows, capacity, seq_devices):
    own_position = lax.dynamic_slice_in_dim(position, seq_index * dev_rows, dev_rows)
    target_dev = own_position // dev_rows
    dest_hits = (target_dev[:, None] == jnp.arange(seq_devices, dtype=jnp.int32)[None, :]).astype(
        jnp.int32
    )
    send_rank = jnp.sum((jnp.cumsum(dest_hits, axis=0) - dest_hits) * dest_hits, axis=1)
    send_index = target_dev * capacity + send_rank
    layout = position.reshape(seq_devices, dev_rows)
    arriving = (layout // dev_rows == seq_index).astype(jnp.int32)
    arrive_rank = jnp.cumsum(arriving, axis=1) - arriving
    source_index = jnp.arange(seq_devices, dtype=jnp.int32)[:, None] * capacity + arrive_rank
    del source_index
    total = position.shape[0]
    wanted = seq_index * dev_rows + jnp.arange(dev_rows, dtype=jnp.int32)
    slot_node = jnp.sum(
        jnp.where(
            position[None, :] == wanted[:, None], jnp.arange(total, dtype=jnp.int32)[None, :], 0
        ),
        axis=1,
    )
    source_for_slot = (slot_node // dev_rows) * capacity + arrive_rank.reshape(-1)[slot_node]
    return (send_index, source_for_slot)


def attention_forward(queries, keyval_all, selected):
    query_heads = split_heads(queries)
    key_heads, value_heads = listed_heads(keyval_all, selected)
    scores = (
        jnp.einsum("aihd,akjhd->haikj", query_heads, key_heads, preferred_element_type=jnp.float32)
        * 0.125
    )
    largest = jnp.max(scores, axis=(3, 4), keepdims=True)
    totals = jnp.sum(jnp.exp(scores - largest), axis=(3, 4), keepdims=True)
    log_totals = largest + jnp.log(totals)
    attn_probs = jnp.exp(scores - log_totals).astype(jnp.bfloat16)
    result = jnp.einsum(
        "haikj,akjhd->aihd", attn_probs, value_heads, preferred_element_type=jnp.float32
    )
    return (result.astype(jnp.bfloat16).reshape(queries.shape[0], D), log_totals)


def attention_backward(queries, keyval_all, selected, attn_out, log_totals, grad_attn):
    query_heads = split_heads(queries)
    key_heads, value_heads = listed_heads(keyval_all, selected)
    out_heads = split_heads(attn_out)
    grad_heads = split_heads(grad_attn)
    scores = (
        jnp.einsum("aihd,akjhd->haikj", query_heads, key_heads, preferred_element_type=jnp.float32)
        * 0.125
    )
    attn_exact = jnp.exp(scores - log_totals)
    attn_probs = attn_exact.astype(jnp.bfloat16)
    grad_probs = jnp.einsum(
        "aihd,akjhd->haikj", grad_heads, value_heads, preferred_element_type=jnp.float32
    )
    row_dots = jnp.einsum(
        "aihd,aihd->hai", grad_heads, out_heads, preferred_element_type=jnp.float32
    )[..., None, None]
    grad_scores = (attn_exact * (grad_probs - row_dots) * 0.125).astype(jnp.bfloat16)
    grad_query = jnp.einsum(
        "haikj,akjhd->aihd", grad_scores, key_heads, preferred_element_type=jnp.float32
    )
    total_rows = keyval_all.shape[0]
    one_hot = (
        selected[:, :, None] == jnp.arange(total_rows // BLK, dtype=jnp.int32)[None, None, :]
    ).astype(jnp.bfloat16)
    scores_by_block = jnp.einsum(
        "haikj,akb->haibj", grad_scores, one_hot, preferred_element_type=jnp.float32
    ).astype(jnp.bfloat16)
    probs_by_block = jnp.einsum(
        "haikj,akb->haibj", attn_probs, one_hot, preferred_element_type=jnp.float32
    ).astype(jnp.bfloat16)
    grad_keys = jnp.einsum(
        "haibj,aihd->bjhd", scores_by_block, query_heads, preferred_element_type=jnp.float32
    )
    grad_values = jnp.einsum(
        "haibj,aihd->bjhd", probs_by_block, grad_heads, preferred_element_type=jnp.float32
    )
    grad_keyval = jnp.concatenate(
        [grad_keys.reshape(total_rows, D), grad_values.reshape(total_rows, D)], axis=-1
    )
    return (
        grad_query.astype(jnp.bfloat16).reshape(queries.shape[0], D),
        grad_keyval.reshape(total_rows, 2 * D),
    )


MESH_IDS = pl.DeviceIdType.MESH
RING_KINDS = ("x", "y", "z")
AXIS_ORDERS = (("x", "y", "z"), ("y", "z", "x"), ("z", "x", "y"))


def reduce_kernel(w_ref, g_ref, wout_ref, gout_ref, send0, recv0, gsend0, grecv0, *rest):
    parts = len(AXIS_ORDERS)
    ring_bufs = [[rest[9 * p + 3 * s : 9 * p + 3 * s + 3] for s in range(3)] for p in range(parts)]
    gather_bufs = [rest[9 * parts + 3 * p : 9 * parts + 3 * p + 3] for p in range(parts)]
    gsend, grecv, send_sem, recv_sem = rest[12 * parts :]
    seq = lax.axis_index("seq")
    dp = lax.axis_index("dp")
    core = seq % 2
    place = {"x": (seq // 2) % 4, "y": seq // 8, "z": dp}

    def peer(kind, member):
        if kind == "core":
            return (seq + 1 - 2 * core, dp)
        if kind == "x":
            return (seq + (member - place["x"]) * 2, dp)
        if kind == "y":
            return (seq + (member - place["y"]) * 8, dp)
        return (seq, member)

    barrier = pltpu.get_barrier_semaphore()
    peers = [peer("core", 0)]
    for kind in RING_KINDS:
        for shift in (1, 2, 3):
            peers.append(peer(kind, (place[kind] + shift) % 4))
    for target in peers:
        pl.semaphore_signal(barrier, inc=1, device_id=target, device_id_type=MESH_IDS)
    pl.semaphore_wait(barrier, len(peers))

    counter = [0]
    sent = []

    def send(src, dst, recv_index, target):
        copy = pltpu.make_async_remote_copy(
            src_ref=src,
            dst_ref=dst,
            send_sem=send_sem.at[counter[0]],
            recv_sem=recv_sem.at[recv_index],
            device_id=target,
            device_id_type=MESH_IDS,
        )
        counter[0] += 1
        copy.start()
        sent.append(copy)

    def arrive(dst, recv_index):
        pltpu.make_async_remote_copy(
            src_ref=dst,
            dst_ref=dst,
            send_sem=send_sem.at[0],
            recv_sem=recv_sem.at[recv_index],
            device_id=peers[0],
            device_id_type=MESH_IDS,
        ).wait_recv()

    half = send0.shape[0]
    third = half // parts
    gsend0[...] = g_ref[...].astype(jnp.bfloat16)
    send(gsend0, grecv0, 1, peers[0])
    for part in range(parts):
        rows = pl.ds(pl.multiple_of(part * third, 16), third)
        source_rows = pl.ds(pl.multiple_of((1 - core) * half + part * third, 16), third)
        send0[rows, :] = w_ref[source_rows, :].astype(jnp.bfloat16)
        send(send0.at[rows], recv0.at[rows], 150 + part, peers[0])
    arrive(grecv0, 1)
    gains = gsend0[...].astype(jnp.float32) + grecv0[...].astype(jnp.float32)

    def first_chunk(part, member, size):
        offset = part * third + member * size
        mine = w_ref[pl.ds(pl.multiple_of(core * half + offset, 16), size), :]
        return mine + recv0[pl.ds(pl.multiple_of(offset, 16), size), :].astype(jnp.float32)

    sources = [None] * parts
    for stage in range(3):
        for part in range(parts):
            kind = AXIS_ORDERS[part][stage]
            sbuf, rbuf, total = ring_bufs[part][stage]
            size = sbuf.shape[1]
            pos = place[kind]
            base = 2 + 12 * (3 * part + stage)
            source = sources[part]

            def chunk(member, source=source, size=size, part=part):
                if source is None:
                    return first_chunk(part, member, size)
                return source[pl.ds(pl.multiple_of(member * size, 16), size), :]

            if stage == 0:
                arrive(recv0.at[pl.ds(pl.multiple_of(part * third, 16), third)], 150 + part)
            if part == 0:
                gsend[stage] = gains.astype(jnp.bfloat16)
                grecv[stage, pos] = gsend[stage]
            for shift in (1, 2, 3):
                member = (pos + shift) % 4
                sbuf[member] = chunk(member).astype(jnp.bfloat16)
                send(sbuf.at[member], rbuf.at[pos], base + pos, peer(kind, member))
                if part == 0:
                    send(gsend.at[stage], grecv.at[stage, pos], base + 4 + pos, peer(kind, member))
            total[...] = chunk(pos)
        for part in range(parts):
            kind = AXIS_ORDERS[part][stage]
            sbuf, rbuf, total = ring_bufs[part][stage]
            pos = place[kind]
            base = 2 + 12 * (3 * part + stage)
            for shift in (1, 2, 3):
                slot = (pos - shift) % 4
                arrive(rbuf.at[slot], base + slot)
                total[...] += rbuf[slot].astype(jnp.float32)
                if part == 0:
                    arrive(grecv.at[stage, slot], base + 4 + slot)
            if part == 0:
                got = grecv[stage].astype(jnp.float32)
                gains = (got[0] + got[1]) + (got[2] + got[3])
            sources[part] = total
    gout_ref[...] = gains

    owns = [sources[part][...].astype(jnp.bfloat16) for part in range(parts)]
    for stage in range(3):
        for part in range(parts):
            kind = AXIS_ORDERS[part][2 - stage]
            gathered = gather_bufs[part][stage]
            pos = place[kind]
            base = 2 + 12 * 9 + 4 * (3 * part + stage)
            gathered[pos] = owns[part]
            for shift in (1, 2, 3):
                member = (pos + shift) % 4
                send(gathered.at[pos], gathered.at[pos], base + pos, peer(kind, member))
        for part in range(parts):
            kind = AXIS_ORDERS[part][2 - stage]
            gathered = gather_bufs[part][stage]
            pos = place[kind]
            base = 2 + 12 * 9 + 4 * (3 * part + stage)
            for shift in (1, 2, 3):
                arrive(gathered.at[(pos - shift) % 4], base + (pos - shift) % 4)
            owns[part] = gathered[...].reshape(4 * gathered.shape[1], gathered.shape[2])
            if stage == 2:
                rows = pl.ds(pl.multiple_of(core * half + part * third, 16), third)
                wout_ref[rows, :] = owns[part]
                send(wout_ref.at[rows], wout_ref.at[rows], 154 + part, peers[0])
    for part in range(parts):
        rows = pl.ds(pl.multiple_of((1 - core) * half + part * third, 16), third)
        arrive(wout_ref.at[rows], 154 + part)
    for copy in sent:
        copy.wait_send()


def reduce_everywhere(rows, gains):
    total_rows, width = rows.shape
    parts = len(AXIS_ORDERS)
    third = total_rows // 2 // parts
    sizes = [third // 4, third // 16, third // 64]
    scratch = [
        pltpu.VMEM((total_rows // 2, width), jnp.bfloat16),
        pltpu.VMEM((total_rows // 2, width), jnp.bfloat16),
        pltpu.VMEM(gains.shape, jnp.bfloat16),
        pltpu.VMEM(gains.shape, jnp.bfloat16),
    ]
    for part in range(parts):
        for size in sizes:
            scratch += [
                pltpu.VMEM((4, size, width), jnp.bfloat16),
                pltpu.VMEM((4, size, width), jnp.bfloat16),
                pltpu.VMEM((size, width), jnp.float32),
            ]
    for part in range(parts):
        for size in reversed(sizes):
            scratch.append(pltpu.VMEM((4, size, width), jnp.bfloat16))
    scratch += [
        pltpu.VMEM((3,) + gains.shape, jnp.bfloat16),
        pltpu.VMEM((3, 4) + gains.shape, jnp.bfloat16),
        pltpu.SemaphoreType.DMA((160,)),
        pltpu.SemaphoreType.DMA((160,)),
    ]
    full, gains = pl.pallas_call(
        reduce_kernel,
        out_shape=(
            jax.ShapeDtypeStruct((total_rows, width), jnp.bfloat16),
            jax.ShapeDtypeStruct(gains.shape, jnp.float32),
        ),
        in_specs=[pl.BlockSpec(memory_space=pltpu.VMEM)] * 2,
        out_specs=(
            pl.BlockSpec(memory_space=pltpu.VMEM),
            pl.BlockSpec(memory_space=pltpu.VMEM),
        ),
        scratch_shapes=scratch,
        compiler_params=pltpu.CompilerParams(
            collective_id=0, has_side_effects=True, vmem_limit_bytes=60 * 1024 * 1024
        ),
    )(rows, gains)
    return full.astype(jnp.float32), gains

def on_device(
    features, curve_pos, pattern, ln1_gain, w_qkv, w_out, ln2_gain, w_up, w_down, out_grad
):
    seq_devices = lax.axis_size("seq")
    seq_index = lax.axis_index("seq")
    dev_rows = features.shape[1]
    capacity = 2 * dev_rows // seq_devices
    blocks_dev = dev_rows // BLK
    position = curve_pos[0]
    send_index, source_for_slot = node_plan(position, seq_index, dev_rows, capacity, seq_devices)
    outgoing = jnp.zeros((seq_devices * capacity, D), jnp.bfloat16).at[send_index].set(features[0])
    arrived = lax.all_to_all(
        outgoing.reshape(seq_devices, capacity, D), "seq", split_axis=0, concat_axis=0, tiled=True
    )
    curve_rows = arrived.reshape(seq_devices * capacity, D)[source_for_slot]
    normed_a, normed1, inverse1 = layer_norm(curve_rows, ln1_gain)
    qkv = jnp.dot(normed_a, w_qkv, preferred_element_type=jnp.float32).astype(jnp.bfloat16)
    queries = qkv[:, :D]
    keyval = qkv[:, D:]
    distances = shift_distances(seq_devices)
    pieces = [keyval]
    for distance in distances:
        pieces.append(from_behind(keyval, "seq", distance))
    keyval_all = jnp.concatenate(pieces, axis=0)
    source_dev = jnp.stack(
        [seq_index] + [(seq_index - distance) % seq_devices for distance in distances]
    )
    key_blocks = (
        source_dev[:, None] * blocks_dev + jnp.arange(blocks_dev, dtype=jnp.int32)[None, :]
    ).reshape(-1)
    own_lists = lax.dynamic_slice_in_dim(pattern[0], seq_index * blocks_dev, blocks_dev, axis=0)
    matches = (own_lists[:, :, None] == key_blocks[None, None, :]).astype(jnp.int32)
    selected = jnp.sum(
        matches * jnp.arange(key_blocks.shape[0], dtype=jnp.int32)[None, None, :], axis=-1
    )
    attn_out, log_totals = attention_forward(queries, keyval_all, selected)
    hidden_res = (
        curve_rows.astype(jnp.float32)
        + jnp.dot(attn_out, w_out, preferred_element_type=jnp.float32)
    ).astype(jnp.bfloat16)
    normed_b, normed2, inverse2 = layer_norm(hidden_res, ln2_gain)
    pre_act = jnp.dot(normed_b, w_up, preferred_element_type=jnp.float32)
    activated = jax.nn.gelu(pre_act, approximate=True).astype(jnp.bfloat16)
    curve_out = (
        hidden_res.astype(jnp.float32)
        + jnp.dot(activated, w_down, preferred_element_type=jnp.float32)
    ).astype(jnp.bfloat16)
    leaving = (
        jnp.zeros((seq_devices * capacity, D), jnp.bfloat16).at[source_for_slot].set(curve_out)
    )
    returned = lax.all_to_all(
        leaving.reshape(seq_devices, capacity, D), "seq", split_axis=0, concat_axis=0, tiled=True
    )
    block_out = returned.reshape(seq_devices * capacity, D)[send_index]
    grad_outgoing = (
        jnp.zeros((seq_devices * capacity, D), jnp.bfloat16).at[send_index].set(out_grad[0])
    )
    grad_arrived = lax.all_to_all(
        grad_outgoing.reshape(seq_devices, capacity, D),
        "seq",
        split_axis=0,
        concat_axis=0,
        tiled=True,
    )
    grad_curve = grad_arrived.reshape(seq_devices * capacity, D)[source_for_slot]
    grad_pre = gelu_back(pre_act, times_transposed(grad_curve, w_down)).astype(jnp.bfloat16)
    grad_down = inner_rows(activated, grad_curve)
    grad_normed_b = times_transposed(grad_pre, w_up)
    grad_up = inner_rows(normed_b, grad_pre)
    grad_gain2 = jnp.sum(grad_normed_b * normed2, axis=0)
    grad_hidden = (
        grad_curve.astype(jnp.float32) + norm_back(grad_normed_b, ln2_gain, normed2, inverse2)
    ).astype(jnp.bfloat16)
    grad_attn = times_transposed(grad_hidden, w_out).astype(jnp.bfloat16)
    grad_out = inner_rows(attn_out, grad_hidden)
    resent = [keyval]
    for distance in distances:
        resent.append(from_behind(keyval, "seq", distance))
    keyval_back = jnp.concatenate(resent, axis=0)
    grad_query, grad_keyval_all = attention_backward(
        queries, keyval_back, selected, attn_out, log_totals, grad_attn
    )
    grad_keyval = grad_keyval_all[:dev_rows]
    for index_pos, distance in enumerate(distances):
        partial_rows = grad_keyval_all[(index_pos + 1) * dev_rows : (index_pos + 2) * dev_rows]
        grad_keyval = grad_keyval + from_behind(
            partial_rows.astype(jnp.bfloat16), "seq", -distance
        ).astype(partial_rows.dtype)
    grad_qkv_rows = jnp.concatenate([grad_query, grad_keyval.astype(jnp.bfloat16)], axis=1)
    grad_normed_a = times_transposed(grad_qkv_rows, w_qkv)
    grad_qkv = inner_rows(normed_a, grad_qkv_rows)
    grad_gain1 = jnp.sum(grad_normed_a * normed1, axis=0)
    grad_curve_in = (
        grad_hidden.astype(jnp.float32) + norm_back(grad_normed_a, ln1_gain, normed1, inverse1)
    ).astype(jnp.bfloat16)
    grad_leaving = (
        jnp.zeros((seq_devices * capacity, D), jnp.bfloat16).at[source_for_slot].set(grad_curve_in)
    )
    grad_returned = lax.all_to_all(
        grad_leaving.reshape(seq_devices, capacity, D),
        "seq",
        split_axis=0,
        concat_axis=0,
        tiled=True,
    )
    input_grad = grad_returned.reshape(seq_devices * capacity, D)[send_index]
    weight_rows = jnp.concatenate(
        [grad_qkv[:, index * D : (index + 1) * D] for index in range(3)]
        + [grad_out]
        + [grad_up[:, index * D : (index + 1) * D] for index in range(4)]
        + [grad_down],
        axis=0,
    )
    gain_rows = jnp.zeros((8, D), jnp.float32).at[0].set(grad_gain1).at[1].set(grad_gain2)
    weight_rows, gain_rows = reduce_everywhere(weight_rows, gain_rows)
    grad_qkv = jnp.concatenate([weight_rows[index * D : (index + 1) * D] for index in range(3)], axis=1)
    grad_out = weight_rows[3 * D : 4 * D]
    grad_up = jnp.concatenate(
        [weight_rows[(4 + index) * D : (5 + index) * D] for index in range(4)], axis=1
    )
    grad_down = weight_rows[8 * D :]
    grad_gain1 = gain_rows[0]
    grad_gain2 = gain_rows[1]
    return (
        block_out[None],
        input_grad[None],
        grad_qkv,
        grad_out,
        grad_up,
        grad_down,
        grad_gain1,
        grad_gain2,
    )


def solution(mesh):
    return jax.shard_map(
        on_device,
        mesh=mesh,
        in_specs=(
            P("dp", "seq", None),
            P("dp", None),
            P("dp", None, None),
            P(),
            P(),
            P(),
            P(),
            P(),
            P(),
            P("dp", "seq", None),
        ),
        out_specs=(P("dp", "seq", None), P("dp", "seq", None), P(), P(), P(), P(), P(), P()),
        check_vma=False,
    )
```

```python
from functools import partial

import jax
import jax.numpy as jnp
from jax import lax
from jax.experimental import pallas as pl
from jax.experimental.pallas import tpu as pltpu
from jax.sharding import PartitionSpec as P

D = 512
HEADS = 8
BLK = 128


EPSILON = 1e-05


def from_behind(x, axis, by):
    length = lax.axis_size(axis)
    return lax.ppermute(x, axis, [(i, (i + by) % length) for i in range(length)])


def layer_norm(rows_in, gain_vec):
    values = rows_in.astype(jnp.float32)
    centered = values - jnp.mean(values, axis=-1, keepdims=True)
    inverse = lax.rsqrt(jnp.mean(centered * centered, axis=-1, keepdims=True) + EPSILON)
    normed = centered * inverse
    return ((normed * gain_vec).astype(jnp.bfloat16), normed, inverse)


def norm_back(incoming, gain_vec, normed, inverse):
    scaled = incoming * gain_vec
    return inverse * (
        scaled
        - jnp.mean(scaled, axis=-1, keepdims=True)
        - normed * jnp.mean(scaled * normed, axis=-1, keepdims=True)
    )


def gelu_back(pre_act, incoming):
    return jax.vjp(partial(jax.nn.gelu, approximate=True), pre_act)[1](incoming)[0]


def inner_rows(left_mat, right_mat):
    return lax.dot_general(
        left_mat, right_mat, (((0,), (0,)), ((), ())), preferred_element_type=jnp.float32
    )


def times_transposed(left_mat, right_mat):
    return lax.dot_general(
        left_mat, right_mat, (((1,), (1,)), ((), ())), preferred_element_type=jnp.float32
    )


def split_heads(rows_in):
    return rows_in.reshape(rows_in.shape[0] // BLK, BLK, HEADS, D // HEADS)


def listed_heads(keyval_all, selected):
    blocks = keyval_all.reshape(keyval_all.shape[0] // BLK, BLK, 2 * D)
    picked = blocks[selected]
    shape_out = picked.shape[:3] + (HEADS, D // HEADS)
    return (picked[..., :D].reshape(shape_out), picked[..., D:].reshape(shape_out))


def shift_distances(seq_devices):
    levels = seq_devices.bit_length() - 1
    distances = []
    for level_idx in range(levels):
        stride = 2**level_idx
        if 2 * stride == seq_devices:
            distances.append(stride)
        else:
            distances.extend([stride, -stride])
    return distances


def node_plan(position, seq_index, dev_rows, capacity, seq_devices):
    own_position = lax.dynamic_slice_in_dim(position, seq_index * dev_rows, dev_rows)
    target_dev = own_position // dev_rows
    dest_hits = (target_dev[:, None] == jnp.arange(seq_devices, dtype=jnp.int32)[None, :]).astype(
        jnp.int32
    )
    send_rank = jnp.sum((jnp.cumsum(dest_hits, axis=0) - dest_hits) * dest_hits, axis=1)
    send_index = target_dev * capacity + send_rank
    layout = position.reshape(seq_devices, dev_rows)
    arriving = (layout // dev_rows == seq_index).astype(jnp.int32)
    arrive_rank = jnp.cumsum(arriving, axis=1) - arriving
    source_index = jnp.arange(seq_devices, dtype=jnp.int32)[:, None] * capacity + arrive_rank
    del source_index
    total = position.shape[0]
    wanted = seq_index * dev_rows + jnp.arange(dev_rows, dtype=jnp.int32)
    slot_node = jnp.sum(
        jnp.where(
            position[None, :] == wanted[:, None], jnp.arange(total, dtype=jnp.int32)[None, :], 0
        ),
        axis=1,
    )
    source_for_slot = (slot_node // dev_rows) * capacity + arrive_rank.reshape(-1)[slot_node]
    return (send_index, source_for_slot)


def attention_forward(queries, keyval_all, selected):
    query_heads = split_heads(queries)
    key_heads, value_heads = listed_heads(keyval_all, selected)
    scores = (
        jnp.einsum("aihd,akjhd->haikj", query_heads, key_heads, preferred_element_type=jnp.float32)
        * 0.125
    )
    largest = jnp.max(scores, axis=(3, 4), keepdims=True)
    totals = jnp.sum(jnp.exp(scores - largest), axis=(3, 4), keepdims=True)
    log_totals = largest + jnp.log(totals)
    attn_probs = jnp.exp(scores - log_totals).astype(jnp.bfloat16)
    result = jnp.einsum(
        "haikj,akjhd->aihd", attn_probs, value_heads, preferred_element_type=jnp.float32
    )
    return (result.astype(jnp.bfloat16).reshape(queries.shape[0], D), log_totals)


def attention_backward(queries, keyval_all, selected, attn_out, log_totals, grad_attn):
    query_heads = split_heads(queries)
    key_heads, value_heads = listed_heads(keyval_all, selected)
    out_heads = split_heads(attn_out)
    grad_heads = split_heads(grad_attn)
    scores = (
        jnp.einsum("aihd,akjhd->haikj", query_heads, key_heads, preferred_element_type=jnp.float32)
        * 0.125
    )
    attn_exact = jnp.exp(scores - log_totals)
    attn_probs = attn_exact.astype(jnp.bfloat16)
    grad_probs = jnp.einsum(
        "aihd,akjhd->haikj", grad_heads, value_heads, preferred_element_type=jnp.float32
    )
    row_dots = jnp.einsum(
        "aihd,aihd->hai", grad_heads, out_heads, preferred_element_type=jnp.float32
    )[..., None, None]
    grad_scores = (attn_exact * (grad_probs - row_dots) * 0.125).astype(jnp.bfloat16)
    grad_query = jnp.einsum(
        "haikj,akjhd->aihd", grad_scores, key_heads, preferred_element_type=jnp.float32
    )
    grad_keys = jnp.einsum(
        "haikj,aihd->akjhd", grad_scores, query_heads, preferred_element_type=jnp.float32
    )
    grad_values = jnp.einsum(
        "haikj,aihd->akjhd", attn_probs, grad_heads, preferred_element_type=jnp.float32
    )
    block_shape = grad_keys.shape[:3] + (D,)
    grad_picked = jnp.concatenate(
        [grad_keys.reshape(block_shape), grad_values.reshape(block_shape)], axis=-1
    )
    total_rows = keyval_all.shape[0]
    one_hot = (
        selected[:, :, None] == jnp.arange(total_rows // BLK, dtype=jnp.int32)[None, None, :]
    ).astype(jnp.float32)
    grad_keyval = jnp.einsum(
        "akb,akjc->bjc",
        one_hot,
        grad_picked,
        precision=lax.Precision.HIGHEST,
        preferred_element_type=jnp.float32,
    )
    return (
        grad_query.astype(jnp.bfloat16).reshape(queries.shape[0], D),
        grad_keyval.reshape(total_rows, 2 * D),
    )


MESH_IDS = pl.DeviceIdType.MESH
RING_KINDS = ("x", "y", "z")
AXIS_ORDERS = (("x", "y", "z"), ("y", "z", "x"), ("z", "x", "y"))


def reduce_kernel(w_ref, g_ref, wout_ref, gout_ref, send0, recv0, gsend0, grecv0, *rest):
    parts = len(AXIS_ORDERS)
    ring_bufs = [[rest[9 * p + 3 * s : 9 * p + 3 * s + 3] for s in range(3)] for p in range(parts)]
    gather_bufs = [rest[9 * parts + 3 * p : 9 * parts + 3 * p + 3] for p in range(parts)]
    gsend, grecv, send_sem, recv_sem = rest[12 * parts :]
    seq = lax.axis_index("seq")
    dp = lax.axis_index("dp")
    core = seq % 2
    place = {"x": (seq // 2) % 4, "y": seq // 8, "z": dp}

    def peer(kind, member):
        if kind == "core":
            return (seq + 1 - 2 * core, dp)
        if kind == "x":
            return (seq + (member - place["x"]) * 2, dp)
        if kind == "y":
            return (seq + (member - place["y"]) * 8, dp)
        return (seq, member)

    barrier = pltpu.get_barrier_semaphore()
    peers = [peer("core", 0)]
    for kind in RING_KINDS:
        for shift in (1, 2, 3):
            peers.append(peer(kind, (place[kind] + shift) % 4))
    for target in peers:
        pl.semaphore_signal(barrier, inc=1, device_id=target, device_id_type=MESH_IDS)
    pl.semaphore_wait(barrier, len(peers))

    counter = [0]
    sent = []

    def send(src, dst, recv_index, target):
        copy = pltpu.make_async_remote_copy(
            src_ref=src,
            dst_ref=dst,
            send_sem=send_sem.at[counter[0]],
            recv_sem=recv_sem.at[recv_index],
            device_id=target,
            device_id_type=MESH_IDS,
        )
        counter[0] += 1
        copy.start()
        sent.append(copy)

    def arrive(dst, recv_index):
        pltpu.make_async_remote_copy(
            src_ref=dst,
            dst_ref=dst,
            send_sem=send_sem.at[0],
            recv_sem=recv_sem.at[recv_index],
            device_id=peers[0],
            device_id_type=MESH_IDS,
        ).wait_recv()

    half = send0.shape[0]
    third = half // parts
    gsend0[...] = g_ref[...].astype(jnp.bfloat16)
    send(gsend0, grecv0, 1, peers[0])
    for part in range(parts):
        rows = pl.ds(pl.multiple_of(part * third, 16), third)
        source_rows = pl.ds(pl.multiple_of((1 - core) * half + part * third, 16), third)
        send0[rows, :] = w_ref[source_rows, :].astype(jnp.bfloat16)
        send(send0.at[rows], recv0.at[rows], 150 + part, peers[0])
    arrive(grecv0, 1)
    gains = gsend0[...].astype(jnp.float32) + grecv0[...].astype(jnp.float32)

    def first_chunk(part, member, size):
        offset = part * third + member * size
        mine = w_ref[pl.ds(pl.multiple_of(core * half + offset, 16), size), :]
        return mine + recv0[pl.ds(pl.multiple_of(offset, 16), size), :].astype(jnp.float32)

    sources = [None] * parts
    def ring_send_step(stage, part, gains):
            kind = AXIS_ORDERS[part][stage]
            sbuf, rbuf, total = ring_bufs[part][stage]
            size = sbuf.shape[1]
            pos = place[kind]
            base = 2 + 12 * (3 * part + stage)
            source = sources[part]

            def chunk(member, source=source, size=size, part=part):
                if source is None:
                    return first_chunk(part, member, size)
                return source[pl.ds(pl.multiple_of(member * size, 16), size), :]

            if stage == 0:
                arrive(recv0.at[pl.ds(pl.multiple_of(part * third, 16), third)], 150 + part)
            if part == 0:
                gsend[stage] = gains.astype(jnp.bfloat16)
                grecv[stage, pos] = gsend[stage]
            for shift in (1, 2, 3):
                member = (pos + shift) % 4
                sbuf[member] = chunk(member).astype(jnp.bfloat16)
                send(sbuf.at[member], rbuf.at[pos], base + pos, peer(kind, member))
                if part == 0:
                    send(gsend.at[stage], grecv.at[stage, pos], base + 4 + pos, peer(kind, member))
            total[...] = chunk(pos)
            return gains

    def ring_wait_step(stage, part, gains):
            kind = AXIS_ORDERS[part][stage]
            sbuf, rbuf, total = ring_bufs[part][stage]
            pos = place[kind]
            base = 2 + 12 * (3 * part + stage)
            for shift in (1, 2, 3):
                slot = (pos - shift) % 4
                arrive(rbuf.at[slot], base + slot)
                total[...] += rbuf[slot].astype(jnp.float32)
                if part == 0:
                    arrive(grecv.at[stage, slot], base + 4 + slot)
            if part == 0:
                got = grecv[stage].astype(jnp.float32)
                gains = (got[0] + got[1]) + (got[2] + got[3])
            sources[part] = total
            return gains

    for part in range(parts):
        gains = ring_send_step(0, part, gains)
    for stage in range(3):
        for part in range(parts):
            gains = ring_wait_step(stage, part, gains)
            if stage < 2:
                gains = ring_send_step(stage + 1, part, gains)
    gout_ref[...] = gains

    owns = [sources[part][...].astype(jnp.bfloat16) for part in range(parts)]

    def gather_send_step(stage, part):
        kind = AXIS_ORDERS[part][2 - stage]
        gathered = gather_bufs[part][stage]
        pos = place[kind]
        base = 2 + 12 * 9 + 4 * (3 * part + stage)
        gathered[pos] = owns[part]
        for shift in (1, 2, 3):
            member = (pos + shift) % 4
            send(gathered.at[pos], gathered.at[pos], base + pos, peer(kind, member))

    def gather_wait_step(stage, part):
        kind = AXIS_ORDERS[part][2 - stage]
        gathered = gather_bufs[part][stage]
        pos = place[kind]
        base = 2 + 12 * 9 + 4 * (3 * part + stage)
        for shift in (1, 2, 3):
            arrive(gathered.at[(pos - shift) % 4], base + (pos - shift) % 4)
        owns[part] = gathered[...].reshape(4 * gathered.shape[1], gathered.shape[2])

    for part in range(parts):
        gather_send_step(0, part)
    for stage in range(3):
        for part in range(parts):
            gather_wait_step(stage, part)
            if stage < 2:
                gather_send_step(stage + 1, part)
            else:
                rows = pl.ds(pl.multiple_of(core * half + part * third, 16), third)
                wout_ref[rows, :] = owns[part]
                send(wout_ref.at[rows], wout_ref.at[rows], 154 + part, peers[0])
    for part in range(parts):
        rows = pl.ds(pl.multiple_of((1 - core) * half + part * third, 16), third)
        arrive(wout_ref.at[rows], 154 + part)
    for copy in sent:
        copy.wait_send()


def reduce_everywhere(rows, gains):
    total_rows, width = rows.shape
    parts = len(AXIS_ORDERS)
    third = total_rows // 2 // parts
    sizes = [third // 4, third // 16, third // 64]
    scratch = [
        pltpu.VMEM((total_rows // 2, width), jnp.bfloat16),
        pltpu.VMEM((total_rows // 2, width), jnp.bfloat16),
        pltpu.VMEM(gains.shape, jnp.bfloat16),
        pltpu.VMEM(gains.shape, jnp.bfloat16),
    ]
    for part in range(parts):
        for size in sizes:
            scratch += [
                pltpu.VMEM((4, size, width), jnp.bfloat16),
                pltpu.VMEM((4, size, width), jnp.bfloat16),
                pltpu.VMEM((size, width), jnp.float32),
            ]
    for part in range(parts):
        for size in reversed(sizes):
            scratch.append(pltpu.VMEM((4, size, width), jnp.bfloat16))
    scratch += [
        pltpu.VMEM((3,) + gains.shape, jnp.bfloat16),
        pltpu.VMEM((3, 4) + gains.shape, jnp.bfloat16),
        pltpu.SemaphoreType.DMA((160,)),
        pltpu.SemaphoreType.DMA((160,)),
    ]
    full, gains = pl.pallas_call(
        reduce_kernel,
        out_shape=(
            jax.ShapeDtypeStruct((total_rows, width), jnp.bfloat16),
            jax.ShapeDtypeStruct(gains.shape, jnp.float32),
        ),
        in_specs=[pl.BlockSpec(memory_space=pltpu.VMEM)] * 2,
        out_specs=(
            pl.BlockSpec(memory_space=pltpu.VMEM),
            pl.BlockSpec(memory_space=pltpu.VMEM),
        ),
        scratch_shapes=scratch,
        compiler_params=pltpu.CompilerParams(
            collective_id=0, has_side_effects=True, vmem_limit_bytes=60 * 1024 * 1024
        ),
    )(rows, gains)
    return full.astype(jnp.float32), gains

def on_device(
    features, curve_pos, pattern, ln1_gain, w_qkv, w_out, ln2_gain, w_up, w_down, out_grad
):
    seq_devices = lax.axis_size("seq")
    seq_index = lax.axis_index("seq")
    dev_rows = features.shape[1]
    capacity = 2 * dev_rows // seq_devices
    blocks_dev = dev_rows // BLK
    position = curve_pos[0]
    send_index, source_for_slot = node_plan(position, seq_index, dev_rows, capacity, seq_devices)
    outgoing = jnp.zeros((seq_devices * capacity, D), jnp.bfloat16).at[send_index].set(features[0])
    arrived = lax.all_to_all(
        outgoing.reshape(seq_devices, capacity, D), "seq", split_axis=0, concat_axis=0, tiled=True
    )
    curve_rows = arrived.reshape(seq_devices * capacity, D)[source_for_slot]
    normed_a, normed1, inverse1 = layer_norm(curve_rows, ln1_gain)
    qkv = jnp.dot(normed_a, w_qkv, preferred_element_type=jnp.float32).astype(jnp.bfloat16)
    queries = qkv[:, :D]
    keyval = qkv[:, D:]
    distances = shift_distances(seq_devices)
    pieces = [keyval]
    for distance in distances:
        pieces.append(from_behind(keyval, "seq", distance))
    keyval_all = jnp.concatenate(pieces, axis=0)
    source_dev = jnp.stack(
        [seq_index] + [(seq_index - distance) % seq_devices for distance in distances]
    )
    key_blocks = (
        source_dev[:, None] * blocks_dev + jnp.arange(blocks_dev, dtype=jnp.int32)[None, :]
    ).reshape(-1)
    own_lists = lax.dynamic_slice_in_dim(pattern[0], seq_index * blocks_dev, blocks_dev, axis=0)
    matches = (own_lists[:, :, None] == key_blocks[None, None, :]).astype(jnp.int32)
    selected = jnp.sum(
        matches * jnp.arange(key_blocks.shape[0], dtype=jnp.int32)[None, None, :], axis=-1
    )
    attn_out, log_totals = attention_forward(queries, keyval_all, selected)
    hidden_res = (
        curve_rows.astype(jnp.float32)
        + jnp.dot(attn_out, w_out, preferred_element_type=jnp.float32)
    ).astype(jnp.bfloat16)
    normed_b, normed2, inverse2 = layer_norm(hidden_res, ln2_gain)
    pre_act = jnp.dot(normed_b, w_up, preferred_element_type=jnp.float32)
    activated = jax.nn.gelu(pre_act, approximate=True).astype(jnp.bfloat16)
    curve_out = (
        hidden_res.astype(jnp.float32)
        + jnp.dot(activated, w_down, preferred_element_type=jnp.float32)
    ).astype(jnp.bfloat16)
    leaving = (
        jnp.zeros((seq_devices * capacity, D), jnp.bfloat16).at[source_for_slot].set(curve_out)
    )
    returned = lax.all_to_all(
        leaving.reshape(seq_devices, capacity, D), "seq", split_axis=0, concat_axis=0, tiled=True
    )
    block_out = returned.reshape(seq_devices * capacity, D)[send_index]
    grad_outgoing = (
        jnp.zeros((seq_devices * capacity, D), jnp.bfloat16).at[send_index].set(out_grad[0])
    )
    grad_arrived = lax.all_to_all(
        grad_outgoing.reshape(seq_devices, capacity, D),
        "seq",
        split_axis=0,
        concat_axis=0,
        tiled=True,
    )
    grad_curve = grad_arrived.reshape(seq_devices * capacity, D)[source_for_slot]
    grad_pre = gelu_back(pre_act, times_transposed(grad_curve, w_down)).astype(jnp.bfloat16)
    grad_down = inner_rows(activated, grad_curve)
    grad_normed_b = times_transposed(grad_pre, w_up)
    grad_up = inner_rows(normed_b, grad_pre)
    grad_gain2 = jnp.sum(grad_normed_b * normed2, axis=0)
    grad_hidden = (
        grad_curve.astype(jnp.float32) + norm_back(grad_normed_b, ln2_gain, normed2, inverse2)
    ).astype(jnp.bfloat16)
    grad_attn = times_transposed(grad_hidden, w_out).astype(jnp.bfloat16)
    grad_out = inner_rows(attn_out, grad_hidden)
    resent = [keyval]
    for distance in distances:
        resent.append(from_behind(keyval, "seq", distance))
    keyval_back = jnp.concatenate(resent, axis=0)
    grad_query, grad_keyval_all = attention_backward(
        queries, keyval_back, selected, attn_out, log_totals, grad_attn
    )
    grad_keyval = grad_keyval_all[:dev_rows]
    for index_pos, distance in enumerate(distances):
        partial_rows = grad_keyval_all[(index_pos + 1) * dev_rows : (index_pos + 2) * dev_rows]
        grad_keyval = grad_keyval + from_behind(
            partial_rows.astype(jnp.bfloat16), "seq", -distance
        ).astype(partial_rows.dtype)
    grad_qkv_rows = jnp.concatenate([grad_query, grad_keyval.astype(jnp.bfloat16)], axis=1)
    grad_normed_a = times_transposed(grad_qkv_rows, w_qkv)
    grad_qkv = inner_rows(normed_a, grad_qkv_rows)
    grad_gain1 = jnp.sum(grad_normed_a * normed1, axis=0)
    grad_curve_in = (
        grad_hidden.astype(jnp.float32) + norm_back(grad_normed_a, ln1_gain, normed1, inverse1)
    ).astype(jnp.bfloat16)
    grad_leaving = (
        jnp.zeros((seq_devices * capacity, D), jnp.bfloat16).at[source_for_slot].set(grad_curve_in)
    )
    grad_returned = lax.all_to_all(
        grad_leaving.reshape(seq_devices, capacity, D),
        "seq",
        split_axis=0,
        concat_axis=0,
        tiled=True,
    )
    input_grad = grad_returned.reshape(seq_devices * capacity, D)[send_index]
    weight_rows = jnp.concatenate(
        [grad_qkv[:, index * D : (index + 1) * D] for index in range(3)]
        + [grad_out]
        + [grad_up[:, index * D : (index + 1) * D] for index in range(4)]
        + [grad_down],
        axis=0,
    )
    gain_rows = jnp.zeros((8, D), jnp.float32).at[0].set(grad_gain1).at[1].set(grad_gain2)
    weight_rows, gain_rows = reduce_everywhere(weight_rows, gain_rows)
    grad_qkv = jnp.concatenate([weight_rows[index * D : (index + 1) * D] for index in range(3)], axis=1)
    grad_out = weight_rows[3 * D : 4 * D]
    grad_up = jnp.concatenate(
        [weight_rows[(4 + index) * D : (5 + index) * D] for index in range(4)], axis=1
    )
    grad_down = weight_rows[8 * D :]
    grad_gain1 = gain_rows[0]
    grad_gain2 = gain_rows[1]
    return (
        block_out[None],
        input_grad[None],
        grad_qkv,
        grad_out,
        grad_up,
        grad_down,
        grad_gain1,
        grad_gain2,
    )


def solution(mesh):
    return jax.shard_map(
        on_device,
        mesh=mesh,
        in_specs=(
            P("dp", "seq", None),
            P("dp", None),
            P("dp", None, None),
            P(),
            P(),
            P(),
            P(),
            P(),
            P(),
            P("dp", "seq", None),
        ),
        out_specs=(P("dp", "seq", None), P("dp", "seq", None), P(), P(), P(), P(), P(), P()),
        check_vma=False,
    )
```

```python
from functools import partial

import jax
import jax.numpy as jnp
from jax import lax
from jax.experimental import pallas as pl
from jax.experimental.pallas import tpu as pltpu
from jax.sharding import PartitionSpec as P

D = 512
HEADS = 8
BLK = 128


EPSILON = 1e-05


def from_behind(x, axis, by):
    length = lax.axis_size(axis)
    return lax.ppermute(x, axis, [(i, (i + by) % length) for i in range(length)])


def layer_norm(rows_in, gain_vec):
    values = rows_in.astype(jnp.float32)
    centered = values - jnp.mean(values, axis=-1, keepdims=True)
    inverse = lax.rsqrt(jnp.mean(centered * centered, axis=-1, keepdims=True) + EPSILON)
    normed = centered * inverse
    return ((normed * gain_vec).astype(jnp.bfloat16), normed, inverse)


def norm_back(incoming, gain_vec, normed, inverse):
    scaled = incoming * gain_vec
    return inverse * (
        scaled
        - jnp.mean(scaled, axis=-1, keepdims=True)
        - normed * jnp.mean(scaled * normed, axis=-1, keepdims=True)
    )


def gelu_back(pre_act, incoming):
    return jax.vjp(partial(jax.nn.gelu, approximate=True), pre_act)[1](incoming)[0]


def inner_rows(left_mat, right_mat):
    return lax.dot_general(
        left_mat, right_mat, (((0,), (0,)), ((), ())), preferred_element_type=jnp.float32
    )


def times_transposed(left_mat, right_mat):
    return lax.dot_general(
        left_mat, right_mat, (((1,), (1,)), ((), ())), preferred_element_type=jnp.float32
    )


def split_heads(rows_in):
    return rows_in.reshape(rows_in.shape[0] // BLK, BLK, HEADS, D // HEADS)


def listed_heads(keyval_all, selected):
    blocks = keyval_all.reshape(keyval_all.shape[0] // BLK, BLK, 2 * D)
    picked = blocks[selected]
    shape_out = picked.shape[:3] + (HEADS, D // HEADS)
    return (picked[..., :D].reshape(shape_out), picked[..., D:].reshape(shape_out))


def shift_distances(seq_devices):
    levels = seq_devices.bit_length() - 1
    distances = []
    for level_idx in range(levels):
        stride = 2**level_idx
        if 2 * stride == seq_devices:
            distances.append(stride)
        else:
            distances.extend([stride, -stride])
    return distances


def node_plan(position, seq_index, dev_rows, capacity, seq_devices):
    own_position = lax.dynamic_slice_in_dim(position, seq_index * dev_rows, dev_rows)
    target_dev = own_position // dev_rows
    dest_hits = (target_dev[:, None] == jnp.arange(seq_devices, dtype=jnp.int32)[None, :]).astype(
        jnp.int32
    )
    send_rank = jnp.sum((jnp.cumsum(dest_hits, axis=0) - dest_hits) * dest_hits, axis=1)
    send_index = target_dev * capacity + send_rank
    layout = position.reshape(seq_devices, dev_rows)
    arriving = (layout // dev_rows == seq_index).astype(jnp.int32)
    arrive_rank = jnp.cumsum(arriving, axis=1) - arriving
    source_index = jnp.arange(seq_devices, dtype=jnp.int32)[:, None] * capacity + arrive_rank
    del source_index
    total = position.shape[0]
    wanted = seq_index * dev_rows + jnp.arange(dev_rows, dtype=jnp.int32)
    slot_node = jnp.sum(
        jnp.where(
            position[None, :] == wanted[:, None], jnp.arange(total, dtype=jnp.int32)[None, :], 0
        ),
        axis=1,
    )
    source_for_slot = (slot_node // dev_rows) * capacity + arrive_rank.reshape(-1)[slot_node]
    return (send_index, source_for_slot)


def attention_forward(queries, keyval_all, selected):
    query_heads = split_heads(queries)
    key_heads, value_heads = listed_heads(keyval_all, selected)
    scores = (
        jnp.einsum("aihd,akjhd->haikj", query_heads, key_heads, preferred_element_type=jnp.float32)
        * 0.125
    )
    largest = jnp.max(scores, axis=(3, 4), keepdims=True)
    totals = jnp.sum(jnp.exp(scores - largest), axis=(3, 4), keepdims=True)
    log_totals = largest + jnp.log(totals)
    attn_probs = jnp.exp(scores - log_totals).astype(jnp.bfloat16)
    result = jnp.einsum(
        "haikj,akjhd->aihd", attn_probs, value_heads, preferred_element_type=jnp.float32
    )
    return (result.astype(jnp.bfloat16).reshape(queries.shape[0], D), log_totals)


def attention_backward(queries, keyval_all, selected, attn_out, log_totals, grad_attn):
    query_heads = split_heads(queries)
    key_heads, value_heads = listed_heads(keyval_all, selected)
    out_heads = split_heads(attn_out)
    grad_heads = split_heads(grad_attn)
    scores = (
        jnp.einsum("aihd,akjhd->haikj", query_heads, key_heads, preferred_element_type=jnp.float32)
        * 0.125
    )
    attn_exact = jnp.exp(scores - log_totals)
    attn_probs = attn_exact.astype(jnp.bfloat16)
    grad_probs = jnp.einsum(
        "aihd,akjhd->haikj", grad_heads, value_heads, preferred_element_type=jnp.float32
    )
    row_dots = jnp.einsum(
        "aihd,aihd->hai", grad_heads, out_heads, preferred_element_type=jnp.float32
    )[..., None, None]
    grad_scores = (attn_exact * (grad_probs - row_dots) * 0.125).astype(jnp.bfloat16)
    grad_query = jnp.einsum(
        "haikj,akjhd->aihd", grad_scores, key_heads, preferred_element_type=jnp.float32
    )
    grad_keys = jnp.einsum(
        "haikj,aihd->akjhd", grad_scores, query_heads, preferred_element_type=jnp.float32
    )
    grad_values = jnp.einsum(
        "haikj,aihd->akjhd", attn_probs, grad_heads, preferred_element_type=jnp.float32
    )
    block_shape = grad_keys.shape[:3] + (D,)
    grad_picked = jnp.concatenate(
        [grad_keys.reshape(block_shape), grad_values.reshape(block_shape)], axis=-1
    )
    total_rows = keyval_all.shape[0]
    one_hot = (
        selected[:, :, None] == jnp.arange(total_rows // BLK, dtype=jnp.int32)[None, None, :]
    ).astype(jnp.float32)
    grad_keyval = jnp.einsum(
        "akb,akjc->bjc",
        one_hot,
        grad_picked,
        precision=lax.Precision.HIGHEST,
        preferred_element_type=jnp.float32,
    )
    return (
        grad_query.astype(jnp.bfloat16).reshape(queries.shape[0], D),
        grad_keyval.reshape(total_rows, 2 * D),
    )


MESH_IDS = pl.DeviceIdType.MESH
RING_KINDS = ("x", "y", "z")
AXIS_ORDERS = (("x", "y", "z"), ("y", "z", "x"), ("z", "x", "y"))


def reduce_kernel(w_ref, g_ref, wout_ref, gout_ref, send0, recv0, gsend0, grecv0, *rest):
    parts = len(AXIS_ORDERS)
    ring_bufs = [[rest[9 * p + 3 * s : 9 * p + 3 * s + 3] for s in range(3)] for p in range(parts)]
    gather_bufs = [rest[9 * parts + 3 * p : 9 * parts + 3 * p + 3] for p in range(parts)]
    gsend, grecv, send_sem, recv_sem = rest[12 * parts :]
    seq = lax.axis_index("seq")
    dp = lax.axis_index("dp")
    core = seq % 2
    place = {"x": (seq // 2) % 4, "y": seq // 8, "z": dp}

    def peer(kind, member):
        if kind == "core":
            return (seq + 1 - 2 * core, dp)
        if kind == "x":
            return (seq + (member - place["x"]) * 2, dp)
        if kind == "y":
            return (seq + (member - place["y"]) * 8, dp)
        return (seq, member)

    barrier = pltpu.get_barrier_semaphore()
    peers = [peer("core", 0)]
    for kind in RING_KINDS:
        for shift in (1, 2, 3):
            peers.append(peer(kind, (place[kind] + shift) % 4))
    for target in peers:
        pl.semaphore_signal(barrier, inc=1, device_id=target, device_id_type=MESH_IDS)
    pl.semaphore_wait(barrier, len(peers))

    counter = [0]
    sent = []

    def send(src, dst, recv_index, target):
        copy = pltpu.make_async_remote_copy(
            src_ref=src,
            dst_ref=dst,
            send_sem=send_sem.at[counter[0]],
            recv_sem=recv_sem.at[recv_index],
            device_id=target,
            device_id_type=MESH_IDS,
        )
        counter[0] += 1
        copy.start()
        sent.append(copy)

    def arrive(dst, recv_index):
        pltpu.make_async_remote_copy(
            src_ref=dst,
            dst_ref=dst,
            send_sem=send_sem.at[0],
            recv_sem=recv_sem.at[recv_index],
            device_id=peers[0],
            device_id_type=MESH_IDS,
        ).wait_recv()

    half = send0.shape[0]
    third = half // parts
    gsend0[...] = g_ref[...].astype(jnp.bfloat16)
    send(gsend0, grecv0, 1, peers[0])
    for part in range(parts):
        rows = pl.ds(pl.multiple_of(part * third, 16), third)
        source_rows = pl.ds(pl.multiple_of((1 - core) * half + part * third, 16), third)
        send0[rows, :] = w_ref[source_rows, :].astype(jnp.bfloat16)
        send(send0.at[rows], recv0.at[rows], 150 + part, peers[0])
    arrive(grecv0, 1)
    gains = gsend0[...].astype(jnp.float32) + grecv0[...].astype(jnp.float32)

    def first_chunk(part, member, size):
        offset = part * third + member * size
        mine = w_ref[pl.ds(pl.multiple_of(core * half + offset, 16), size), :]
        return mine + recv0[pl.ds(pl.multiple_of(offset, 16), size), :].astype(jnp.float32)

    sources = [None] * parts
    def ring_send_step(stage, part, gains):
            kind = AXIS_ORDERS[part][stage]
            sbuf, rbuf, total = ring_bufs[part][stage]
            size = sbuf.shape[1]
            pos = place[kind]
            base = 2 + 12 * (3 * part + stage)
            source = sources[part]

            def chunk(member, source=source, size=size, part=part):
                if source is None:
                    return first_chunk(part, member, size)
                return source[pl.ds(pl.multiple_of(member * size, 16), size), :]

            if stage == 0:
                arrive(recv0.at[pl.ds(pl.multiple_of(part * third, 16), third)], 150 + part)
            if part == 0:
                gsend[stage] = gains.astype(jnp.bfloat16)
                grecv[stage, pos] = gsend[stage]
            for shift in (1, 2, 3):
                member = (pos + shift) % 4
                sbuf[member] = chunk(member).astype(jnp.bfloat16)
                send(sbuf.at[member], rbuf.at[pos], base + pos, peer(kind, member))
                if part == 0:
                    send(gsend.at[stage], grecv.at[stage, pos], base + 4 + pos, peer(kind, member))
            total[...] = chunk(pos)
            return gains

    def ring_wait_step(stage, part, gains):
            kind = AXIS_ORDERS[part][stage]
            sbuf, rbuf, total = ring_bufs[part][stage]
            pos = place[kind]
            base = 2 + 12 * (3 * part + stage)
            for shift in (1, 2, 3):
                slot = (pos - shift) % 4
                arrive(rbuf.at[slot], base + slot)
                total[...] += rbuf[slot].astype(jnp.float32)
                if part == 0:
                    arrive(grecv.at[stage, slot], base + 4 + slot)
            if part == 0:
                got = grecv[stage].astype(jnp.float32)
                gains = (got[0] + got[1]) + (got[2] + got[3])
            sources[part] = total
            return gains

    for part in range(parts):
        gains = ring_send_step(0, part, gains)
    for stage in range(3):
        for part in range(parts):
            gains = ring_wait_step(stage, part, gains)
            if stage < 2:
                gains = ring_send_step(stage + 1, part, gains)
    gout_ref[...] = gains

    owns = [sources[part][...].astype(jnp.bfloat16) for part in range(parts)]

    def gather_send_step(stage, part):
        kind = AXIS_ORDERS[part][2 - stage]
        gathered = gather_bufs[part][stage]
        pos = place[kind]
        base = 2 + 12 * 9 + 4 * (3 * part + stage)
        gathered[pos] = owns[part]
        for shift in (1, 2, 3):
            member = (pos + shift) % 4
            send(gathered.at[pos], gathered.at[pos], base + pos, peer(kind, member))

    def gather_wait_step(stage, part):
        kind = AXIS_ORDERS[part][2 - stage]
        gathered = gather_bufs[part][stage]
        pos = place[kind]
        base = 2 + 12 * 9 + 4 * (3 * part + stage)
        for shift in (1, 2, 3):
            arrive(gathered.at[(pos - shift) % 4], base + (pos - shift) % 4)
        owns[part] = gathered[...].reshape(4 * gathered.shape[1], gathered.shape[2])

    for part in range(parts):
        gather_send_step(0, part)
    for stage in range(3):
        for part in range(parts):
            gather_wait_step(stage, part)
            if stage < 2:
                gather_send_step(stage + 1, part)
            else:
                rows = pl.ds(pl.multiple_of(core * half + part * third, 16), third)
                wout_ref[rows, :] = owns[part]
                send(wout_ref.at[rows], wout_ref.at[rows], 154 + part, peers[0])
    for part in range(parts):
        rows = pl.ds(pl.multiple_of((1 - core) * half + part * third, 16), third)
        arrive(wout_ref.at[rows], 154 + part)
    for copy in sent:
        copy.wait_send()


def reduce_everywhere(rows, gains):
    total_rows, width = rows.shape
    parts = len(AXIS_ORDERS)
    third = total_rows // 2 // parts
    sizes = [third // 4, third // 16, third // 64]
    scratch = [
        pltpu.VMEM((total_rows // 2, width), jnp.bfloat16),
        pltpu.VMEM((total_rows // 2, width), jnp.bfloat16),
        pltpu.VMEM(gains.shape, jnp.bfloat16),
        pltpu.VMEM(gains.shape, jnp.bfloat16),
    ]
    for part in range(parts):
        for size in sizes:
            scratch += [
                pltpu.VMEM((4, size, width), jnp.bfloat16),
                pltpu.VMEM((4, size, width), jnp.bfloat16),
                pltpu.VMEM((size, width), jnp.float32),
            ]
    for part in range(parts):
        for size in reversed(sizes):
            scratch.append(pltpu.VMEM((4, size, width), jnp.bfloat16))
    scratch += [
        pltpu.VMEM((3,) + gains.shape, jnp.bfloat16),
        pltpu.VMEM((3, 4) + gains.shape, jnp.bfloat16),
        pltpu.SemaphoreType.DMA((160,)),
        pltpu.SemaphoreType.DMA((160,)),
    ]
    full, gains = pl.pallas_call(
        reduce_kernel,
        out_shape=(
            jax.ShapeDtypeStruct((total_rows, width), jnp.bfloat16),
            jax.ShapeDtypeStruct(gains.shape, jnp.float32),
        ),
        in_specs=[pl.BlockSpec(memory_space=pltpu.VMEM)] * 2,
        out_specs=(
            pl.BlockSpec(memory_space=pltpu.VMEM),
            pl.BlockSpec(memory_space=pltpu.VMEM),
        ),
        scratch_shapes=scratch,
        compiler_params=pltpu.CompilerParams(
            collective_id=0, has_side_effects=True, vmem_limit_bytes=60 * 1024 * 1024
        ),
    )(rows, gains)
    return full.astype(jnp.float32), gains

def on_device(
    features, curve_pos, pattern, ln1_gain, w_qkv, w_out, ln2_gain, w_up, w_down, out_grad
):
    seq_devices = lax.axis_size("seq")
    seq_index = lax.axis_index("seq")
    dev_rows = features.shape[1]
    capacity = 2 * dev_rows // seq_devices
    blocks_dev = dev_rows // BLK
    position = curve_pos[0]
    send_index, source_for_slot = node_plan(position, seq_index, dev_rows, capacity, seq_devices)
    outgoing = jnp.zeros((seq_devices * capacity, D), jnp.bfloat16).at[send_index].set(features[0])
    arrived = lax.all_to_all(
        outgoing.reshape(seq_devices, capacity, D), "seq", split_axis=0, concat_axis=0, tiled=True
    )
    curve_rows = arrived.reshape(seq_devices * capacity, D)[source_for_slot]
    normed_a, normed1, inverse1 = layer_norm(curve_rows, ln1_gain)
    qkv = jnp.dot(normed_a, w_qkv, preferred_element_type=jnp.float32).astype(jnp.bfloat16)
    queries = qkv[:, :D]
    keyval = qkv[:, D:]
    distances = shift_distances(seq_devices)
    pieces = [keyval]
    for distance in distances:
        pieces.append(from_behind(keyval, "seq", distance))
    keyval_all = jnp.concatenate(pieces, axis=0)
    source_dev = jnp.stack(
        [seq_index] + [(seq_index - distance) % seq_devices for distance in distances]
    )
    key_blocks = (
        source_dev[:, None] * blocks_dev + jnp.arange(blocks_dev, dtype=jnp.int32)[None, :]
    ).reshape(-1)
    own_lists = lax.dynamic_slice_in_dim(pattern[0], seq_index * blocks_dev, blocks_dev, axis=0)
    matches = (own_lists[:, :, None] == key_blocks[None, None, :]).astype(jnp.int32)
    selected = jnp.sum(
        matches * jnp.arange(key_blocks.shape[0], dtype=jnp.int32)[None, None, :], axis=-1
    )
    attn_out, log_totals = attention_forward(queries, keyval_all, selected)
    hidden_res = (
        curve_rows.astype(jnp.float32)
        + jnp.dot(attn_out, w_out, preferred_element_type=jnp.float32)
    ).astype(jnp.bfloat16)
    normed_b, normed2, inverse2 = layer_norm(hidden_res, ln2_gain)
    pre_act = jnp.dot(normed_b, w_up, preferred_element_type=jnp.float32)
    activated = jax.nn.gelu(pre_act, approximate=True).astype(jnp.bfloat16)
    curve_out = (
        hidden_res.astype(jnp.float32)
        + jnp.dot(activated, w_down, preferred_element_type=jnp.float32)
    ).astype(jnp.bfloat16)
    leaving = (
        jnp.zeros((seq_devices * capacity, D), jnp.bfloat16).at[source_for_slot].set(curve_out)
    )
    returned = lax.all_to_all(
        leaving.reshape(seq_devices, capacity, D), "seq", split_axis=0, concat_axis=0, tiled=True
    )
    block_out = returned.reshape(seq_devices * capacity, D)[send_index]
    grad_outgoing = (
        jnp.zeros((seq_devices * capacity, D), jnp.bfloat16).at[send_index].set(out_grad[0])
    )
    grad_arrived = lax.all_to_all(
        grad_outgoing.reshape(seq_devices, capacity, D),
        "seq",
        split_axis=0,
        concat_axis=0,
        tiled=True,
    )
    grad_curve = grad_arrived.reshape(seq_devices * capacity, D)[source_for_slot]
    grad_pre = gelu_back(pre_act, times_transposed(grad_curve, w_down)).astype(jnp.bfloat16)
    grad_down = inner_rows(activated, grad_curve)
    grad_normed_b = times_transposed(grad_pre, w_up)
    grad_up_blocks = [
        inner_rows(normed_b, grad_pre[:, index * D : (index + 1) * D])
        for index in range(grad_pre.shape[1] // D)
    ]
    grad_gain2 = jnp.sum(grad_normed_b * normed2, axis=0)
    grad_hidden = (
        grad_curve.astype(jnp.float32) + norm_back(grad_normed_b, ln2_gain, normed2, inverse2)
    ).astype(jnp.bfloat16)
    grad_attn = times_transposed(grad_hidden, w_out).astype(jnp.bfloat16)
    grad_out = inner_rows(attn_out, grad_hidden)
    resent = [keyval]
    for distance in distances:
        resent.append(from_behind(keyval, "seq", distance))
    keyval_back = jnp.concatenate(resent, axis=0)
    grad_query, grad_keyval_all = attention_backward(
        queries, keyval_back, selected, attn_out, log_totals, grad_attn
    )
    grad_keyval = grad_keyval_all[:dev_rows]
    for index_pos, distance in enumerate(distances):
        partial_rows = grad_keyval_all[(index_pos + 1) * dev_rows : (index_pos + 2) * dev_rows]
        grad_keyval = grad_keyval + from_behind(
            partial_rows.astype(jnp.bfloat16), "seq", -distance
        ).astype(partial_rows.dtype)
    grad_qkv_rows = jnp.concatenate([grad_query, grad_keyval.astype(jnp.bfloat16)], axis=1)
    grad_normed_a = times_transposed(grad_qkv_rows, w_qkv)
    grad_qkv_blocks = [
        inner_rows(normed_a, grad_qkv_rows[:, index * D : (index + 1) * D])
        for index in range(grad_qkv_rows.shape[1] // D)
    ]
    grad_gain1 = jnp.sum(grad_normed_a * normed1, axis=0)
    grad_curve_in = (
        grad_hidden.astype(jnp.float32) + norm_back(grad_normed_a, ln1_gain, normed1, inverse1)
    ).astype(jnp.bfloat16)
    grad_leaving = (
        jnp.zeros((seq_devices * capacity, D), jnp.bfloat16).at[source_for_slot].set(grad_curve_in)
    )
    grad_returned = lax.all_to_all(
        grad_leaving.reshape(seq_devices, capacity, D),
        "seq",
        split_axis=0,
        concat_axis=0,
        tiled=True,
    )
    input_grad = grad_returned.reshape(seq_devices * capacity, D)[send_index]
    weight_rows = jnp.concatenate(
        grad_qkv_blocks + [grad_out] + grad_up_blocks + [grad_down],
        axis=0,
    )
    gain_rows = jnp.zeros((8, D), jnp.float32).at[0].set(grad_gain1).at[1].set(grad_gain2)
    weight_rows, gain_rows = reduce_everywhere(weight_rows, gain_rows)
    grad_qkv = jnp.concatenate([weight_rows[index * D : (index + 1) * D] for index in range(3)], axis=1)
    grad_out = weight_rows[3 * D : 4 * D]
    grad_up = jnp.concatenate(
        [weight_rows[(4 + index) * D : (5 + index) * D] for index in range(4)], axis=1
    )
    grad_down = weight_rows[8 * D :]
    grad_gain1 = gain_rows[0]
    grad_gain2 = gain_rows[1]
    return (
        block_out[None],
        input_grad[None],
        grad_qkv,
        grad_out,
        grad_up,
        grad_down,
        grad_gain1,
        grad_gain2,
    )


def solution(mesh):
    return jax.shard_map(
        on_device,
        mesh=mesh,
        in_specs=(
            P("dp", "seq", None),
            P("dp", None),
            P("dp", None, None),
            P(),
            P(),
            P(),
            P(),
            P(),
            P(),
            P("dp", "seq", None),
        ),
        out_specs=(P("dp", "seq", None), P("dp", "seq", None), P(), P(), P(), P(), P(), P()),
        check_vma=False,
    )
```

```python
from functools import partial

import jax
import jax.numpy as jnp
from jax import lax
from jax.experimental import pallas as pl
from jax.experimental.pallas import tpu as pltpu
from jax.sharding import PartitionSpec as P

D = 512
HEADS = 8
BLK = 128


EPSILON = 1e-05


def from_behind(x, axis, by):
    length = lax.axis_size(axis)
    return lax.ppermute(x, axis, [(i, (i + by) % length) for i in range(length)])


def layer_norm(rows_in, gain_vec):
    values = rows_in.astype(jnp.float32)
    centered = values - jnp.mean(values, axis=-1, keepdims=True)
    inverse = lax.rsqrt(jnp.mean(centered * centered, axis=-1, keepdims=True) + EPSILON)
    normed = centered * inverse
    return ((normed * gain_vec).astype(jnp.bfloat16), normed, inverse)


def norm_back(incoming, gain_vec, normed, inverse):
    scaled = incoming * gain_vec
    return inverse * (
        scaled
        - jnp.mean(scaled, axis=-1, keepdims=True)
        - normed * jnp.mean(scaled * normed, axis=-1, keepdims=True)
    )


def gelu_back(pre_act, incoming):
    return jax.vjp(partial(jax.nn.gelu, approximate=True), pre_act)[1](incoming)[0]


def inner_rows(left_mat, right_mat):
    return lax.dot_general(
        left_mat, right_mat, (((0,), (0,)), ((), ())), preferred_element_type=jnp.float32
    )


def times_transposed(left_mat, right_mat):
    return lax.dot_general(
        left_mat, right_mat, (((1,), (1,)), ((), ())), preferred_element_type=jnp.float32
    )


def split_heads(rows_in):
    return rows_in.reshape(rows_in.shape[0] // BLK, BLK, HEADS, D // HEADS)


def listed_heads(keyval_all, selected):
    blocks = keyval_all.reshape(keyval_all.shape[0] // BLK, BLK, 2 * D)
    picked = blocks[selected]
    shape_out = picked.shape[:3] + (HEADS, D // HEADS)
    return (picked[..., :D].reshape(shape_out), picked[..., D:].reshape(shape_out))


def shift_distances(seq_devices):
    levels = seq_devices.bit_length() - 1
    distances = []
    for level_idx in range(levels):
        stride = 2**level_idx
        if 2 * stride == seq_devices:
            distances.append(stride)
        else:
            distances.extend([stride, -stride])
    return distances


def node_plan(position, seq_index, dev_rows, capacity, seq_devices):
    own_position = lax.dynamic_slice_in_dim(position, seq_index * dev_rows, dev_rows)
    target_dev = own_position // dev_rows
    dest_hits = (target_dev[:, None] == jnp.arange(seq_devices, dtype=jnp.int32)[None, :]).astype(
        jnp.int32
    )
    send_rank = jnp.sum((jnp.cumsum(dest_hits, axis=0) - dest_hits) * dest_hits, axis=1)
    send_index = target_dev * capacity + send_rank
    layout = position.reshape(seq_devices, dev_rows)
    arriving = (layout // dev_rows == seq_index).astype(jnp.int32)
    arrive_rank = jnp.cumsum(arriving, axis=1) - arriving
    source_index = jnp.arange(seq_devices, dtype=jnp.int32)[:, None] * capacity + arrive_rank
    del source_index
    total = position.shape[0]
    wanted = seq_index * dev_rows + jnp.arange(dev_rows, dtype=jnp.int32)
    slot_node = jnp.sum(
        jnp.where(
            position[None, :] == wanted[:, None], jnp.arange(total, dtype=jnp.int32)[None, :], 0
        ),
        axis=1,
    )
    source_for_slot = (slot_node // dev_rows) * capacity + arrive_rank.reshape(-1)[slot_node]
    return (send_index, source_for_slot)


def attention_forward(queries, keyval_all, selected):
    query_heads = split_heads(queries)
    key_heads, value_heads = listed_heads(keyval_all, selected)
    scores = (
        jnp.einsum("aihd,akjhd->haikj", query_heads, key_heads, preferred_element_type=jnp.float32)
        * 0.125
    )
    largest = jnp.max(scores, axis=(3, 4), keepdims=True)
    totals = jnp.sum(jnp.exp(scores - largest), axis=(3, 4), keepdims=True)
    log_totals = largest + jnp.log(totals)
    attn_probs = jnp.exp(scores - log_totals).astype(jnp.bfloat16)
    result = jnp.einsum(
        "haikj,akjhd->aihd", attn_probs, value_heads, preferred_element_type=jnp.float32
    )
    return (result.astype(jnp.bfloat16).reshape(queries.shape[0], D), log_totals)


def attention_backward(queries, keyval_all, selected, attn_out, log_totals, grad_attn):
    query_heads = split_heads(queries)
    key_heads, value_heads = listed_heads(keyval_all, selected)
    out_heads = split_heads(attn_out)
    grad_heads = split_heads(grad_attn)
    scores = (
        jnp.einsum("aihd,akjhd->haikj", query_heads, key_heads, preferred_element_type=jnp.float32)
        * 0.125
    )
    attn_exact = jnp.exp(scores - log_totals)
    attn_probs = attn_exact.astype(jnp.bfloat16)
    grad_probs = jnp.einsum(
        "aihd,akjhd->haikj", grad_heads, value_heads, preferred_element_type=jnp.float32
    )
    row_dots = jnp.einsum(
        "aihd,aihd->hai", grad_heads, out_heads, preferred_element_type=jnp.float32
    )[..., None, None]
    grad_scores = (attn_exact * (grad_probs - row_dots) * 0.125).astype(jnp.bfloat16)
    grad_query = jnp.einsum(
        "haikj,akjhd->aihd", grad_scores, key_heads, preferred_element_type=jnp.float32
    )
    grad_keys = jnp.einsum(
        "haikj,aihd->akjhd", grad_scores, query_heads, preferred_element_type=jnp.float32
    )
    grad_values = jnp.einsum(
        "haikj,aihd->akjhd", attn_probs, grad_heads, preferred_element_type=jnp.float32
    )
    block_shape = grad_keys.shape[:3] + (D,)
    grad_picked = jnp.concatenate(
        [grad_keys.reshape(block_shape), grad_values.reshape(block_shape)], axis=-1
    )
    total_rows = keyval_all.shape[0]
    one_hot = (
        selected[:, :, None] == jnp.arange(total_rows // BLK, dtype=jnp.int32)[None, None, :]
    ).astype(jnp.float32)
    grad_keyval = jnp.einsum(
        "akb,akjc->bjc",
        one_hot,
        grad_picked,
        precision=lax.Precision.HIGHEST,
        preferred_element_type=jnp.float32,
    )
    return (
        grad_query.astype(jnp.bfloat16).reshape(queries.shape[0], D),
        grad_keyval.reshape(total_rows, 2 * D),
    )


MESH_IDS = pl.DeviceIdType.MESH
RING_KINDS = ("x", "y", "z")
AXIS_ORDERS = (("x", "y", "z"), ("y", "z", "x"), ("z", "x", "y"))


def reduce_kernel(
    w_ref, g_ref, qkv_ref, proj_ref, up_ref, down_ref, gout_ref, wout_ref, send0, recv0, gsend0, grecv0, *rest
):
    parts = len(AXIS_ORDERS)
    ring_bufs = [[rest[9 * p + 3 * s : 9 * p + 3 * s + 3] for s in range(3)] for p in range(parts)]
    gather_bufs = [rest[9 * parts + 3 * p : 9 * parts + 3 * p + 3] for p in range(parts)]
    gsend, grecv, send_sem, recv_sem = rest[12 * parts :]
    seq = lax.axis_index("seq")
    dp = lax.axis_index("dp")
    core = seq % 2
    place = {"x": (seq // 2) % 4, "y": seq // 8, "z": dp}

    def peer(kind, member):
        if kind == "core":
            return (seq + 1 - 2 * core, dp)
        if kind == "x":
            return (seq + (member - place["x"]) * 2, dp)
        if kind == "y":
            return (seq + (member - place["y"]) * 8, dp)
        return (seq, member)

    barrier = pltpu.get_barrier_semaphore()
    peers = [peer("core", 0)]
    for kind in RING_KINDS:
        for shift in (1, 2, 3):
            peers.append(peer(kind, (place[kind] + shift) % 4))
    for target in peers:
        pl.semaphore_signal(barrier, inc=1, device_id=target, device_id_type=MESH_IDS)
    pl.semaphore_wait(barrier, len(peers))

    counter = [0]
    sent = []

    def send(src, dst, recv_index, target):
        copy = pltpu.make_async_remote_copy(
            src_ref=src,
            dst_ref=dst,
            send_sem=send_sem.at[counter[0]],
            recv_sem=recv_sem.at[recv_index],
            device_id=target,
            device_id_type=MESH_IDS,
        )
        counter[0] += 1
        copy.start()
        sent.append(copy)

    def arrive(dst, recv_index):
        pltpu.make_async_remote_copy(
            src_ref=dst,
            dst_ref=dst,
            send_sem=send_sem.at[0],
            recv_sem=recv_sem.at[recv_index],
            device_id=peers[0],
            device_id_type=MESH_IDS,
        ).wait_recv()

    half = send0.shape[0]
    third = half // parts
    gsend0[...] = g_ref[...].astype(jnp.bfloat16)
    send(gsend0, grecv0, 1, peers[0])
    for part in range(parts):
        rows = pl.ds(pl.multiple_of(part * third, 16), third)
        source_rows = pl.ds(pl.multiple_of((1 - core) * half + part * third, 16), third)
        send0[rows, :] = w_ref[source_rows, :].astype(jnp.bfloat16)
        send(send0.at[rows], recv0.at[rows], 150 + part, peers[0])
    arrive(grecv0, 1)
    gains = gsend0[...].astype(jnp.float32) + grecv0[...].astype(jnp.float32)

    def first_chunk(part, member, size):
        offset = part * third + member * size
        mine = w_ref[pl.ds(pl.multiple_of(core * half + offset, 16), size), :]
        return mine + recv0[pl.ds(pl.multiple_of(offset, 16), size), :].astype(jnp.float32)

    sources = [None] * parts
    def ring_send_step(stage, part, gains):
            kind = AXIS_ORDERS[part][stage]
            sbuf, rbuf, total = ring_bufs[part][stage]
            size = sbuf.shape[1]
            pos = place[kind]
            base = 2 + 12 * (3 * part + stage)
            source = sources[part]

            def chunk(member, source=source, size=size, part=part):
                if source is None:
                    return first_chunk(part, member, size)
                return source[pl.ds(pl.multiple_of(member * size, 16), size), :]

            if stage == 0:
                arrive(recv0.at[pl.ds(pl.multiple_of(part * third, 16), third)], 150 + part)
            if part == 0:
                gsend[stage] = gains.astype(jnp.bfloat16)
                grecv[stage, pos] = gsend[stage]
            for shift in (1, 2, 3):
                member = (pos + shift) % 4
                sbuf[member] = chunk(member).astype(jnp.bfloat16)
                send(sbuf.at[member], rbuf.at[pos], base + pos, peer(kind, member))
                if part == 0:
                    send(gsend.at[stage], grecv.at[stage, pos], base + 4 + pos, peer(kind, member))
            total[...] = chunk(pos)
            return gains

    def ring_wait_step(stage, part, gains):
            kind = AXIS_ORDERS[part][stage]
            sbuf, rbuf, total = ring_bufs[part][stage]
            pos = place[kind]
            base = 2 + 12 * (3 * part + stage)
            for shift in (1, 2, 3):
                slot = (pos - shift) % 4
                arrive(rbuf.at[slot], base + slot)
                total[...] += rbuf[slot].astype(jnp.float32)
                if part == 0:
                    arrive(grecv.at[stage, slot], base + 4 + slot)
            if part == 0:
                got = grecv[stage].astype(jnp.float32)
                gains = (got[0] + got[1]) + (got[2] + got[3])
            sources[part] = total
            return gains

    for part in range(parts):
        gains = ring_send_step(0, part, gains)
    for stage in range(3):
        for part in range(parts):
            gains = ring_wait_step(stage, part, gains)
            if stage < 2:
                gains = ring_send_step(stage + 1, part, gains)
    gout_ref[...] = gains

    owns = [sources[part][...].astype(jnp.bfloat16) for part in range(parts)]

    def gather_send_step(stage, part):
        kind = AXIS_ORDERS[part][2 - stage]
        gathered = gather_bufs[part][stage]
        pos = place[kind]
        base = 2 + 12 * 9 + 4 * (3 * part + stage)
        gathered[pos] = owns[part]
        for shift in (1, 2, 3):
            member = (pos + shift) % 4
            send(gathered.at[pos], gathered.at[pos], base + pos, peer(kind, member))

    def gather_wait_step(stage, part):
        kind = AXIS_ORDERS[part][2 - stage]
        gathered = gather_bufs[part][stage]
        pos = place[kind]
        base = 2 + 12 * 9 + 4 * (3 * part + stage)
        for shift in (1, 2, 3):
            arrive(gathered.at[(pos - shift) % 4], base + (pos - shift) % 4)
        owns[part] = gathered[...].reshape(4 * gathered.shape[1], gathered.shape[2])

    for part in range(parts):
        gather_send_step(0, part)
    for stage in range(3):
        for part in range(parts):
            gather_wait_step(stage, part)
            if stage < 2:
                gather_send_step(stage + 1, part)
            else:
                rows = pl.ds(pl.multiple_of(core * half + part * third, 16), third)
                wout_ref[rows, :] = owns[part]
                send(wout_ref.at[rows], wout_ref.at[rows], 154 + part, peers[0])
    for part in range(parts):
        rows = pl.ds(pl.multiple_of((1 - core) * half + part * third, 16), third)
        arrive(wout_ref.at[rows], 154 + part)
    for copy in sent:
        copy.wait_send()
    for index in range(qkv_ref.shape[1] // D):
        qkv_ref[:, index * D : (index + 1) * D] = wout_ref[index * D : (index + 1) * D, :].astype(jnp.float32)
    start = qkv_ref.shape[1]
    proj_ref[...] = wout_ref[start : start + D, :].astype(jnp.float32)
    start += D
    for index in range(up_ref.shape[1] // D):
        rows = pl.ds(start + index * D, D)
        up_ref[:, index * D : (index + 1) * D] = wout_ref[rows, :].astype(jnp.float32)
    start += up_ref.shape[1]
    down_ref[...] = wout_ref[start:, :].astype(jnp.float32)


def reduce_everywhere(rows, gains, shapes):
    total_rows, width = rows.shape
    parts = len(AXIS_ORDERS)
    third = total_rows // 2 // parts
    sizes = [third // 4, third // 16, third // 64]
    scratch = [
        pltpu.VMEM((total_rows, width), jnp.bfloat16),
        pltpu.VMEM((total_rows // 2, width), jnp.bfloat16),
        pltpu.VMEM((total_rows // 2, width), jnp.bfloat16),
        pltpu.VMEM(gains.shape, jnp.bfloat16),
        pltpu.VMEM(gains.shape, jnp.bfloat16),
    ]
    for part in range(parts):
        for size in sizes:
            scratch += [
                pltpu.VMEM((4, size, width), jnp.bfloat16),
                pltpu.VMEM((4, size, width), jnp.bfloat16),
                pltpu.VMEM((size, width), jnp.float32),
            ]
    for part in range(parts):
        for size in reversed(sizes):
            scratch.append(pltpu.VMEM((4, size, width), jnp.bfloat16))
    scratch += [
        pltpu.VMEM((3,) + gains.shape, jnp.bfloat16),
        pltpu.VMEM((3, 4) + gains.shape, jnp.bfloat16),
        pltpu.SemaphoreType.DMA((160,)),
        pltpu.SemaphoreType.DMA((160,)),
    ]
    results = pl.pallas_call(
        reduce_kernel,
        out_shape=tuple(jax.ShapeDtypeStruct(shape, jnp.float32) for shape in shapes)
        + (jax.ShapeDtypeStruct(gains.shape, jnp.float32),),
        in_specs=[pl.BlockSpec(memory_space=pltpu.VMEM)] * 2,
        out_specs=tuple(pl.BlockSpec(memory_space=pltpu.VMEM) for _ in range(len(shapes) + 1)),
        scratch_shapes=scratch,
        compiler_params=pltpu.CompilerParams(
            collective_id=0, has_side_effects=True, vmem_limit_bytes=60 * 1024 * 1024
        ),
    )(rows, gains)
    return results

def on_device(
    features, curve_pos, pattern, ln1_gain, w_qkv, w_out, ln2_gain, w_up, w_down, out_grad
):
    seq_devices = lax.axis_size("seq")
    seq_index = lax.axis_index("seq")
    dev_rows = features.shape[1]
    capacity = 2 * dev_rows // seq_devices
    blocks_dev = dev_rows // BLK
    position = curve_pos[0]
    send_index, source_for_slot = node_plan(position, seq_index, dev_rows, capacity, seq_devices)
    outgoing = jnp.zeros((seq_devices * capacity, D), jnp.bfloat16).at[send_index].set(features[0])
    arrived = lax.all_to_all(
        outgoing.reshape(seq_devices, capacity, D), "seq", split_axis=0, concat_axis=0, tiled=True
    )
    curve_rows = arrived.reshape(seq_devices * capacity, D)[source_for_slot]
    normed_a, normed1, inverse1 = layer_norm(curve_rows, ln1_gain)
    qkv = jnp.dot(normed_a, w_qkv, preferred_element_type=jnp.float32).astype(jnp.bfloat16)
    queries = qkv[:, :D]
    keyval = qkv[:, D:]
    distances = shift_distances(seq_devices)
    pieces = [keyval]
    for distance in distances:
        pieces.append(from_behind(keyval, "seq", distance))
    keyval_all = jnp.concatenate(pieces, axis=0)
    source_dev = jnp.stack(
        [seq_index] + [(seq_index - distance) % seq_devices for distance in distances]
    )
    key_blocks = (
        source_dev[:, None] * blocks_dev + jnp.arange(blocks_dev, dtype=jnp.int32)[None, :]
    ).reshape(-1)
    own_lists = lax.dynamic_slice_in_dim(pattern[0], seq_index * blocks_dev, blocks_dev, axis=0)
    matches = (own_lists[:, :, None] == key_blocks[None, None, :]).astype(jnp.int32)
    selected = jnp.sum(
        matches * jnp.arange(key_blocks.shape[0], dtype=jnp.int32)[None, None, :], axis=-1
    )
    attn_out, log_totals = attention_forward(queries, keyval_all, selected)
    hidden_res = (
        curve_rows.astype(jnp.float32)
        + jnp.dot(attn_out, w_out, preferred_element_type=jnp.float32)
    ).astype(jnp.bfloat16)
    normed_b, normed2, inverse2 = layer_norm(hidden_res, ln2_gain)
    pre_act = jnp.dot(normed_b, w_up, preferred_element_type=jnp.float32)
    activated = jax.nn.gelu(pre_act, approximate=True).astype(jnp.bfloat16)
    curve_out = (
        hidden_res.astype(jnp.float32)
        + jnp.dot(activated, w_down, preferred_element_type=jnp.float32)
    ).astype(jnp.bfloat16)
    leaving = (
        jnp.zeros((seq_devices * capacity, D), jnp.bfloat16).at[source_for_slot].set(curve_out)
    )
    returned = lax.all_to_all(
        leaving.reshape(seq_devices, capacity, D), "seq", split_axis=0, concat_axis=0, tiled=True
    )
    block_out = returned.reshape(seq_devices * capacity, D)[send_index]
    grad_outgoing = (
        jnp.zeros((seq_devices * capacity, D), jnp.bfloat16).at[send_index].set(out_grad[0])
    )
    grad_arrived = lax.all_to_all(
        grad_outgoing.reshape(seq_devices, capacity, D),
        "seq",
        split_axis=0,
        concat_axis=0,
        tiled=True,
    )
    grad_curve = grad_arrived.reshape(seq_devices * capacity, D)[source_for_slot]
    grad_pre = gelu_back(pre_act, times_transposed(grad_curve, w_down)).astype(jnp.bfloat16)
    grad_down = inner_rows(activated, grad_curve)
    grad_normed_b = times_transposed(grad_pre, w_up)
    grad_up_blocks = [
        inner_rows(normed_b, grad_pre[:, index * D : (index + 1) * D])
        for index in range(grad_pre.shape[1] // D)
    ]
    grad_gain2 = jnp.sum(grad_normed_b * normed2, axis=0)
    grad_hidden = (
        grad_curve.astype(jnp.float32) + norm_back(grad_normed_b, ln2_gain, normed2, inverse2)
    ).astype(jnp.bfloat16)
    grad_attn = times_transposed(grad_hidden, w_out).astype(jnp.bfloat16)
    grad_out = inner_rows(attn_out, grad_hidden)
    resent = [keyval]
    for distance in distances:
        resent.append(from_behind(keyval, "seq", distance))
    keyval_back = jnp.concatenate(resent, axis=0)
    grad_query, grad_keyval_all = attention_backward(
        queries, keyval_back, selected, attn_out, log_totals, grad_attn
    )
    grad_keyval = grad_keyval_all[:dev_rows]
    for index_pos, distance in enumerate(distances):
        partial_rows = grad_keyval_all[(index_pos + 1) * dev_rows : (index_pos + 2) * dev_rows]
        grad_keyval = grad_keyval + from_behind(
            partial_rows.astype(jnp.bfloat16), "seq", -distance
        ).astype(partial_rows.dtype)
    grad_qkv_rows = jnp.concatenate([grad_query, grad_keyval.astype(jnp.bfloat16)], axis=1)
    grad_normed_a = times_transposed(grad_qkv_rows, w_qkv)
    grad_qkv_blocks = [
        inner_rows(normed_a, grad_qkv_rows[:, index * D : (index + 1) * D])
        for index in range(grad_qkv_rows.shape[1] // D)
    ]
    grad_gain1 = jnp.sum(grad_normed_a * normed1, axis=0)
    grad_curve_in = (
        grad_hidden.astype(jnp.float32) + norm_back(grad_normed_a, ln1_gain, normed1, inverse1)
    ).astype(jnp.bfloat16)
    grad_leaving = (
        jnp.zeros((seq_devices * capacity, D), jnp.bfloat16).at[source_for_slot].set(grad_curve_in)
    )
    grad_returned = lax.all_to_all(
        grad_leaving.reshape(seq_devices, capacity, D),
        "seq",
        split_axis=0,
        concat_axis=0,
        tiled=True,
    )
    input_grad = grad_returned.reshape(seq_devices * capacity, D)[send_index]
    weight_rows = jnp.concatenate(
        grad_qkv_blocks + [grad_out] + grad_up_blocks + [grad_down],
        axis=0,
    )
    gain_rows = jnp.zeros((8, D), jnp.float32).at[0].set(grad_gain1).at[1].set(grad_gain2)
    grad_qkv, grad_out, grad_up, grad_down, gain_rows = reduce_everywhere(
        weight_rows,
        gain_rows,
        [(D, 3 * D), (D, D), (D, grad_pre.shape[1]), (grad_pre.shape[1], D)],
    )
    grad_gain1 = gain_rows[0]
    grad_gain2 = gain_rows[1]
    return (
        block_out[None],
        input_grad[None],
        grad_qkv,
        grad_out,
        grad_up,
        grad_down,
        grad_gain1,
        grad_gain2,
    )


def solution(mesh):
    return jax.shard_map(
        on_device,
        mesh=mesh,
        in_specs=(
            P("dp", "seq", None),
            P("dp", None),
            P("dp", None, None),
            P(),
            P(),
            P(),
            P(),
            P(),
            P(),
            P("dp", "seq", None),
        ),
        out_specs=(P("dp", "seq", None), P("dp", "seq", None), P(), P(), P(), P(), P(), P()),
        check_vma=False,
    )
```

```python
from functools import partial

import jax
import jax.numpy as jnp
from jax import lax
from jax.experimental import pallas as pl
from jax.experimental.pallas import tpu as pltpu
from jax.sharding import PartitionSpec as P

D = 512
HEADS = 8
BLK = 128


EPSILON = 1e-05


def from_behind(x, axis, by):
    length = lax.axis_size(axis)
    return lax.ppermute(x, axis, [(i, (i + by) % length) for i in range(length)])


def layer_norm(rows_in, gain_vec):
    values = rows_in.astype(jnp.float32)
    centered = values - jnp.mean(values, axis=-1, keepdims=True)
    inverse = lax.rsqrt(jnp.mean(centered * centered, axis=-1, keepdims=True) + EPSILON)
    normed = centered * inverse
    return ((normed * gain_vec).astype(jnp.bfloat16), normed, inverse)


def norm_back(incoming, gain_vec, normed, inverse):
    scaled = incoming * gain_vec
    return inverse * (
        scaled
        - jnp.mean(scaled, axis=-1, keepdims=True)
        - normed * jnp.mean(scaled * normed, axis=-1, keepdims=True)
    )


def gelu_back(pre_act, incoming):
    return jax.vjp(partial(jax.nn.gelu, approximate=True), pre_act)[1](incoming)[0]


def inner_rows(left_mat, right_mat):
    return lax.dot_general(
        left_mat, right_mat, (((0,), (0,)), ((), ())), preferred_element_type=jnp.float32
    )


def times_transposed(left_mat, right_mat):
    return lax.dot_general(
        left_mat, right_mat, (((1,), (1,)), ((), ())), preferred_element_type=jnp.float32
    )


def split_heads(rows_in):
    return rows_in.reshape(rows_in.shape[0] // BLK, BLK, HEADS, D // HEADS)


def listed_heads(keyval_all, selected):
    blocks = keyval_all.reshape(keyval_all.shape[0] // BLK, BLK, 2 * D)
    picked = blocks[selected]
    shape_out = picked.shape[:3] + (HEADS, D // HEADS)
    return (picked[..., :D].reshape(shape_out), picked[..., D:].reshape(shape_out))


def shift_distances(seq_devices):
    levels = seq_devices.bit_length() - 1
    distances = []
    for level_idx in range(levels):
        stride = 2**level_idx
        if 2 * stride == seq_devices:
            distances.append(stride)
        else:
            distances.extend([stride, -stride])
    return distances


def node_plan(position, seq_index, dev_rows, capacity, seq_devices):
    own_position = lax.dynamic_slice_in_dim(position, seq_index * dev_rows, dev_rows)
    target_dev = own_position // dev_rows
    dest_hits = (target_dev[:, None] == jnp.arange(seq_devices, dtype=jnp.int32)[None, :]).astype(
        jnp.int32
    )
    send_rank = jnp.sum((jnp.cumsum(dest_hits, axis=0) - dest_hits) * dest_hits, axis=1)
    send_index = target_dev * capacity + send_rank
    layout = position.reshape(seq_devices, dev_rows)
    arriving = (layout // dev_rows == seq_index).astype(jnp.int32)
    arrive_rank = jnp.cumsum(arriving, axis=1) - arriving
    source_index = jnp.arange(seq_devices, dtype=jnp.int32)[:, None] * capacity + arrive_rank
    del source_index
    total = position.shape[0]
    wanted = seq_index * dev_rows + jnp.arange(dev_rows, dtype=jnp.int32)
    slot_node = jnp.sum(
        jnp.where(
            position[None, :] == wanted[:, None], jnp.arange(total, dtype=jnp.int32)[None, :], 0
        ),
        axis=1,
    )
    source_for_slot = (slot_node // dev_rows) * capacity + arrive_rank.reshape(-1)[slot_node]
    return (send_index, source_for_slot)


def attention_forward(queries, keyval_all, selected):
    query_heads = split_heads(queries)
    key_heads, value_heads = listed_heads(keyval_all, selected)
    scores = (
        jnp.einsum("aihd,akjhd->haikj", query_heads, key_heads, preferred_element_type=jnp.float32)
        * 0.125
    )
    largest = jnp.max(scores, axis=(3, 4), keepdims=True)
    totals = jnp.sum(jnp.exp(scores - largest), axis=(3, 4), keepdims=True)
    log_totals = largest + jnp.log(totals)
    attn_probs = jnp.exp(scores - log_totals).astype(jnp.bfloat16)
    result = jnp.einsum(
        "haikj,akjhd->aihd", attn_probs, value_heads, preferred_element_type=jnp.float32
    )
    return (result.astype(jnp.bfloat16).reshape(queries.shape[0], D), log_totals)


def attention_backward(queries, keyval_all, selected, attn_out, log_totals, grad_attn):
    query_heads = split_heads(queries)
    key_heads, value_heads = listed_heads(keyval_all, selected)
    out_heads = split_heads(attn_out)
    grad_heads = split_heads(grad_attn)
    scores = (
        jnp.einsum("aihd,akjhd->haikj", query_heads, key_heads, preferred_element_type=jnp.float32)
        * 0.125
    )
    attn_exact = jnp.exp(scores - log_totals)
    attn_probs = attn_exact.astype(jnp.bfloat16)
    grad_probs = jnp.einsum(
        "aihd,akjhd->haikj", grad_heads, value_heads, preferred_element_type=jnp.float32
    )
    row_dots = jnp.einsum(
        "aihd,aihd->hai", grad_heads, out_heads, preferred_element_type=jnp.float32
    )[..., None, None]
    grad_scores = (attn_exact * (grad_probs - row_dots) * 0.125).astype(jnp.bfloat16)
    grad_query = jnp.einsum(
        "haikj,akjhd->aihd", grad_scores, key_heads, preferred_element_type=jnp.float32
    )
    grad_keys = jnp.einsum(
        "haikj,aihd->akjhd", grad_scores, query_heads, preferred_element_type=jnp.float32
    )
    grad_values = jnp.einsum(
        "haikj,aihd->akjhd", attn_probs, grad_heads, preferred_element_type=jnp.float32
    )
    block_shape = grad_keys.shape[:3] + (D,)
    grad_picked = jnp.concatenate(
        [grad_keys.reshape(block_shape), grad_values.reshape(block_shape)], axis=-1
    )
    total_rows = keyval_all.shape[0]
    one_hot = (
        selected[:, :, None] == jnp.arange(total_rows // BLK, dtype=jnp.int32)[None, None, :]
    ).astype(jnp.float32)
    grad_keyval = jnp.einsum(
        "akb,akjc->bjc",
        one_hot,
        grad_picked,
        precision=lax.Precision.HIGHEST,
        preferred_element_type=jnp.float32,
    )
    return (
        grad_query.astype(jnp.bfloat16).reshape(queries.shape[0], D),
        grad_keyval.reshape(total_rows, 2 * D),
    )


MESH_IDS = pl.DeviceIdType.MESH
RING_KINDS = ("x", "y", "z")
AXIS_ORDERS = (("x", "y", "z"), ("y", "z", "x"), ("z", "x", "y"))


def reduce_kernel(
    w_ref, g_ref, qkv_ref, proj_ref, up_ref, down_ref, gout_ref, wout_ref, send0, recv0, gsend0, grecv0, *rest
):
    parts = len(AXIS_ORDERS)
    ring_bufs = [[rest[9 * p + 3 * s : 9 * p + 3 * s + 3] for s in range(3)] for p in range(parts)]
    gather_bufs = [rest[9 * parts + 3 * p : 9 * parts + 3 * p + 3] for p in range(parts)]
    gsend, grecv, send_sem, recv_sem = rest[12 * parts :]
    seq = lax.axis_index("seq")
    dp = lax.axis_index("dp")
    core = seq % 2
    place = {"x": (seq // 2) % 4, "y": seq // 8, "z": dp}

    def peer(kind, member):
        if kind == "core":
            return (seq + 1 - 2 * core, dp)
        if kind == "x":
            return (seq + (member - place["x"]) * 2, dp)
        if kind == "y":
            return (seq + (member - place["y"]) * 8, dp)
        return (seq, member)

    barrier = pltpu.get_barrier_semaphore()
    peers = [peer("core", 0)]
    for kind in RING_KINDS:
        for shift in (1, 2, 3):
            peers.append(peer(kind, (place[kind] + shift) % 4))
    for target in peers:
        pl.semaphore_signal(barrier, inc=1, device_id=target, device_id_type=MESH_IDS)
    pl.semaphore_wait(barrier, len(peers))

    counter = [0]
    sent = []

    def send(src, dst, recv_index, target):
        copy = pltpu.make_async_remote_copy(
            src_ref=src,
            dst_ref=dst,
            send_sem=send_sem.at[counter[0]],
            recv_sem=recv_sem.at[recv_index],
            device_id=target,
            device_id_type=MESH_IDS,
        )
        counter[0] += 1
        copy.start()
        sent.append(copy)

    def arrive(dst, recv_index):
        pltpu.make_async_remote_copy(
            src_ref=dst,
            dst_ref=dst,
            send_sem=send_sem.at[0],
            recv_sem=recv_sem.at[recv_index],
            device_id=peers[0],
            device_id_type=MESH_IDS,
        ).wait_recv()

    half = send0.shape[0]
    third = half // parts
    gsend0[...] = g_ref[...].astype(jnp.bfloat16)
    send(gsend0, grecv0, 1, peers[0])
    for part in range(parts):
        rows = pl.ds(pl.multiple_of(part * third, 16), third)
        source_rows = pl.ds(pl.multiple_of((1 - core) * half + part * third, 16), third)
        send0[rows, :] = w_ref[source_rows, :].astype(jnp.bfloat16)
        send(send0.at[rows], recv0.at[rows], 150 + part, peers[0])
    arrive(grecv0, 1)
    gains = gsend0[...].astype(jnp.float32) + grecv0[...].astype(jnp.float32)

    def first_chunk(part, member, size):
        offset = part * third + member * size
        mine = w_ref[pl.ds(pl.multiple_of(core * half + offset, 16), size), :]
        return mine + recv0[pl.ds(pl.multiple_of(offset, 16), size), :].astype(jnp.float32)

    sources = [None] * parts
    def ring_send_step(stage, part, gains):
            kind = AXIS_ORDERS[part][stage]
            sbuf, rbuf, total = ring_bufs[part][stage]
            size = sbuf.shape[1]
            pos = place[kind]
            base = 2 + 12 * (3 * part + stage)
            source = sources[part]

            def chunk(member, source=source, size=size, part=part):
                if source is None:
                    return first_chunk(part, member, size)
                return source[pl.ds(pl.multiple_of(member * size, 16), size), :]

            if stage == 0:
                arrive(recv0.at[pl.ds(pl.multiple_of(part * third, 16), third)], 150 + part)
            if part == 0:
                gsend[stage] = gains.astype(jnp.bfloat16)
                grecv[stage, pos] = gsend[stage]
            for shift in (1, 2, 3):
                member = (pos + shift) % 4
                sbuf[member] = chunk(member).astype(jnp.bfloat16)
                send(sbuf.at[member], rbuf.at[pos], base + pos, peer(kind, member))
                if part == 0:
                    send(gsend.at[stage], grecv.at[stage, pos], base + 4 + pos, peer(kind, member))
            total[...] = chunk(pos)
            return gains

    def ring_wait_step(stage, part, gains):
            kind = AXIS_ORDERS[part][stage]
            sbuf, rbuf, total = ring_bufs[part][stage]
            pos = place[kind]
            base = 2 + 12 * (3 * part + stage)
            for shift in (1, 2, 3):
                slot = (pos - shift) % 4
                arrive(rbuf.at[slot], base + slot)
                total[...] += rbuf[slot].astype(jnp.float32)
                if part == 0:
                    arrive(grecv.at[stage, slot], base + 4 + slot)
            if part == 0:
                got = grecv[stage].astype(jnp.float32)
                gains = (got[0] + got[1]) + (got[2] + got[3])
            sources[part] = total
            return gains

    for part in range(parts):
        gains = ring_send_step(0, part, gains)
    for stage in range(3):
        for part in range(parts):
            gains = ring_wait_step(stage, part, gains)
            if stage < 2:
                gains = ring_send_step(stage + 1, part, gains)
    gout_ref[...] = gains

    owns = [sources[part][...].astype(jnp.bfloat16) for part in range(parts)]

    def gather_send_step(stage, part):
        kind = AXIS_ORDERS[part][2 - stage]
        gathered = gather_bufs[part][stage]
        pos = place[kind]
        base = 2 + 12 * 9 + 4 * (3 * part + stage)
        gathered[pos] = owns[part]
        for shift in (1, 2, 3):
            member = (pos + shift) % 4
            send(gathered.at[pos], gathered.at[pos], base + pos, peer(kind, member))

    def gather_wait_step(stage, part):
        kind = AXIS_ORDERS[part][2 - stage]
        gathered = gather_bufs[part][stage]
        pos = place[kind]
        base = 2 + 12 * 9 + 4 * (3 * part + stage)
        for shift in (1, 2, 3):
            arrive(gathered.at[(pos - shift) % 4], base + (pos - shift) % 4)
        owns[part] = gathered[...].reshape(4 * gathered.shape[1], gathered.shape[2])

    for part in range(parts):
        gather_send_step(0, part)
    for stage in range(3):
        for part in range(parts):
            gather_wait_step(stage, part)
            if stage < 2:
                gather_send_step(stage + 1, part)
            else:
                rows = pl.ds(pl.multiple_of(core * half + part * third, 16), third)
                wout_ref[rows, :] = owns[part]
                send(wout_ref.at[rows], wout_ref.at[rows], 154 + part, peers[0])
    for part in range(parts):
        rows = pl.ds(pl.multiple_of((1 - core) * half + part * third, 16), third)
        arrive(wout_ref.at[rows], 154 + part)
    for copy in sent:
        copy.wait_send()
    for index in range(qkv_ref.shape[1] // D):
        qkv_ref[:, index * D : (index + 1) * D] = wout_ref[index * D : (index + 1) * D, :]
    start = qkv_ref.shape[1]
    proj_ref[...] = wout_ref[start : start + D, :]
    start += D
    for index in range(up_ref.shape[1] // D):
        rows = pl.ds(start + index * D, D)
        up_ref[:, index * D : (index + 1) * D] = wout_ref[rows, :]
    start += up_ref.shape[1]
    down_ref[...] = wout_ref[start:, :]


def reduce_everywhere(rows, gains, shapes):
    total_rows, width = rows.shape
    parts = len(AXIS_ORDERS)
    third = total_rows // 2 // parts
    sizes = [third // 4, third // 16, third // 64]
    scratch = [
        pltpu.VMEM((total_rows, width), jnp.bfloat16),
        pltpu.VMEM((total_rows // 2, width), jnp.bfloat16),
        pltpu.VMEM((total_rows // 2, width), jnp.bfloat16),
        pltpu.VMEM(gains.shape, jnp.bfloat16),
        pltpu.VMEM(gains.shape, jnp.bfloat16),
    ]
    for part in range(parts):
        for size in sizes:
            scratch += [
                pltpu.VMEM((4, size, width), jnp.bfloat16),
                pltpu.VMEM((4, size, width), jnp.bfloat16),
                pltpu.VMEM((size, width), jnp.float32),
            ]
    for part in range(parts):
        for size in reversed(sizes):
            scratch.append(pltpu.VMEM((4, size, width), jnp.bfloat16))
    scratch += [
        pltpu.VMEM((3,) + gains.shape, jnp.bfloat16),
        pltpu.VMEM((3, 4) + gains.shape, jnp.bfloat16),
        pltpu.SemaphoreType.DMA((160,)),
        pltpu.SemaphoreType.DMA((160,)),
    ]
    results = pl.pallas_call(
        reduce_kernel,
        out_shape=tuple(jax.ShapeDtypeStruct(shape, jnp.bfloat16) for shape in shapes)
        + (jax.ShapeDtypeStruct(gains.shape, jnp.float32),),
        in_specs=[pl.BlockSpec(memory_space=pltpu.VMEM)] * 2,
        out_specs=tuple(pl.BlockSpec(memory_space=pltpu.VMEM) for _ in range(len(shapes) + 1)),
        scratch_shapes=scratch,
        compiler_params=pltpu.CompilerParams(
            collective_id=0, has_side_effects=True, vmem_limit_bytes=60 * 1024 * 1024
        ),
    )(rows, gains)
    return tuple(result.astype(jnp.float32) for result in results)

def on_device(
    features, curve_pos, pattern, ln1_gain, w_qkv, w_out, ln2_gain, w_up, w_down, out_grad
):
    seq_devices = lax.axis_size("seq")
    seq_index = lax.axis_index("seq")
    dev_rows = features.shape[1]
    capacity = 2 * dev_rows // seq_devices
    blocks_dev = dev_rows // BLK
    position = curve_pos[0]
    send_index, source_for_slot = node_plan(position, seq_index, dev_rows, capacity, seq_devices)
    outgoing = jnp.zeros((seq_devices * capacity, D), jnp.bfloat16).at[send_index].set(features[0])
    arrived = lax.all_to_all(
        outgoing.reshape(seq_devices, capacity, D), "seq", split_axis=0, concat_axis=0, tiled=True
    )
    curve_rows = arrived.reshape(seq_devices * capacity, D)[source_for_slot]
    normed_a, normed1, inverse1 = layer_norm(curve_rows, ln1_gain)
    qkv = jnp.dot(normed_a, w_qkv, preferred_element_type=jnp.float32).astype(jnp.bfloat16)
    queries = qkv[:, :D]
    keyval = qkv[:, D:]
    distances = shift_distances(seq_devices)
    pieces = [keyval]
    for distance in distances:
        pieces.append(from_behind(keyval, "seq", distance))
    keyval_all = jnp.concatenate(pieces, axis=0)
    source_dev = jnp.stack(
        [seq_index] + [(seq_index - distance) % seq_devices for distance in distances]
    )
    key_blocks = (
        source_dev[:, None] * blocks_dev + jnp.arange(blocks_dev, dtype=jnp.int32)[None, :]
    ).reshape(-1)
    own_lists = lax.dynamic_slice_in_dim(pattern[0], seq_index * blocks_dev, blocks_dev, axis=0)
    matches = (own_lists[:, :, None] == key_blocks[None, None, :]).astype(jnp.int32)
    selected = jnp.sum(
        matches * jnp.arange(key_blocks.shape[0], dtype=jnp.int32)[None, None, :], axis=-1
    )
    attn_out, log_totals = attention_forward(queries, keyval_all, selected)
    hidden_res = (
        curve_rows.astype(jnp.float32)
        + jnp.dot(attn_out, w_out, preferred_element_type=jnp.float32)
    ).astype(jnp.bfloat16)
    normed_b, normed2, inverse2 = layer_norm(hidden_res, ln2_gain)
    pre_act = jnp.dot(normed_b, w_up, preferred_element_type=jnp.float32)
    activated = jax.nn.gelu(pre_act, approximate=True).astype(jnp.bfloat16)
    curve_out = (
        hidden_res.astype(jnp.float32)
        + jnp.dot(activated, w_down, preferred_element_type=jnp.float32)
    ).astype(jnp.bfloat16)
    leaving = (
        jnp.zeros((seq_devices * capacity, D), jnp.bfloat16).at[source_for_slot].set(curve_out)
    )
    returned = lax.all_to_all(
        leaving.reshape(seq_devices, capacity, D), "seq", split_axis=0, concat_axis=0, tiled=True
    )
    block_out = returned.reshape(seq_devices * capacity, D)[send_index]
    grad_outgoing = (
        jnp.zeros((seq_devices * capacity, D), jnp.bfloat16).at[send_index].set(out_grad[0])
    )
    grad_arrived = lax.all_to_all(
        grad_outgoing.reshape(seq_devices, capacity, D),
        "seq",
        split_axis=0,
        concat_axis=0,
        tiled=True,
    )
    grad_curve = grad_arrived.reshape(seq_devices * capacity, D)[source_for_slot]
    grad_pre = gelu_back(pre_act, times_transposed(grad_curve, w_down)).astype(jnp.bfloat16)
    grad_down = inner_rows(activated, grad_curve)
    grad_normed_b = times_transposed(grad_pre, w_up)
    grad_up_blocks = [
        inner_rows(normed_b, grad_pre[:, index * D : (index + 1) * D])
        for index in range(grad_pre.shape[1] // D)
    ]
    grad_gain2 = jnp.sum(grad_normed_b * normed2, axis=0)
    grad_hidden = (
        grad_curve.astype(jnp.float32) + norm_back(grad_normed_b, ln2_gain, normed2, inverse2)
    ).astype(jnp.bfloat16)
    grad_attn = times_transposed(grad_hidden, w_out).astype(jnp.bfloat16)
    grad_out = inner_rows(attn_out, grad_hidden)
    resent = [keyval]
    for distance in distances:
        resent.append(from_behind(keyval, "seq", distance))
    keyval_back = jnp.concatenate(resent, axis=0)
    grad_query, grad_keyval_all = attention_backward(
        queries, keyval_back, selected, attn_out, log_totals, grad_attn
    )
    grad_keyval = grad_keyval_all[:dev_rows]
    for index_pos, distance in enumerate(distances):
        partial_rows = grad_keyval_all[(index_pos + 1) * dev_rows : (index_pos + 2) * dev_rows]
        grad_keyval = grad_keyval + from_behind(
            partial_rows.astype(jnp.bfloat16), "seq", -distance
        ).astype(partial_rows.dtype)
    grad_qkv_rows = jnp.concatenate([grad_query, grad_keyval.astype(jnp.bfloat16)], axis=1)
    grad_normed_a = times_transposed(grad_qkv_rows, w_qkv)
    grad_qkv_blocks = [
        inner_rows(normed_a, grad_qkv_rows[:, index * D : (index + 1) * D])
        for index in range(grad_qkv_rows.shape[1] // D)
    ]
    grad_gain1 = jnp.sum(grad_normed_a * normed1, axis=0)
    grad_curve_in = (
        grad_hidden.astype(jnp.float32) + norm_back(grad_normed_a, ln1_gain, normed1, inverse1)
    ).astype(jnp.bfloat16)
    grad_leaving = (
        jnp.zeros((seq_devices * capacity, D), jnp.bfloat16).at[source_for_slot].set(grad_curve_in)
    )
    grad_returned = lax.all_to_all(
        grad_leaving.reshape(seq_devices, capacity, D),
        "seq",
        split_axis=0,
        concat_axis=0,
        tiled=True,
    )
    input_grad = grad_returned.reshape(seq_devices * capacity, D)[send_index]
    weight_rows = jnp.concatenate(
        grad_qkv_blocks + [grad_out] + grad_up_blocks + [grad_down],
        axis=0,
    )
    gain_rows = jnp.zeros((8, D), jnp.float32).at[0].set(grad_gain1).at[1].set(grad_gain2)
    grad_qkv, grad_out, grad_up, grad_down, gain_rows = reduce_everywhere(
        weight_rows,
        gain_rows,
        [(D, 3 * D), (D, D), (D, grad_pre.shape[1]), (grad_pre.shape[1], D)],
    )
    grad_gain1 = gain_rows[0]
    grad_gain2 = gain_rows[1]
    return (
        block_out[None],
        input_grad[None],
        grad_qkv,
        grad_out,
        grad_up,
        grad_down,
        grad_gain1,
        grad_gain2,
    )


def solution(mesh):
    return jax.shard_map(
        on_device,
        mesh=mesh,
        in_specs=(
            P("dp", "seq", None),
            P("dp", None),
            P("dp", None, None),
            P(),
            P(),
            P(),
            P(),
            P(),
            P(),
            P("dp", "seq", None),
        ),
        out_specs=(P("dp", "seq", None), P("dp", "seq", None), P(), P(), P(), P(), P(), P()),
        check_vma=False,
    )
```

```python
from functools import partial

import jax
import jax.numpy as jnp
from jax import lax
from jax.experimental import pallas as pl
from jax.experimental.pallas import tpu as pltpu
from jax.sharding import PartitionSpec as P

D = 512
HEADS = 8
BLK = 128


EPSILON = 1e-05


def from_behind(x, axis, by):
    length = lax.axis_size(axis)
    return lax.ppermute(x, axis, [(i, (i + by) % length) for i in range(length)])


def layer_norm(rows_in, gain_vec):
    values = rows_in.astype(jnp.float32)
    centered = values - jnp.mean(values, axis=-1, keepdims=True)
    inverse = lax.rsqrt(jnp.mean(centered * centered, axis=-1, keepdims=True) + EPSILON)
    normed = centered * inverse
    return ((normed * gain_vec).astype(jnp.bfloat16), normed, inverse)


def norm_back(incoming, gain_vec, normed, inverse):
    scaled = incoming * gain_vec
    return inverse * (
        scaled
        - jnp.mean(scaled, axis=-1, keepdims=True)
        - normed * jnp.mean(scaled * normed, axis=-1, keepdims=True)
    )


def gelu_back(pre_act, incoming):
    return jax.vjp(partial(jax.nn.gelu, approximate=True), pre_act)[1](incoming)[0]


def inner_rows(left_mat, right_mat):
    return lax.dot_general(
        left_mat, right_mat, (((0,), (0,)), ((), ())), preferred_element_type=jnp.float32
    )


def times_transposed(left_mat, right_mat):
    return lax.dot_general(
        left_mat, right_mat, (((1,), (1,)), ((), ())), preferred_element_type=jnp.float32
    )


def split_heads(rows_in):
    return rows_in.reshape(rows_in.shape[0] // BLK, BLK, HEADS, D // HEADS)


def listed_heads(keyval_all, selected):
    blocks = keyval_all.reshape(keyval_all.shape[0] // BLK, BLK, 2 * D)
    picked = blocks[selected]
    shape_out = picked.shape[:3] + (HEADS, D // HEADS)
    return (picked[..., :D].reshape(shape_out), picked[..., D:].reshape(shape_out))


def shift_distances(seq_devices):
    levels = seq_devices.bit_length() - 1
    distances = []
    for level_idx in range(levels):
        stride = 2**level_idx
        if 2 * stride == seq_devices:
            distances.append(stride)
        else:
            distances.extend([stride, -stride])
    return distances


def node_plan(position, seq_index, dev_rows, capacity, seq_devices):
    own_position = lax.dynamic_slice_in_dim(position, seq_index * dev_rows, dev_rows)
    target_dev = own_position // dev_rows
    dest_hits = (target_dev[:, None] == jnp.arange(seq_devices, dtype=jnp.int32)[None, :]).astype(
        jnp.int32
    )
    send_rank = jnp.sum((jnp.cumsum(dest_hits, axis=0) - dest_hits) * dest_hits, axis=1)
    send_index = target_dev * capacity + send_rank
    layout = position.reshape(seq_devices, dev_rows)
    arriving = (layout // dev_rows == seq_index).astype(jnp.int32)
    arrive_rank = jnp.cumsum(arriving, axis=1) - arriving
    source_index = jnp.arange(seq_devices, dtype=jnp.int32)[:, None] * capacity + arrive_rank
    del source_index
    total = position.shape[0]
    wanted = seq_index * dev_rows + jnp.arange(dev_rows, dtype=jnp.int32)
    slot_node = jnp.sum(
        jnp.where(
            position[None, :] == wanted[:, None], jnp.arange(total, dtype=jnp.int32)[None, :], 0
        ),
        axis=1,
    )
    source_for_slot = (slot_node // dev_rows) * capacity + arrive_rank.reshape(-1)[slot_node]
    return (send_index, source_for_slot)


def attention_forward(queries, keyval_all, selected):
    query_heads = split_heads(queries)
    key_heads, value_heads = listed_heads(keyval_all, selected)
    scores = (
        jnp.einsum("aihd,akjhd->haikj", query_heads, key_heads, preferred_element_type=jnp.float32)
        * 0.125
    )
    largest = jnp.max(scores, axis=(3, 4), keepdims=True)
    totals = jnp.sum(jnp.exp(scores - largest), axis=(3, 4), keepdims=True)
    log_totals = largest + jnp.log(totals)
    attn_probs = jnp.exp(scores - log_totals).astype(jnp.bfloat16)
    result = jnp.einsum(
        "haikj,akjhd->aihd", attn_probs, value_heads, preferred_element_type=jnp.float32
    )
    return (result.astype(jnp.bfloat16).reshape(queries.shape[0], D), log_totals)


def attention_backward(queries, keyval_all, selected, attn_out, log_totals, grad_attn):
    query_heads = split_heads(queries)
    key_heads, value_heads = listed_heads(keyval_all, selected)
    out_heads = split_heads(attn_out)
    grad_heads = split_heads(grad_attn)
    scores = (
        jnp.einsum("aihd,akjhd->haikj", query_heads, key_heads, preferred_element_type=jnp.float32)
        * 0.125
    )
    attn_exact = jnp.exp(scores - log_totals)
    attn_probs = attn_exact.astype(jnp.bfloat16)
    grad_probs = jnp.einsum(
        "aihd,akjhd->haikj", grad_heads, value_heads, preferred_element_type=jnp.float32
    )
    row_dots = jnp.einsum(
        "aihd,aihd->hai", grad_heads, out_heads, preferred_element_type=jnp.float32
    )[..., None, None]
    grad_scores = (attn_exact * (grad_probs - row_dots) * 0.125).astype(jnp.bfloat16)
    grad_query = jnp.einsum(
        "haikj,akjhd->aihd", grad_scores, key_heads, preferred_element_type=jnp.float32
    )
    grad_keys = jnp.einsum(
        "haikj,aihd->akjhd", grad_scores, query_heads, preferred_element_type=jnp.float32
    )
    grad_values = jnp.einsum(
        "haikj,aihd->akjhd", attn_probs, grad_heads, preferred_element_type=jnp.float32
    )
    block_shape = grad_keys.shape[:3] + (D,)
    grad_picked = jnp.concatenate(
        [grad_keys.reshape(block_shape), grad_values.reshape(block_shape)], axis=-1
    )
    total_rows = keyval_all.shape[0]
    one_hot = (
        selected[:, :, None] == jnp.arange(total_rows // BLK, dtype=jnp.int32)[None, None, :]
    ).astype(jnp.float32)
    grad_keyval = jnp.einsum(
        "akb,akjc->bjc",
        one_hot,
        grad_picked,
        precision=lax.Precision.HIGHEST,
        preferred_element_type=jnp.float32,
    )
    return (
        grad_query.astype(jnp.bfloat16).reshape(queries.shape[0], D),
        grad_keyval.reshape(total_rows, 2 * D),
    )


MESH_IDS = pl.DeviceIdType.MESH
RING_KINDS = ("x", "y", "z")
AXIS_ORDERS = (("x", "y", "z"), ("y", "z", "x"), ("z", "x", "y"))


def reduce_kernel(
    w_ref, g_ref, qkv_ref, proj_ref, up_ref, down_ref, gout_ref, wout_ref, send0, recv0, gsend0, grecv0, *rest
):
    parts = len(AXIS_ORDERS)
    ring_bufs = [[rest[9 * p + 3 * s : 9 * p + 3 * s + 3] for s in range(3)] for p in range(parts)]
    gather_bufs = [rest[9 * parts + 3 * p : 9 * parts + 3 * p + 3] for p in range(parts)]
    gsend, grecv, send_sem, recv_sem, w_vmem, load_sem = rest[12 * parts :]
    seq = lax.axis_index("seq")
    dp = lax.axis_index("dp")
    core = seq % 2
    place = {"x": (seq // 2) % 4, "y": seq // 8, "z": dp}

    def peer(kind, member):
        if kind == "core":
            return (seq + 1 - 2 * core, dp)
        if kind == "x":
            return (seq + (member - place["x"]) * 2, dp)
        if kind == "y":
            return (seq + (member - place["y"]) * 8, dp)
        return (seq, member)

    barrier = pltpu.get_barrier_semaphore()
    peers = [peer("core", 0)]
    for kind in RING_KINDS:
        for shift in (1, 2, 3):
            peers.append(peer(kind, (place[kind] + shift) % 4))
    for target in peers:
        pl.semaphore_signal(barrier, inc=1, device_id=target, device_id_type=MESH_IDS)
    pl.semaphore_wait(barrier, len(peers))

    counter = [0]
    sent = []

    def send(src, dst, recv_index, target):
        copy = pltpu.make_async_remote_copy(
            src_ref=src,
            dst_ref=dst,
            send_sem=send_sem.at[counter[0]],
            recv_sem=recv_sem.at[recv_index],
            device_id=target,
            device_id_type=MESH_IDS,
        )
        counter[0] += 1
        copy.start()
        sent.append(copy)

    def arrive(dst, recv_index):
        pltpu.make_async_remote_copy(
            src_ref=dst,
            dst_ref=dst,
            send_sem=send_sem.at[0],
            recv_sem=recv_sem.at[recv_index],
            device_id=peers[0],
            device_id_type=MESH_IDS,
        ).wait_recv()

    half = send0.shape[0]
    third = half // parts
    loads = {}
    for side in (1, 0):
        for part in range(parts):
            first = (side * (1 - core) + (1 - side) * core) * half + part * third
            rows = pl.ds(pl.multiple_of(first, 16), third)
            load = pltpu.make_async_copy(w_ref.at[rows], w_vmem.at[rows], load_sem.at[side * parts + part])
            load.start()
            loads[(side, part)] = load
    gsend0[...] = g_ref[...].astype(jnp.bfloat16)
    send(gsend0, grecv0, 1, peers[0])
    for part in range(parts):
        rows = pl.ds(pl.multiple_of(part * third, 16), third)
        source_rows = pl.ds(pl.multiple_of((1 - core) * half + part * third, 16), third)
        loads[(1, part)].wait()
        send0[rows, :] = w_vmem[source_rows, :].astype(jnp.bfloat16)
        send(send0.at[rows], recv0.at[rows], 150 + part, peers[0])
    arrive(grecv0, 1)
    gains = gsend0[...].astype(jnp.float32) + grecv0[...].astype(jnp.float32)

    def first_chunk(part, member, size):
        offset = part * third + member * size
        mine = w_vmem[pl.ds(pl.multiple_of(core * half + offset, 16), size), :]
        return mine + recv0[pl.ds(pl.multiple_of(offset, 16), size), :].astype(jnp.float32)

    sources = [None] * parts
    def ring_send_step(stage, part, gains):
            kind = AXIS_ORDERS[part][stage]
            sbuf, rbuf, total = ring_bufs[part][stage]
            size = sbuf.shape[1]
            pos = place[kind]
            base = 2 + 12 * (3 * part + stage)
            source = sources[part]

            def chunk(member, source=source, size=size, part=part):
                if source is None:
                    return first_chunk(part, member, size)
                return source[pl.ds(pl.multiple_of(member * size, 16), size), :]

            if stage == 0:
                loads[(0, part)].wait()
                arrive(recv0.at[pl.ds(pl.multiple_of(part * third, 16), third)], 150 + part)
            if part == 0:
                gsend[stage] = gains.astype(jnp.bfloat16)
                grecv[stage, pos] = gsend[stage]
            for shift in (1, 2, 3):
                member = (pos + shift) % 4
                sbuf[member] = chunk(member).astype(jnp.bfloat16)
                send(sbuf.at[member], rbuf.at[pos], base + pos, peer(kind, member))
                if part == 0:
                    send(gsend.at[stage], grecv.at[stage, pos], base + 4 + pos, peer(kind, member))
            total[...] = chunk(pos)
            return gains

    def ring_wait_step(stage, part, gains):
            kind = AXIS_ORDERS[part][stage]
            sbuf, rbuf, total = ring_bufs[part][stage]
            pos = place[kind]
            base = 2 + 12 * (3 * part + stage)
            for shift in (1, 2, 3):
                slot = (pos - shift) % 4
                arrive(rbuf.at[slot], base + slot)
                total[...] += rbuf[slot].astype(jnp.float32)
                if part == 0:
                    arrive(grecv.at[stage, slot], base + 4 + slot)
            if part == 0:
                got = grecv[stage].astype(jnp.float32)
                gains = (got[0] + got[1]) + (got[2] + got[3])
            sources[part] = total
            return gains

    for part in range(parts):
        gains = ring_send_step(0, part, gains)
    for stage in range(3):
        for part in range(parts):
            gains = ring_wait_step(stage, part, gains)
            if stage < 2:
                gains = ring_send_step(stage + 1, part, gains)
    gout_ref[...] = gains

    owns = [sources[part][...].astype(jnp.bfloat16) for part in range(parts)]

    def gather_send_step(stage, part):
        kind = AXIS_ORDERS[part][2 - stage]
        gathered = gather_bufs[part][stage]
        pos = place[kind]
        base = 2 + 12 * 9 + 4 * (3 * part + stage)
        gathered[pos] = owns[part]
        for shift in (1, 2, 3):
            member = (pos + shift) % 4
            send(gathered.at[pos], gathered.at[pos], base + pos, peer(kind, member))

    def gather_wait_step(stage, part):
        kind = AXIS_ORDERS[part][2 - stage]
        gathered = gather_bufs[part][stage]
        pos = place[kind]
        base = 2 + 12 * 9 + 4 * (3 * part + stage)
        for shift in (1, 2, 3):
            arrive(gathered.at[(pos - shift) % 4], base + (pos - shift) % 4)
        owns[part] = gathered[...].reshape(4 * gathered.shape[1], gathered.shape[2])

    for part in range(parts):
        gather_send_step(0, part)
    for stage in range(3):
        for part in range(parts):
            gather_wait_step(stage, part)
            if stage < 2:
                gather_send_step(stage + 1, part)
            else:
                rows = pl.ds(pl.multiple_of(core * half + part * third, 16), third)
                wout_ref[rows, :] = owns[part]
                send(wout_ref.at[rows], wout_ref.at[rows], 154 + part, peers[0])
    for part in range(parts):
        rows = pl.ds(pl.multiple_of((1 - core) * half + part * third, 16), third)
        arrive(wout_ref.at[rows], 154 + part)
    for copy in sent:
        copy.wait_send()
    for index in range(qkv_ref.shape[1] // D):
        qkv_ref[:, index * D : (index + 1) * D] = wout_ref[index * D : (index + 1) * D, :]
    start = qkv_ref.shape[1]
    proj_ref[...] = wout_ref[start : start + D, :]
    start += D
    for index in range(up_ref.shape[1] // D):
        rows = pl.ds(start + index * D, D)
        up_ref[:, index * D : (index + 1) * D] = wout_ref[rows, :]
    start += up_ref.shape[1]
    down_ref[...] = wout_ref[start:, :]


def reduce_everywhere(rows, gains, shapes):
    total_rows, width = rows.shape
    parts = len(AXIS_ORDERS)
    third = total_rows // 2 // parts
    sizes = [third // 4, third // 16, third // 64]
    scratch = [
        pltpu.VMEM((total_rows, width), jnp.bfloat16),
        pltpu.VMEM((total_rows // 2, width), jnp.bfloat16),
        pltpu.VMEM((total_rows // 2, width), jnp.bfloat16),
        pltpu.VMEM(gains.shape, jnp.bfloat16),
        pltpu.VMEM(gains.shape, jnp.bfloat16),
    ]
    for part in range(parts):
        for size in sizes:
            scratch += [
                pltpu.VMEM((4, size, width), jnp.bfloat16),
                pltpu.VMEM((4, size, width), jnp.bfloat16),
                pltpu.VMEM((size, width), jnp.float32),
            ]
    for part in range(parts):
        for size in reversed(sizes):
            scratch.append(pltpu.VMEM((4, size, width), jnp.bfloat16))
    scratch += [
        pltpu.VMEM((3,) + gains.shape, jnp.bfloat16),
        pltpu.VMEM((3, 4) + gains.shape, jnp.bfloat16),
        pltpu.SemaphoreType.DMA((160,)),
        pltpu.SemaphoreType.DMA((160,)),
        pltpu.VMEM((total_rows, width), jnp.float32),
        pltpu.SemaphoreType.DMA((2 * parts,)),
    ]
    results = pl.pallas_call(
        reduce_kernel,
        out_shape=tuple(jax.ShapeDtypeStruct(shape, jnp.bfloat16) for shape in shapes)
        + (jax.ShapeDtypeStruct(gains.shape, jnp.float32),),
        in_specs=[pl.BlockSpec(memory_space=pl.ANY), pl.BlockSpec(memory_space=pltpu.VMEM)],
        out_specs=tuple(pl.BlockSpec(memory_space=pltpu.VMEM) for _ in range(len(shapes) + 1)),
        scratch_shapes=scratch,
        compiler_params=pltpu.CompilerParams(
            collective_id=0, has_side_effects=True, vmem_limit_bytes=60 * 1024 * 1024
        ),
    )(rows, gains)
    return tuple(result.astype(jnp.float32) for result in results)

def on_device(
    features, curve_pos, pattern, ln1_gain, w_qkv, w_out, ln2_gain, w_up, w_down, out_grad
):
    seq_devices = lax.axis_size("seq")
    seq_index = lax.axis_index("seq")
    dev_rows = features.shape[1]
    capacity = 2 * dev_rows // seq_devices
    blocks_dev = dev_rows // BLK
    position = curve_pos[0]
    send_index, source_for_slot = node_plan(position, seq_index, dev_rows, capacity, seq_devices)
    outgoing = jnp.zeros((seq_devices * capacity, D), jnp.bfloat16).at[send_index].set(features[0])
    arrived = lax.all_to_all(
        outgoing.reshape(seq_devices, capacity, D), "seq", split_axis=0, concat_axis=0, tiled=True
    )
    curve_rows = arrived.reshape(seq_devices * capacity, D)[source_for_slot]
    normed_a, normed1, inverse1 = layer_norm(curve_rows, ln1_gain)
    qkv = jnp.dot(normed_a, w_qkv, preferred_element_type=jnp.float32).astype(jnp.bfloat16)
    queries = qkv[:, :D]
    keyval = qkv[:, D:]
    distances = shift_distances(seq_devices)
    pieces = [keyval]
    for distance in distances:
        pieces.append(from_behind(keyval, "seq", distance))
    keyval_all = jnp.concatenate(pieces, axis=0)
    source_dev = jnp.stack(
        [seq_index] + [(seq_index - distance) % seq_devices for distance in distances]
    )
    key_blocks = (
        source_dev[:, None] * blocks_dev + jnp.arange(blocks_dev, dtype=jnp.int32)[None, :]
    ).reshape(-1)
    own_lists = lax.dynamic_slice_in_dim(pattern[0], seq_index * blocks_dev, blocks_dev, axis=0)
    matches = (own_lists[:, :, None] == key_blocks[None, None, :]).astype(jnp.int32)
    selected = jnp.sum(
        matches * jnp.arange(key_blocks.shape[0], dtype=jnp.int32)[None, None, :], axis=-1
    )
    attn_out, log_totals = attention_forward(queries, keyval_all, selected)
    hidden_res = (
        curve_rows.astype(jnp.float32)
        + jnp.dot(attn_out, w_out, preferred_element_type=jnp.float32)
    ).astype(jnp.bfloat16)
    normed_b, normed2, inverse2 = layer_norm(hidden_res, ln2_gain)
    pre_act = jnp.dot(normed_b, w_up, preferred_element_type=jnp.float32)
    activated = jax.nn.gelu(pre_act, approximate=True).astype(jnp.bfloat16)
    curve_out = (
        hidden_res.astype(jnp.float32)
        + jnp.dot(activated, w_down, preferred_element_type=jnp.float32)
    ).astype(jnp.bfloat16)
    leaving = (
        jnp.zeros((seq_devices * capacity, D), jnp.bfloat16).at[source_for_slot].set(curve_out)
    )
    returned = lax.all_to_all(
        leaving.reshape(seq_devices, capacity, D), "seq", split_axis=0, concat_axis=0, tiled=True
    )
    block_out = returned.reshape(seq_devices * capacity, D)[send_index]
    grad_outgoing = (
        jnp.zeros((seq_devices * capacity, D), jnp.bfloat16).at[send_index].set(out_grad[0])
    )
    grad_arrived = lax.all_to_all(
        grad_outgoing.reshape(seq_devices, capacity, D),
        "seq",
        split_axis=0,
        concat_axis=0,
        tiled=True,
    )
    grad_curve = grad_arrived.reshape(seq_devices * capacity, D)[source_for_slot]
    grad_pre = gelu_back(pre_act, times_transposed(grad_curve, w_down)).astype(jnp.bfloat16)
    grad_down = inner_rows(activated, grad_curve)
    grad_normed_b = times_transposed(grad_pre, w_up)
    grad_up_blocks = [
        inner_rows(normed_b, grad_pre[:, index * D : (index + 1) * D])
        for index in range(grad_pre.shape[1] // D)
    ]
    grad_gain2 = jnp.sum(grad_normed_b * normed2, axis=0)
    grad_hidden = (
        grad_curve.astype(jnp.float32) + norm_back(grad_normed_b, ln2_gain, normed2, inverse2)
    ).astype(jnp.bfloat16)
    grad_attn = times_transposed(grad_hidden, w_out).astype(jnp.bfloat16)
    grad_out = inner_rows(attn_out, grad_hidden)
    resent = [keyval]
    for distance in distances:
        resent.append(from_behind(keyval, "seq", distance))
    keyval_back = jnp.concatenate(resent, axis=0)
    grad_query, grad_keyval_all = attention_backward(
        queries, keyval_back, selected, attn_out, log_totals, grad_attn
    )
    grad_keyval = grad_keyval_all[:dev_rows]
    for index_pos, distance in enumerate(distances):
        partial_rows = grad_keyval_all[(index_pos + 1) * dev_rows : (index_pos + 2) * dev_rows]
        grad_keyval = grad_keyval + from_behind(
            partial_rows.astype(jnp.bfloat16), "seq", -distance
        ).astype(partial_rows.dtype)
    grad_qkv_rows = jnp.concatenate([grad_query, grad_keyval.astype(jnp.bfloat16)], axis=1)
    grad_normed_a = times_transposed(grad_qkv_rows, w_qkv)
    grad_qkv_blocks = [
        inner_rows(normed_a, grad_qkv_rows[:, index * D : (index + 1) * D])
        for index in range(grad_qkv_rows.shape[1] // D)
    ]
    grad_gain1 = jnp.sum(grad_normed_a * normed1, axis=0)
    grad_curve_in = (
        grad_hidden.astype(jnp.float32) + norm_back(grad_normed_a, ln1_gain, normed1, inverse1)
    ).astype(jnp.bfloat16)
    grad_leaving = (
        jnp.zeros((seq_devices * capacity, D), jnp.bfloat16).at[source_for_slot].set(grad_curve_in)
    )
    grad_returned = lax.all_to_all(
        grad_leaving.reshape(seq_devices, capacity, D),
        "seq",
        split_axis=0,
        concat_axis=0,
        tiled=True,
    )
    input_grad = grad_returned.reshape(seq_devices * capacity, D)[send_index]
    weight_rows = jnp.concatenate(
        grad_qkv_blocks + [grad_out] + grad_up_blocks + [grad_down],
        axis=0,
    )
    gain_rows = jnp.zeros((8, D), jnp.float32).at[0].set(grad_gain1).at[1].set(grad_gain2)
    grad_qkv, grad_out, grad_up, grad_down, gain_rows = reduce_everywhere(
        weight_rows,
        gain_rows,
        [(D, 3 * D), (D, D), (D, grad_pre.shape[1]), (grad_pre.shape[1], D)],
    )
    grad_gain1 = gain_rows[0]
    grad_gain2 = gain_rows[1]
    return (
        block_out[None],
        input_grad[None],
        grad_qkv,
        grad_out,
        grad_up,
        grad_down,
        grad_gain1,
        grad_gain2,
    )


def solution(mesh):
    return jax.shard_map(
        on_device,
        mesh=mesh,
        in_specs=(
            P("dp", "seq", None),
            P("dp", None),
            P("dp", None, None),
            P(),
            P(),
            P(),
            P(),
            P(),
            P(),
            P("dp", "seq", None),
        ),
        out_specs=(P("dp", "seq", None), P("dp", "seq", None), P(), P(), P(), P(), P(), P()),
        check_vma=False,
    )
```

```python
from functools import partial

import jax
import jax.numpy as jnp
from jax import lax
from jax.experimental import pallas as pl
from jax.experimental.pallas import tpu as pltpu
from jax.sharding import PartitionSpec as P

D = 512
HEADS = 8
BLK = 128


EPSILON = 1e-05


def from_behind(x, axis, by):
    length = lax.axis_size(axis)
    return lax.ppermute(x, axis, [(i, (i + by) % length) for i in range(length)])


def layer_norm(rows_in, gain_vec):
    values = rows_in.astype(jnp.float32)
    centered = values - jnp.mean(values, axis=-1, keepdims=True)
    inverse = lax.rsqrt(jnp.mean(centered * centered, axis=-1, keepdims=True) + EPSILON)
    normed = centered * inverse
    return ((normed * gain_vec).astype(jnp.bfloat16), normed, inverse)


def norm_back(incoming, gain_vec, normed, inverse):
    scaled = incoming * gain_vec
    return inverse * (
        scaled
        - jnp.mean(scaled, axis=-1, keepdims=True)
        - normed * jnp.mean(scaled * normed, axis=-1, keepdims=True)
    )


def gelu_back(pre_act, incoming):
    return jax.vjp(partial(jax.nn.gelu, approximate=True), pre_act)[1](incoming)[0]


def inner_rows(left_mat, right_mat):
    return lax.dot_general(
        left_mat, right_mat, (((0,), (0,)), ((), ())), preferred_element_type=jnp.float32
    )


def times_transposed(left_mat, right_mat):
    return lax.dot_general(
        left_mat, right_mat, (((1,), (1,)), ((), ())), preferred_element_type=jnp.float32
    )


def split_heads(rows_in):
    return rows_in.reshape(rows_in.shape[0] // BLK, BLK, HEADS, D // HEADS)


def listed_heads(keyval_all, selected):
    blocks = keyval_all.reshape(keyval_all.shape[0] // BLK, BLK, 2 * D)
    picked = blocks[selected]
    shape_out = picked.shape[:3] + (HEADS, D // HEADS)
    return (picked[..., :D].reshape(shape_out), picked[..., D:].reshape(shape_out))


def shift_distances(seq_devices):
    levels = seq_devices.bit_length() - 1
    distances = []
    for level_idx in range(levels):
        stride = 2**level_idx
        if 2 * stride == seq_devices:
            distances.append(stride)
        else:
            distances.extend([stride, -stride])
    return distances


def node_plan(position, seq_index, dev_rows, capacity, seq_devices):
    own_position = lax.dynamic_slice_in_dim(position, seq_index * dev_rows, dev_rows)
    target_dev = own_position // dev_rows
    dest_hits = (target_dev[:, None] == jnp.arange(seq_devices, dtype=jnp.int32)[None, :]).astype(
        jnp.int32
    )
    send_rank = jnp.sum((jnp.cumsum(dest_hits, axis=0) - dest_hits) * dest_hits, axis=1)
    send_index = target_dev * capacity + send_rank
    layout = position.reshape(seq_devices, dev_rows)
    arriving = (layout // dev_rows == seq_index).astype(jnp.int32)
    arrive_rank = jnp.cumsum(arriving, axis=1) - arriving
    source_index = jnp.arange(seq_devices, dtype=jnp.int32)[:, None] * capacity + arrive_rank
    del source_index
    total = position.shape[0]
    wanted = seq_index * dev_rows + jnp.arange(dev_rows, dtype=jnp.int32)
    slot_node = jnp.sum(
        jnp.where(
            position[None, :] == wanted[:, None], jnp.arange(total, dtype=jnp.int32)[None, :], 0
        ),
        axis=1,
    )
    source_for_slot = (slot_node // dev_rows) * capacity + arrive_rank.reshape(-1)[slot_node]
    return (send_index, source_for_slot)


def attention_forward(queries, keyval_all, selected):
    query_heads = split_heads(queries)
    key_heads, value_heads = listed_heads(keyval_all, selected)
    scores = (
        jnp.einsum("aihd,akjhd->haikj", query_heads, key_heads, preferred_element_type=jnp.float32)
        * 0.125
    )
    largest = jnp.max(scores, axis=(3, 4), keepdims=True)
    totals = jnp.sum(jnp.exp(scores - largest), axis=(3, 4), keepdims=True)
    log_totals = largest + jnp.log(totals)
    attn_probs = jnp.exp(scores - log_totals).astype(jnp.bfloat16)
    result = jnp.einsum(
        "haikj,akjhd->aihd", attn_probs, value_heads, preferred_element_type=jnp.float32
    )
    return (result.astype(jnp.bfloat16).reshape(queries.shape[0], D), log_totals)


def attention_backward(queries, keyval_all, selected, attn_out, log_totals, grad_attn):
    query_heads = split_heads(queries)
    key_heads, value_heads = listed_heads(keyval_all, selected)
    out_heads = split_heads(attn_out)
    grad_heads = split_heads(grad_attn)
    scores = (
        jnp.einsum("aihd,akjhd->haikj", query_heads, key_heads, preferred_element_type=jnp.float32)
        * 0.125
    )
    attn_exact = jnp.exp(scores - log_totals)
    attn_probs = attn_exact.astype(jnp.bfloat16)
    grad_probs = jnp.einsum(
        "aihd,akjhd->haikj", grad_heads, value_heads, preferred_element_type=jnp.float32
    )
    row_dots = jnp.einsum(
        "aihd,aihd->hai", grad_heads, out_heads, preferred_element_type=jnp.float32
    )[..., None, None]
    grad_scores = (attn_exact * (grad_probs - row_dots) * 0.125).astype(jnp.bfloat16)
    grad_query = jnp.einsum(
        "haikj,akjhd->aihd", grad_scores, key_heads, preferred_element_type=jnp.float32
    )
    grad_keys = jnp.einsum(
        "haikj,aihd->akjhd", grad_scores, query_heads, preferred_element_type=jnp.float32
    )
    grad_values = jnp.einsum(
        "haikj,aihd->akjhd", attn_probs, grad_heads, preferred_element_type=jnp.float32
    )
    block_shape = grad_keys.shape[:3] + (D,)
    grad_picked = jnp.concatenate(
        [grad_keys.reshape(block_shape), grad_values.reshape(block_shape)], axis=-1
    )
    total_rows = keyval_all.shape[0]
    one_hot = (
        selected[:, :, None] == jnp.arange(total_rows // BLK, dtype=jnp.int32)[None, None, :]
    ).astype(jnp.float32)
    grad_keyval = jnp.einsum(
        "akb,akjc->bjc",
        one_hot,
        grad_picked,
        precision=lax.Precision.HIGHEST,
        preferred_element_type=jnp.float32,
    )
    return (
        grad_query.astype(jnp.bfloat16).reshape(queries.shape[0], D),
        grad_keyval.reshape(total_rows, 2 * D),
    )


MESH_IDS = pl.DeviceIdType.MESH
RING_KINDS = ("x", "y", "z")
AXIS_ORDERS = (("x", "y", "z"), ("y", "z", "x"), ("z", "x", "y"))


def reduce_kernel(
    w_ref, g_ref, qkv_ref, proj_ref, up_ref, down_ref, gout_ref, wout_ref, send0, recv0, gsend0, grecv0, *rest
):
    parts = len(AXIS_ORDERS)
    ring_bufs = [[rest[9 * p + 3 * s : 9 * p + 3 * s + 3] for s in range(3)] for p in range(parts)]
    gather_bufs = [rest[9 * parts + 3 * p : 9 * parts + 3 * p + 3] for p in range(parts)]
    gsend, grecv, send_sem, recv_sem, w_vmem, load_sem, write_sem = rest[12 * parts :]
    seq = lax.axis_index("seq")
    dp = lax.axis_index("dp")
    core = seq % 2
    place = {"x": (seq // 2) % 4, "y": seq // 8, "z": dp}

    def peer(kind, member):
        if kind == "core":
            return (seq + 1 - 2 * core, dp)
        if kind == "x":
            return (seq + (member - place["x"]) * 2, dp)
        if kind == "y":
            return (seq + (member - place["y"]) * 8, dp)
        return (seq, member)

    barrier = pltpu.get_barrier_semaphore()
    peers = [peer("core", 0)]
    for kind in RING_KINDS:
        for shift in (1, 2, 3):
            peers.append(peer(kind, (place[kind] + shift) % 4))
    for target in peers:
        pl.semaphore_signal(barrier, inc=1, device_id=target, device_id_type=MESH_IDS)
    pl.semaphore_wait(barrier, len(peers))

    counter = [0]
    sent = []

    def send(src, dst, recv_index, target):
        copy = pltpu.make_async_remote_copy(
            src_ref=src,
            dst_ref=dst,
            send_sem=send_sem.at[counter[0]],
            recv_sem=recv_sem.at[recv_index],
            device_id=target,
            device_id_type=MESH_IDS,
        )
        counter[0] += 1
        copy.start()
        sent.append(copy)

    def arrive(dst, recv_index):
        pltpu.make_async_remote_copy(
            src_ref=dst,
            dst_ref=dst,
            send_sem=send_sem.at[0],
            recv_sem=recv_sem.at[recv_index],
            device_id=peers[0],
            device_id_type=MESH_IDS,
        ).wait_recv()

    half = send0.shape[0]
    third = half // parts
    loads = {}
    for side in (1, 0):
        for part in range(parts):
            first = (side * (1 - core) + (1 - side) * core) * half + part * third
            rows = pl.ds(pl.multiple_of(first, 16), third)
            load = pltpu.make_async_copy(w_ref.at[rows], w_vmem.at[rows], load_sem.at[side * parts + part])
            load.start()
            loads[(side, part)] = load
    gsend0[...] = g_ref[...].astype(jnp.bfloat16)
    send(gsend0, grecv0, 1, peers[0])
    for part in range(parts):
        rows = pl.ds(pl.multiple_of(part * third, 16), third)
        source_rows = pl.ds(pl.multiple_of((1 - core) * half + part * third, 16), third)
        loads[(1, part)].wait()
        send0[rows, :] = w_vmem[source_rows, :].astype(jnp.bfloat16)
        send(send0.at[rows], recv0.at[rows], 150 + part, peers[0])
    arrive(grecv0, 1)
    gains = gsend0[...].astype(jnp.float32) + grecv0[...].astype(jnp.float32)

    def first_chunk(part, member, size):
        offset = part * third + member * size
        mine = w_vmem[pl.ds(pl.multiple_of(core * half + offset, 16), size), :]
        return mine + recv0[pl.ds(pl.multiple_of(offset, 16), size), :].astype(jnp.float32)

    sources = [None] * parts
    def ring_send_step(stage, part, gains):
            kind = AXIS_ORDERS[part][stage]
            sbuf, rbuf, total = ring_bufs[part][stage]
            size = sbuf.shape[1]
            pos = place[kind]
            base = 2 + 12 * (3 * part + stage)
            source = sources[part]

            def chunk(member, source=source, size=size, part=part):
                if source is None:
                    return first_chunk(part, member, size)
                return source[pl.ds(pl.multiple_of(member * size, 16), size), :]

            if stage == 0:
                loads[(0, part)].wait()
                arrive(recv0.at[pl.ds(pl.multiple_of(part * third, 16), third)], 150 + part)
            if part == 0:
                gsend[stage] = gains.astype(jnp.bfloat16)
                grecv[stage, pos] = gsend[stage]
            for shift in (1, 2, 3):
                member = (pos + shift) % 4
                sbuf[member] = chunk(member).astype(jnp.bfloat16)
                send(sbuf.at[member], rbuf.at[pos], base + pos, peer(kind, member))
                if part == 0:
                    send(gsend.at[stage], grecv.at[stage, pos], base + 4 + pos, peer(kind, member))
            total[...] = chunk(pos)
            return gains

    def ring_wait_step(stage, part, gains):
            kind = AXIS_ORDERS[part][stage]
            sbuf, rbuf, total = ring_bufs[part][stage]
            pos = place[kind]
            base = 2 + 12 * (3 * part + stage)
            for shift in (1, 2, 3):
                slot = (pos - shift) % 4
                arrive(rbuf.at[slot], base + slot)
                total[...] += rbuf[slot].astype(jnp.float32)
                if part == 0:
                    arrive(grecv.at[stage, slot], base + 4 + slot)
            if part == 0:
                got = grecv[stage].astype(jnp.float32)
                gains = (got[0] + got[1]) + (got[2] + got[3])
            sources[part] = total
            return gains

    for part in range(parts):
        gains = ring_send_step(0, part, gains)
    for stage in range(3):
        for part in range(parts):
            gains = ring_wait_step(stage, part, gains)
            if stage < 2:
                gains = ring_send_step(stage + 1, part, gains)
    gout_ref[...] = gains

    owns = [sources[part][...].astype(jnp.bfloat16) for part in range(parts)]

    def gather_send_step(stage, part):
        kind = AXIS_ORDERS[part][2 - stage]
        gathered = gather_bufs[part][stage]
        pos = place[kind]
        base = 2 + 12 * 9 + 4 * (3 * part + stage)
        gathered[pos] = owns[part]
        for shift in (1, 2, 3):
            member = (pos + shift) % 4
            send(gathered.at[pos], gathered.at[pos], base + pos, peer(kind, member))

    def gather_wait_step(stage, part):
        kind = AXIS_ORDERS[part][2 - stage]
        gathered = gather_bufs[part][stage]
        pos = place[kind]
        base = 2 + 12 * 9 + 4 * (3 * part + stage)
        for shift in (1, 2, 3):
            arrive(gathered.at[(pos - shift) % 4], base + (pos - shift) % 4)
        owns[part] = gathered[...].reshape(4 * gathered.shape[1], gathered.shape[2])

    for part in range(parts):
        gather_send_step(0, part)
    for stage in range(3):
        for part in range(parts):
            gather_wait_step(stage, part)
            if stage < 2:
                gather_send_step(stage + 1, part)
            else:
                rows = pl.ds(pl.multiple_of(core * half + part * third, 16), third)
                wout_ref[rows, :] = owns[part]
                send(wout_ref.at[rows], wout_ref.at[rows], 154 + part, peers[0])
    for part in range(parts):
        rows = pl.ds(pl.multiple_of((1 - core) * half + part * third, 16), third)
        arrive(wout_ref.at[rows], 154 + part)
    for copy in sent:
        copy.wait_send()
    targets = [qkv_ref.at[:, pl.ds(index * D, D)] for index in range(qkv_ref.shape[1] // D)]
    targets.append(proj_ref)
    targets += [up_ref.at[:, pl.ds(index * D, D)] for index in range(up_ref.shape[1] // D)]
    targets += [down_ref.at[pl.ds(index * D, D), :] for index in range(down_ref.shape[0] // D)]
    writes = []
    for index, target in enumerate(targets):
        write = pltpu.make_async_copy(wout_ref.at[pl.ds(index * D, D)], target, write_sem.at[index])
        write.start()
        writes.append(write)
    for write in writes:
        write.wait()


def reduce_everywhere(rows, gains, shapes):
    total_rows, width = rows.shape
    parts = len(AXIS_ORDERS)
    third = total_rows // 2 // parts
    sizes = [third // 4, third // 16, third // 64]
    scratch = [
        pltpu.VMEM((total_rows, width), jnp.bfloat16),
        pltpu.VMEM((total_rows // 2, width), jnp.bfloat16),
        pltpu.VMEM((total_rows // 2, width), jnp.bfloat16),
        pltpu.VMEM(gains.shape, jnp.bfloat16),
        pltpu.VMEM(gains.shape, jnp.bfloat16),
    ]
    for part in range(parts):
        for size in sizes:
            scratch += [
                pltpu.VMEM((4, size, width), jnp.bfloat16),
                pltpu.VMEM((4, size, width), jnp.bfloat16),
                pltpu.VMEM((size, width), jnp.float32),
            ]
    for part in range(parts):
        for size in reversed(sizes):
            scratch.append(pltpu.VMEM((4, size, width), jnp.bfloat16))
    scratch += [
        pltpu.VMEM((3,) + gains.shape, jnp.bfloat16),
        pltpu.VMEM((3, 4) + gains.shape, jnp.bfloat16),
        pltpu.SemaphoreType.DMA((160,)),
        pltpu.SemaphoreType.DMA((160,)),
        pltpu.VMEM((total_rows, width), jnp.float32),
        pltpu.SemaphoreType.DMA((2 * parts,)),
        pltpu.SemaphoreType.DMA((total_rows // width,)),
    ]
    results = pl.pallas_call(
        reduce_kernel,
        out_shape=tuple(jax.ShapeDtypeStruct(shape, jnp.bfloat16) for shape in shapes)
        + (jax.ShapeDtypeStruct(gains.shape, jnp.float32),),
        in_specs=[pl.BlockSpec(memory_space=pl.ANY), pl.BlockSpec(memory_space=pltpu.VMEM)],
        out_specs=tuple(pl.BlockSpec(memory_space=pl.ANY) for _ in shapes)
        + (pl.BlockSpec(memory_space=pltpu.VMEM),),
        scratch_shapes=scratch,
        compiler_params=pltpu.CompilerParams(
            collective_id=0, has_side_effects=True, vmem_limit_bytes=60 * 1024 * 1024
        ),
    )(rows, gains)
    return tuple(result.astype(jnp.float32) for result in results)

def on_device(
    features, curve_pos, pattern, ln1_gain, w_qkv, w_out, ln2_gain, w_up, w_down, out_grad
):
    seq_devices = lax.axis_size("seq")
    seq_index = lax.axis_index("seq")
    dev_rows = features.shape[1]
    capacity = 2 * dev_rows // seq_devices
    blocks_dev = dev_rows // BLK
    position = curve_pos[0]
    send_index, source_for_slot = node_plan(position, seq_index, dev_rows, capacity, seq_devices)
    outgoing = jnp.zeros((seq_devices * capacity, D), jnp.bfloat16).at[send_index].set(features[0])
    arrived = lax.all_to_all(
        outgoing.reshape(seq_devices, capacity, D), "seq", split_axis=0, concat_axis=0, tiled=True
    )
    curve_rows = arrived.reshape(seq_devices * capacity, D)[source_for_slot]
    normed_a, normed1, inverse1 = layer_norm(curve_rows, ln1_gain)
    qkv = jnp.dot(normed_a, w_qkv, preferred_element_type=jnp.float32).astype(jnp.bfloat16)
    queries = qkv[:, :D]
    keyval = qkv[:, D:]
    distances = shift_distances(seq_devices)
    pieces = [keyval]
    for distance in distances:
        pieces.append(from_behind(keyval, "seq", distance))
    keyval_all = jnp.concatenate(pieces, axis=0)
    source_dev = jnp.stack(
        [seq_index] + [(seq_index - distance) % seq_devices for distance in distances]
    )
    key_blocks = (
        source_dev[:, None] * blocks_dev + jnp.arange(blocks_dev, dtype=jnp.int32)[None, :]
    ).reshape(-1)
    own_lists = lax.dynamic_slice_in_dim(pattern[0], seq_index * blocks_dev, blocks_dev, axis=0)
    matches = (own_lists[:, :, None] == key_blocks[None, None, :]).astype(jnp.int32)
    selected = jnp.sum(
        matches * jnp.arange(key_blocks.shape[0], dtype=jnp.int32)[None, None, :], axis=-1
    )
    attn_out, log_totals = attention_forward(queries, keyval_all, selected)
    hidden_res = (
        curve_rows.astype(jnp.float32)
        + jnp.dot(attn_out, w_out, preferred_element_type=jnp.float32)
    ).astype(jnp.bfloat16)
    normed_b, normed2, inverse2 = layer_norm(hidden_res, ln2_gain)
    pre_act = jnp.dot(normed_b, w_up, preferred_element_type=jnp.float32)
    activated = jax.nn.gelu(pre_act, approximate=True).astype(jnp.bfloat16)
    curve_out = (
        hidden_res.astype(jnp.float32)
        + jnp.dot(activated, w_down, preferred_element_type=jnp.float32)
    ).astype(jnp.bfloat16)
    leaving = (
        jnp.zeros((seq_devices * capacity, D), jnp.bfloat16).at[source_for_slot].set(curve_out)
    )
    returned = lax.all_to_all(
        leaving.reshape(seq_devices, capacity, D), "seq", split_axis=0, concat_axis=0, tiled=True
    )
    block_out = returned.reshape(seq_devices * capacity, D)[send_index]
    grad_outgoing = (
        jnp.zeros((seq_devices * capacity, D), jnp.bfloat16).at[send_index].set(out_grad[0])
    )
    grad_arrived = lax.all_to_all(
        grad_outgoing.reshape(seq_devices, capacity, D),
        "seq",
        split_axis=0,
        concat_axis=0,
        tiled=True,
    )
    grad_curve = grad_arrived.reshape(seq_devices * capacity, D)[source_for_slot]
    grad_pre = gelu_back(pre_act, times_transposed(grad_curve, w_down)).astype(jnp.bfloat16)
    grad_down = inner_rows(activated, grad_curve)
    grad_normed_b = times_transposed(grad_pre, w_up)
    grad_up_blocks = [
        inner_rows(normed_b, grad_pre[:, index * D : (index + 1) * D])
        for index in range(grad_pre.shape[1] // D)
    ]
    grad_gain2 = jnp.sum(grad_normed_b * normed2, axis=0)
    grad_hidden = (
        grad_curve.astype(jnp.float32) + norm_back(grad_normed_b, ln2_gain, normed2, inverse2)
    ).astype(jnp.bfloat16)
    grad_attn = times_transposed(grad_hidden, w_out).astype(jnp.bfloat16)
    grad_out = inner_rows(attn_out, grad_hidden)
    resent = [keyval]
    for distance in distances:
        resent.append(from_behind(keyval, "seq", distance))
    keyval_back = jnp.concatenate(resent, axis=0)
    grad_query, grad_keyval_all = attention_backward(
        queries, keyval_back, selected, attn_out, log_totals, grad_attn
    )
    grad_keyval = grad_keyval_all[:dev_rows]
    for index_pos, distance in enumerate(distances):
        partial_rows = grad_keyval_all[(index_pos + 1) * dev_rows : (index_pos + 2) * dev_rows]
        grad_keyval = grad_keyval + from_behind(
            partial_rows.astype(jnp.bfloat16), "seq", -distance
        ).astype(partial_rows.dtype)
    grad_qkv_rows = jnp.concatenate([grad_query, grad_keyval.astype(jnp.bfloat16)], axis=1)
    grad_normed_a = times_transposed(grad_qkv_rows, w_qkv)
    grad_qkv_blocks = [
        inner_rows(normed_a, grad_qkv_rows[:, index * D : (index + 1) * D])
        for index in range(grad_qkv_rows.shape[1] // D)
    ]
    grad_gain1 = jnp.sum(grad_normed_a * normed1, axis=0)
    grad_curve_in = (
        grad_hidden.astype(jnp.float32) + norm_back(grad_normed_a, ln1_gain, normed1, inverse1)
    ).astype(jnp.bfloat16)
    grad_leaving = (
        jnp.zeros((seq_devices * capacity, D), jnp.bfloat16).at[source_for_slot].set(grad_curve_in)
    )
    grad_returned = lax.all_to_all(
        grad_leaving.reshape(seq_devices, capacity, D),
        "seq",
        split_axis=0,
        concat_axis=0,
        tiled=True,
    )
    input_grad = grad_returned.reshape(seq_devices * capacity, D)[send_index]
    weight_rows = jnp.concatenate(
        grad_qkv_blocks + [grad_out] + grad_up_blocks + [grad_down],
        axis=0,
    )
    gain_rows = jnp.zeros((8, D), jnp.float32).at[0].set(grad_gain1).at[1].set(grad_gain2)
    grad_qkv, grad_out, grad_up, grad_down, gain_rows = reduce_everywhere(
        weight_rows,
        gain_rows,
        [(D, 3 * D), (D, D), (D, grad_pre.shape[1]), (grad_pre.shape[1], D)],
    )
    grad_gain1 = gain_rows[0]
    grad_gain2 = gain_rows[1]
    return (
        block_out[None],
        input_grad[None],
        grad_qkv,
        grad_out,
        grad_up,
        grad_down,
        grad_gain1,
        grad_gain2,
    )


def solution(mesh):
    return jax.shard_map(
        on_device,
        mesh=mesh,
        in_specs=(
            P("dp", "seq", None),
            P("dp", None),
            P("dp", None, None),
            P(),
            P(),
            P(),
            P(),
            P(),
            P(),
            P("dp", "seq", None),
        ),
        out_specs=(P("dp", "seq", None), P("dp", "seq", None), P(), P(), P(), P(), P(), P()),
        check_vma=False,
    )
```

```python
from functools import partial

import jax
import jax.numpy as jnp
from jax import lax
from jax.experimental import pallas as pl
from jax.experimental.pallas import tpu as pltpu
from jax.sharding import PartitionSpec as P

D = 512
HEADS = 8
BLK = 128


EPSILON = 1e-05


def from_behind(x, axis, by):
    length = lax.axis_size(axis)
    return lax.ppermute(x, axis, [(i, (i + by) % length) for i in range(length)])


def layer_norm(rows_in, gain_vec):
    values = rows_in.astype(jnp.float32)
    centered = values - jnp.mean(values, axis=-1, keepdims=True)
    inverse = lax.rsqrt(jnp.mean(centered * centered, axis=-1, keepdims=True) + EPSILON)
    normed = centered * inverse
    return ((normed * gain_vec).astype(jnp.bfloat16), normed, inverse)


def norm_back(incoming, gain_vec, normed, inverse):
    scaled = incoming * gain_vec
    return inverse * (
        scaled
        - jnp.mean(scaled, axis=-1, keepdims=True)
        - normed * jnp.mean(scaled * normed, axis=-1, keepdims=True)
    )


def gelu_back(pre_act, incoming):
    return jax.vjp(partial(jax.nn.gelu, approximate=True), pre_act)[1](incoming)[0]


def inner_rows(left_mat, right_mat):
    return lax.dot_general(
        left_mat, right_mat, (((0,), (0,)), ((), ())), preferred_element_type=jnp.float32
    )


def times_transposed(left_mat, right_mat):
    return lax.dot_general(
        left_mat, right_mat, (((1,), (1,)), ((), ())), preferred_element_type=jnp.float32
    )


def split_heads(rows_in):
    return rows_in.reshape(rows_in.shape[0] // BLK, BLK, HEADS, D // HEADS)


def listed_heads(keyval_all, selected):
    blocks = keyval_all.reshape(keyval_all.shape[0] // BLK, BLK, 2 * D)
    picked = blocks[selected]
    shape_out = picked.shape[:3] + (HEADS, D // HEADS)
    return (picked[..., :D].reshape(shape_out), picked[..., D:].reshape(shape_out))


def shift_distances(seq_devices):
    levels = seq_devices.bit_length() - 1
    distances = []
    for level_idx in range(levels):
        stride = 2**level_idx
        if 2 * stride == seq_devices:
            distances.append(stride)
        else:
            distances.extend([stride, -stride])
    return distances


def node_plan(position, seq_index, dev_rows, capacity, seq_devices):
    own_position = lax.dynamic_slice_in_dim(position, seq_index * dev_rows, dev_rows)
    target_dev = own_position // dev_rows
    dest_hits = (target_dev[:, None] == jnp.arange(seq_devices, dtype=jnp.int32)[None, :]).astype(
        jnp.int32
    )
    send_rank = jnp.sum((jnp.cumsum(dest_hits, axis=0) - dest_hits) * dest_hits, axis=1)
    send_index = target_dev * capacity + send_rank
    layout = position.reshape(seq_devices, dev_rows)
    arriving = (layout // dev_rows == seq_index).astype(jnp.int32)
    arrive_rank = jnp.cumsum(arriving, axis=1) - arriving
    source_index = jnp.arange(seq_devices, dtype=jnp.int32)[:, None] * capacity + arrive_rank
    del source_index
    total = position.shape[0]
    wanted = seq_index * dev_rows + jnp.arange(dev_rows, dtype=jnp.int32)
    slot_node = jnp.sum(
        jnp.where(
            position[None, :] == wanted[:, None], jnp.arange(total, dtype=jnp.int32)[None, :], 0
        ),
        axis=1,
    )
    source_for_slot = (slot_node // dev_rows) * capacity + arrive_rank.reshape(-1)[slot_node]
    return (send_index, source_for_slot)


def attention_forward(queries, keyval_all, selected):
    query_heads = split_heads(queries)
    key_heads, value_heads = listed_heads(keyval_all, selected)
    scores = (
        jnp.einsum("aihd,akjhd->haikj", query_heads, key_heads, preferred_element_type=jnp.float32)
        * 0.125
    )
    largest = jnp.max(scores, axis=(3, 4), keepdims=True)
    totals = jnp.sum(jnp.exp(scores - largest), axis=(3, 4), keepdims=True)
    log_totals = largest + jnp.log(totals)
    attn_probs = jnp.exp(scores - log_totals).astype(jnp.bfloat16)
    result = jnp.einsum(
        "haikj,akjhd->aihd", attn_probs, value_heads, preferred_element_type=jnp.float32
    )
    return (result.astype(jnp.bfloat16).reshape(queries.shape[0], D), log_totals)


def attention_backward(queries, keyval_all, selected, attn_out, log_totals, grad_attn):
    query_heads = split_heads(queries)
    key_heads, value_heads = listed_heads(keyval_all, selected)
    out_heads = split_heads(attn_out)
    grad_heads = split_heads(grad_attn)
    scores = (
        jnp.einsum("aihd,akjhd->haikj", query_heads, key_heads, preferred_element_type=jnp.float32)
        * 0.125
    )
    attn_exact = jnp.exp(scores - log_totals)
    attn_probs = attn_exact.astype(jnp.bfloat16)
    grad_probs = jnp.einsum(
        "aihd,akjhd->haikj", grad_heads, value_heads, preferred_element_type=jnp.float32
    )
    row_dots = jnp.einsum(
        "aihd,aihd->hai", grad_heads, out_heads, preferred_element_type=jnp.float32
    )[..., None, None]
    grad_scores = (attn_exact * (grad_probs - row_dots) * 0.125).astype(jnp.bfloat16)
    grad_query = jnp.einsum(
        "haikj,akjhd->aihd", grad_scores, key_heads, preferred_element_type=jnp.float32
    )
    grad_keys = jnp.einsum(
        "haikj,aihd->akjhd", grad_scores, query_heads, preferred_element_type=jnp.float32
    )
    grad_values = jnp.einsum(
        "haikj,aihd->akjhd", attn_probs, grad_heads, preferred_element_type=jnp.float32
    )
    block_shape = grad_keys.shape[:3] + (D,)
    grad_picked = jnp.concatenate(
        [grad_keys.reshape(block_shape), grad_values.reshape(block_shape)], axis=-1
    )
    total_rows = keyval_all.shape[0]
    one_hot = (
        selected[:, :, None] == jnp.arange(total_rows // BLK, dtype=jnp.int32)[None, None, :]
    ).astype(jnp.float32)
    grad_keyval = jnp.einsum(
        "akb,akjc->bjc",
        one_hot,
        grad_picked,
        precision=lax.Precision.HIGHEST,
        preferred_element_type=jnp.float32,
    )
    return (
        grad_query.astype(jnp.bfloat16).reshape(queries.shape[0], D),
        grad_keyval.reshape(total_rows, 2 * D),
    )


MESH_IDS = pl.DeviceIdType.MESH
RING_KINDS = ("x", "y", "z")
AXIS_ORDERS = (("x", "y", "z"), ("y", "z", "x"), ("z", "x", "y"))


def reduce_kernel(
    w_ref, g_ref, qkv_ref, proj_ref, up_ref, down_ref, gout_ref, wout_ref, send0, recv0, gsend0, grecv0, *rest
):
    parts = len(AXIS_ORDERS)
    ring_bufs = [[rest[9 * p + 3 * s : 9 * p + 3 * s + 3] for s in range(3)] for p in range(parts)]
    gather_bufs = [rest[9 * parts + 3 * p : 9 * parts + 3 * p + 3] for p in range(parts)]
    gsend, grecv, send_sem, recv_sem, w_vmem, load_sem = rest[12 * parts :]
    seq = lax.axis_index("seq")
    dp = lax.axis_index("dp")
    core = seq % 2
    place = {"x": (seq // 2) % 4, "y": seq // 8, "z": dp}

    def peer(kind, member):
        if kind == "core":
            return (seq + 1 - 2 * core, dp)
        if kind == "x":
            return (seq + (member - place["x"]) * 2, dp)
        if kind == "y":
            return (seq + (member - place["y"]) * 8, dp)
        return (seq, member)

    barrier = pltpu.get_barrier_semaphore()
    peers = [peer("core", 0)]
    for kind in RING_KINDS:
        for shift in (1, 2, 3):
            peers.append(peer(kind, (place[kind] + shift) % 4))
    for target in peers:
        pl.semaphore_signal(barrier, inc=1, device_id=target, device_id_type=MESH_IDS)
    pl.semaphore_wait(barrier, len(peers))

    counter = [0]
    sent = []

    def send(src, dst, recv_index, target):
        copy = pltpu.make_async_remote_copy(
            src_ref=src,
            dst_ref=dst,
            send_sem=send_sem.at[counter[0]],
            recv_sem=recv_sem.at[recv_index],
            device_id=target,
            device_id_type=MESH_IDS,
        )
        counter[0] += 1
        copy.start()
        sent.append(copy)

    def arrive(dst, recv_index):
        pltpu.make_async_remote_copy(
            src_ref=dst,
            dst_ref=dst,
            send_sem=send_sem.at[0],
            recv_sem=recv_sem.at[recv_index],
            device_id=peers[0],
            device_id_type=MESH_IDS,
        ).wait_recv()

    half = send0.shape[0]
    third = half // parts
    loads = {}
    for side in (1, 0):
        for part in range(parts):
            first = (side * (1 - core) + (1 - side) * core) * half + part * third
            rows = pl.ds(pl.multiple_of(first, 16), third)
            load = pltpu.make_async_copy(w_ref.at[rows], w_vmem.at[rows], load_sem.at[side * parts + part])
            load.start()
            loads[(side, part)] = load
    gsend0[...] = g_ref[...].astype(jnp.bfloat16)
    send(gsend0, grecv0, 1, peers[0])
    for part in range(parts):
        rows = pl.ds(pl.multiple_of(part * third, 16), third)
        source_rows = pl.ds(pl.multiple_of((1 - core) * half + part * third, 16), third)
        loads[(1, part)].wait()
        send0[rows, :] = w_vmem[source_rows, :].astype(jnp.bfloat16)
        send(send0.at[rows], recv0.at[rows], 150 + part, peers[0])
    arrive(grecv0, 1)
    gains = gsend0[...].astype(jnp.float32) + grecv0[...].astype(jnp.float32)

    def first_chunk(part, member, size):
        offset = part * third + member * size
        mine = w_vmem[pl.ds(pl.multiple_of(core * half + offset, 16), size), :]
        return mine + recv0[pl.ds(pl.multiple_of(offset, 16), size), :].astype(jnp.float32)

    sources = [None] * parts
    def ring_send_step(stage, part, gains):
            kind = AXIS_ORDERS[part][stage]
            sbuf, rbuf, total = ring_bufs[part][stage]
            size = sbuf.shape[1]
            pos = place[kind]
            base = 2 + 12 * (3 * part + stage)
            source = sources[part]

            def chunk(member, source=source, size=size, part=part):
                if source is None:
                    return first_chunk(part, member, size)
                return source[pl.ds(pl.multiple_of(member * size, 16), size), :]

            if stage == 0:
                loads[(0, part)].wait()
                arrive(recv0.at[pl.ds(pl.multiple_of(part * third, 16), third)], 150 + part)
            if part == 0:
                gsend[stage] = gains.astype(jnp.bfloat16)
                grecv[stage, pos] = gsend[stage]
            for shift in (1, 2, 3):
                member = (pos + shift) % 4
                sbuf[member] = chunk(member).astype(jnp.bfloat16)
                send(sbuf.at[member], rbuf.at[pos], base + pos, peer(kind, member))
                if part == 0:
                    send(gsend.at[stage], grecv.at[stage, pos], base + 4 + pos, peer(kind, member))
            total[...] = chunk(pos)
            return gains

    def ring_wait_step(stage, part, gains):
            kind = AXIS_ORDERS[part][stage]
            sbuf, rbuf, total = ring_bufs[part][stage]
            pos = place[kind]
            base = 2 + 12 * (3 * part + stage)
            for shift in (1, 2, 3):
                slot = (pos - shift) % 4
                arrive(rbuf.at[slot], base + slot)
                total[...] += rbuf[slot].astype(jnp.float32)
                if part == 0:
                    arrive(grecv.at[stage, slot], base + 4 + slot)
            if part == 0:
                got = grecv[stage].astype(jnp.float32)
                gains = (got[0] + got[1]) + (got[2] + got[3])
            sources[part] = total
            return gains

    for part in range(parts):
        gains = ring_send_step(0, part, gains)
    for stage in range(3):
        for part in range(parts):
            gains = ring_wait_step(stage, part, gains)
            if stage < 2:
                gains = ring_send_step(stage + 1, part, gains)
    gout_ref[...] = gains

    owns = [sources[part][...].astype(jnp.bfloat16) for part in range(parts)]

    def gather_send_step(stage, part):
        kind = AXIS_ORDERS[part][2 - stage]
        gathered = gather_bufs[part][stage]
        pos = place[kind]
        base = 2 + 12 * 9 + 4 * (3 * part + stage)
        gathered[pos] = owns[part]
        for shift in (1, 2, 3):
            member = (pos + shift) % 4
            send(gathered.at[pos], gathered.at[pos], base + pos, peer(kind, member))

    def gather_wait_step(stage, part):
        kind = AXIS_ORDERS[part][2 - stage]
        gathered = gather_bufs[part][stage]
        pos = place[kind]
        base = 2 + 12 * 9 + 4 * (3 * part + stage)
        for shift in (1, 2, 3):
            arrive(gathered.at[(pos - shift) % 4], base + (pos - shift) % 4)
        owns[part] = gathered[...].reshape(4 * gathered.shape[1], gathered.shape[2])

    for part in range(parts):
        gather_send_step(0, part)
    for stage in range(3):
        for part in range(parts):
            gather_wait_step(stage, part)
            if stage < 2:
                gather_send_step(stage + 1, part)
            else:
                rows = pl.ds(pl.multiple_of(core * half + part * third, 16), third)
                wout_ref[rows, :] = owns[part]
                send(wout_ref.at[rows], wout_ref.at[rows], 154 + part, peers[0])
    for part in range(parts):
        rows = pl.ds(pl.multiple_of((1 - core) * half + part * third, 16), third)
        arrive(wout_ref.at[rows], 154 + part)
    for copy in sent:
        copy.wait_send()
    for index in range(qkv_ref.shape[1] // D):
        qkv_ref[:, index * D : (index + 1) * D] = wout_ref[index * D : (index + 1) * D, :]
    start = qkv_ref.shape[1]
    proj_ref[...] = wout_ref[start : start + D, :]
    start += D
    for index in range(up_ref.shape[1] // D):
        rows = pl.ds(start + index * D, D)
        up_ref[:, index * D : (index + 1) * D] = wout_ref[rows, :]
    start += up_ref.shape[1]
    down_ref[...] = wout_ref[start:, :]


def reduce_everywhere(rows, gains, shapes):
    total_rows, width = rows.shape
    parts = len(AXIS_ORDERS)
    third = total_rows // 2 // parts
    sizes = [third // 4, third // 16, third // 64]
    scratch = [
        pltpu.VMEM((total_rows, width), jnp.bfloat16),
        pltpu.VMEM((total_rows // 2, width), jnp.bfloat16),
        pltpu.VMEM((total_rows // 2, width), jnp.bfloat16),
        pltpu.VMEM(gains.shape, jnp.bfloat16),
        pltpu.VMEM(gains.shape, jnp.bfloat16),
    ]
    for part in range(parts):
        for size in sizes:
            scratch += [
                pltpu.VMEM((4, size, width), jnp.bfloat16),
                pltpu.VMEM((4, size, width), jnp.bfloat16),
                pltpu.VMEM((size, width), jnp.float32),
            ]
    for part in range(parts):
        for size in reversed(sizes):
            scratch.append(pltpu.VMEM((4, size, width), jnp.bfloat16))
    scratch += [
        pltpu.VMEM((3,) + gains.shape, jnp.bfloat16),
        pltpu.VMEM((3, 4) + gains.shape, jnp.bfloat16),
        pltpu.SemaphoreType.DMA((160,)),
        pltpu.SemaphoreType.DMA((160,)),
        pltpu.VMEM((total_rows, width), jnp.float32),
        pltpu.SemaphoreType.DMA((2 * parts,)),
    ]
    results = pl.pallas_call(
        reduce_kernel,
        out_shape=tuple(jax.ShapeDtypeStruct(shape, jnp.bfloat16) for shape in shapes)
        + (jax.ShapeDtypeStruct(gains.shape, jnp.float32),),
        in_specs=[pl.BlockSpec(memory_space=pl.ANY), pl.BlockSpec(memory_space=pltpu.VMEM)],
        out_specs=tuple(pl.BlockSpec(memory_space=pltpu.VMEM) for _ in range(len(shapes) + 1)),
        scratch_shapes=scratch,
        compiler_params=pltpu.CompilerParams(
            collective_id=0, has_side_effects=True, vmem_limit_bytes=60 * 1024 * 1024
        ),
    )(rows, gains)
    return tuple(result.astype(jnp.float32) for result in results)

def on_device(
    features, curve_pos, pattern, ln1_gain, w_qkv, w_out, ln2_gain, w_up, w_down, out_grad
):
    seq_devices = lax.axis_size("seq")
    seq_index = lax.axis_index("seq")
    dev_rows = features.shape[1]
    capacity = 2 * dev_rows // seq_devices
    blocks_dev = dev_rows // BLK
    position = curve_pos[0]
    send_index, source_for_slot = node_plan(position, seq_index, dev_rows, capacity, seq_devices)
    outgoing = jnp.zeros((seq_devices * capacity, D), jnp.bfloat16).at[send_index].set(features[0])
    arrived = lax.all_to_all(
        outgoing.reshape(seq_devices, capacity, D), "seq", split_axis=0, concat_axis=0, tiled=True
    )
    curve_rows = arrived.reshape(seq_devices * capacity, D)[source_for_slot]
    normed_a, normed1, inverse1 = layer_norm(curve_rows, ln1_gain)
    keyval = jnp.dot(normed_a, w_qkv[:, D:], preferred_element_type=jnp.float32).astype(
        jnp.bfloat16
    )
    queries = jnp.dot(normed_a, w_qkv[:, :D], preferred_element_type=jnp.float32).astype(
        jnp.bfloat16
    )
    distances = shift_distances(seq_devices)
    pieces = [keyval]
    for distance in distances:
        pieces.append(from_behind(keyval, "seq", distance))
    keyval_all = jnp.concatenate(pieces, axis=0)
    source_dev = jnp.stack(
        [seq_index] + [(seq_index - distance) % seq_devices for distance in distances]
    )
    key_blocks = (
        source_dev[:, None] * blocks_dev + jnp.arange(blocks_dev, dtype=jnp.int32)[None, :]
    ).reshape(-1)
    own_lists = lax.dynamic_slice_in_dim(pattern[0], seq_index * blocks_dev, blocks_dev, axis=0)
    matches = (own_lists[:, :, None] == key_blocks[None, None, :]).astype(jnp.int32)
    selected = jnp.sum(
        matches * jnp.arange(key_blocks.shape[0], dtype=jnp.int32)[None, None, :], axis=-1
    )
    attn_out, log_totals = attention_forward(queries, keyval_all, selected)
    hidden_res = (
        curve_rows.astype(jnp.float32)
        + jnp.dot(attn_out, w_out, preferred_element_type=jnp.float32)
    ).astype(jnp.bfloat16)
    normed_b, normed2, inverse2 = layer_norm(hidden_res, ln2_gain)
    pre_act = jnp.dot(normed_b, w_up, preferred_element_type=jnp.float32)
    activated = jax.nn.gelu(pre_act, approximate=True).astype(jnp.bfloat16)
    curve_out = (
        hidden_res.astype(jnp.float32)
        + jnp.dot(activated, w_down, preferred_element_type=jnp.float32)
    ).astype(jnp.bfloat16)
    leaving = (
        jnp.zeros((seq_devices * capacity, D), jnp.bfloat16).at[source_for_slot].set(curve_out)
    )
    returned = lax.all_to_all(
        leaving.reshape(seq_devices, capacity, D), "seq", split_axis=0, concat_axis=0, tiled=True
    )
    block_out = returned.reshape(seq_devices * capacity, D)[send_index]
    grad_outgoing = (
        jnp.zeros((seq_devices * capacity, D), jnp.bfloat16).at[send_index].set(out_grad[0])
    )
    grad_arrived = lax.all_to_all(
        grad_outgoing.reshape(seq_devices, capacity, D),
        "seq",
        split_axis=0,
        concat_axis=0,
        tiled=True,
    )
    grad_curve = grad_arrived.reshape(seq_devices * capacity, D)[source_for_slot]
    grad_pre = gelu_back(pre_act, times_transposed(grad_curve, w_down)).astype(jnp.bfloat16)
    grad_down = inner_rows(activated, grad_curve)
    grad_normed_b = times_transposed(grad_pre, w_up)
    grad_up_blocks = [
        inner_rows(normed_b, grad_pre[:, index * D : (index + 1) * D])
        for index in range(grad_pre.shape[1] // D)
    ]
    grad_gain2 = jnp.sum(grad_normed_b * normed2, axis=0)
    grad_hidden = (
        grad_curve.astype(jnp.float32) + norm_back(grad_normed_b, ln2_gain, normed2, inverse2)
    ).astype(jnp.bfloat16)
    grad_attn = times_transposed(grad_hidden, w_out).astype(jnp.bfloat16)
    grad_out = inner_rows(attn_out, grad_hidden)
    resent = [keyval]
    for distance in distances:
        resent.append(from_behind(keyval, "seq", distance))
    keyval_back = jnp.concatenate(resent, axis=0)
    grad_query, grad_keyval_all = attention_backward(
        queries, keyval_back, selected, attn_out, log_totals, grad_attn
    )
    grad_keyval = grad_keyval_all[:dev_rows]
    for index_pos, distance in enumerate(distances):
        partial_rows = grad_keyval_all[(index_pos + 1) * dev_rows : (index_pos + 2) * dev_rows]
        grad_keyval = grad_keyval + from_behind(
            partial_rows.astype(jnp.bfloat16), "seq", -distance
        ).astype(partial_rows.dtype)
    grad_qkv_rows = jnp.concatenate([grad_query, grad_keyval.astype(jnp.bfloat16)], axis=1)
    grad_normed_a = times_transposed(grad_qkv_rows, w_qkv)
    grad_qkv_blocks = [
        inner_rows(normed_a, grad_qkv_rows[:, index * D : (index + 1) * D])
        for index in range(grad_qkv_rows.shape[1] // D)
    ]
    grad_gain1 = jnp.sum(grad_normed_a * normed1, axis=0)
    grad_curve_in = (
        grad_hidden.astype(jnp.float32) + norm_back(grad_normed_a, ln1_gain, normed1, inverse1)
    ).astype(jnp.bfloat16)
    grad_leaving = (
        jnp.zeros((seq_devices * capacity, D), jnp.bfloat16).at[source_for_slot].set(grad_curve_in)
    )
    grad_returned = lax.all_to_all(
        grad_leaving.reshape(seq_devices, capacity, D),
        "seq",
        split_axis=0,
        concat_axis=0,
        tiled=True,
    )
    input_grad = grad_returned.reshape(seq_devices * capacity, D)[send_index]
    weight_rows = jnp.concatenate(
        grad_qkv_blocks + [grad_out] + grad_up_blocks + [grad_down],
        axis=0,
    )
    gain_rows = jnp.zeros((8, D), jnp.float32).at[0].set(grad_gain1).at[1].set(grad_gain2)
    grad_qkv, grad_out, grad_up, grad_down, gain_rows = reduce_everywhere(
        weight_rows,
        gain_rows,
        [(D, 3 * D), (D, D), (D, grad_pre.shape[1]), (grad_pre.shape[1], D)],
    )
    grad_gain1 = gain_rows[0]
    grad_gain2 = gain_rows[1]
    return (
        block_out[None],
        input_grad[None],
        grad_qkv,
        grad_out,
        grad_up,
        grad_down,
        grad_gain1,
        grad_gain2,
    )


def solution(mesh):
    return jax.shard_map(
        on_device,
        mesh=mesh,
        in_specs=(
            P("dp", "seq", None),
            P("dp", None),
            P("dp", None, None),
            P(),
            P(),
            P(),
            P(),
            P(),
            P(),
            P("dp", "seq", None),
        ),
        out_specs=(P("dp", "seq", None), P("dp", "seq", None), P(), P(), P(), P(), P(), P()),
        check_vma=False,
    )
```
